32 devices in a mesh: fsdp: 32 (over z, y, x, core).
Axes of the slice: x: 2, y: 2, z: 4, core: 2. Of those that a mesh axis runs over, the one named last changes fastest.
Arguments:
- hidden: bfloat16 [2, 32, 128, 1024], P(None, 'fsdp'), may hold values from -6 to 6
- encoder: bfloat16 [2, 32, 256, 1024], P(None, 'fsdp'), may hold values from -6 to 6
- cotangent: bfloat16 [2, 32, 128, 1024], P(None, 'fsdp'), may hold values from -6 to 6
- segment_ids: int32 [2, 32, 128], replicated, may hold values from 0 to 3, never falling along the last dimension, each value on 1 to 64 neighbouring positions
- rel_buckets: int32 [2, 32, 128], replicated, may hold values from 0 to 31
- enc_rows: int32 [2, 32], replicated, may hold values from 64 to 256, as said below
- dealing: int32 [2, 32], replicated, may hold values from 0 to 31, each once within a row
- gain_self: bfloat16 [1024], P('fsdp'), may hold values from 0.5 to 1.5
- gain_cross: bfloat16 [1024], P('fsdp'), may hold values from 0.5 to 1.5
- gain_ffn: bfloat16 [1024], P('fsdp'), may hold values from 0.5 to 1.5
- rel_bias: bfloat16 [512], P('fsdp'), may hold values from -4 to 4
- self_query: bfloat16 [1024, 1024], P('fsdp'), may hold values from -0.046875 to 0.046875
- self_key: bfloat16 [1024, 1024], P('fsdp'), may hold values from -0.1875 to 0.1875
- self_value: bfloat16 [1024, 1024], P('fsdp'), may hold values from -0.1875 to 0.1875
- self_out: bfloat16 [1024, 1024], P('fsdp'), may hold values from -0.5 to 0.5
- cross_query: bfloat16 [1024, 1024], P('fsdp'), may hold values from -0.046875 to 0.046875
- cross_key: bfloat16 [1024, 1024], P('fsdp'), may hold values from -0.1875 to 0.1875
- cross_value: bfloat16 [1024, 1024], P('fsdp'), may hold values from -0.1875 to 0.1875
- cross_out: bfloat16 [1024, 1024], P('fsdp'), may hold values from -0.5 to 0.5
- feed_gate: bfloat16 [1024, 2816], P('fsdp'), may hold values from -0.1875 to 0.1875
- feed_up: bfloat16 [1024, 2816], P('fsdp'), may hold values from -0.1875 to 0.1875
- feed_down: bfloat16 [2816, 1024], P('fsdp'), may hold values from -0.15625 to 0.15625
Outputs:
- layer_out: bfloat16 [2, 32, 128, 1024], P(None, 'fsdp')
- grad_hidden: float32 [2, 32, 128, 1024], P(None, 'fsdp')
- grad_encoder: float32 [2, 32, 256, 1024], P(None, 'fsdp')
- grad_gain_self: float32 [1024], P('fsdp')
- grad_gain_cross: float32 [1024], P('fsdp')
- grad_gain_ffn: float32 [1024], P('fsdp')
- grad_rel_bias: float32 [512], P('fsdp')
- grad_self_query: float32 [1024, 1024], P('fsdp')
- grad_self_key: float32 [1024, 1024], P('fsdp')
- grad_self_value: float32 [1024, 1024], P('fsdp')
- grad_self_out: float32 [1024, 1024], P('fsdp')
- grad_cross_query: float32 [1024, 1024], P('fsdp')
- grad_cross_key: float32 [1024, 1024], P('fsdp')
- grad_cross_value: float32 [1024, 1024], P('fsdp')
- grad_cross_out: float32 [1024, 1024], P('fsdp')
- grad_feed_gate: float32 [1024, 2816], P('fsdp')
- grad_feed_up: float32 [1024, 2816], P('fsdp')
- grad_feed_down: float32 [2816, 1024], P('fsdp')
The draws below stay inside these ranges and needn't reach their ends.
Inputs may be any that keep to these rules, and one draw needn't show every extreme that they name: `enc_rows`: live encoder rows of each block; in every micro-batch some block has all 256. `dealing`: each micro-batch's row names every block once. `segment_ids`: document ids never fall along a block; a document has at most 64 tokens.
All inputs are finite; a program needn't handle non-finite values.
Results may differ from the reference program's by a relative error of at most 0.02.
The reference program's roundings to bfloat16 on the way count: a program that leaves them out, or rounds other values in their place, can miss the bound.
Values may be sent and summed in bfloat16 or wider, within the bound.
A program may use at most 192 MiB of HBM per device.

```python
import math
import jax
import jax.numpy as jnp
import numpy as np
from jax import lax

D = 1024
H = 16
DH = 64
FF = 2816
NB = 32
SEQ = 128
ENC = 256
MB = 2
DOCS = 4
SEQS = 32


def draw_enc_rows(key, part):
    lengths = jax.random.randint(key, (MB, SEQS), ENC // 4, ENC + 1)
    chosen = jax.random.randint(jax.random.fold_in(key, 7), (MB,), 0, SEQS)
    filled = jnp.arange(SEQS)[None, :] == chosen[:, None]
    return jnp.where(filled, ENC, lengths).astype(jnp.int32)


def touch_ends(values, stream_key, low, high):
    longest = values.shape.index(max(values.shape))
    spots = []
    for shift in (0, 1):
        where = [jax.random.randint(jax.random.fold_in(stream_key, axis), (), 0, length) for axis, length in enumerate(values.shape)]
        where[longest] = (where[longest] + shift) % values.shape[longest]
        spots.append(tuple(where))
    return values.at[spots[0]].set(low).at[spots[1]].set(high)


def block_levels(key, dims, shards, least, high):
    def one(dim, shards_of):
        heights = jax.random.uniform(jax.random.fold_in(jax.random.fold_in(key, 6), dim), (shards_of,), jnp.float32, least / len(shards), high / len(shards))
        return jnp.repeat(jnp.exp(heights), dims[dim] // shards_of).reshape((-1,) + (1,) * (len(dims) - dim - 1))

    factor_of = one(*shards[0])
    for cut in shards[1:]:
        factor_of = factor_of * one(*cut)
    return factor_of


def profile(count, total, bound, slope):
    weights = [(1 << 20) // math.isqrt(rank ** slope) + 1 for rank in range(2, count + 1)]
    surplus, holding = total - bound - (count - 1), [1] * (count - 1)
    while surplus > 0:
        free = [i for i in range(count - 1) if holding[i] < bound]
        whole, budget = sum([weights[i] for i in free]), surplus
        for i in free:
            addition = min(bound - holding[i], max(1, budget * weights[i] // whole), surplus)
            holding[i] = holding[i] + addition
            surplus = surplus - addition
    return np.array([bound] + holding)


def uneven_parts(stream_key, amount, total, reach, lean):
    if amount == 2:
        one = jax.random.randint(stream_key, (), max(1, total - reach), min(reach, total - 1) + 1)
        return jnp.stack([one, total - one])
    tallies = jnp.asarray(profile(amount, total, reach, lean), jnp.int32)
    twos = (amount - 1) // 2
    donor, taker = tallies[1:1 + 2 * twos:2], tallies[2:2 + 2 * twos:2]
    room = jnp.minimum(donor - 1, reach - taker)
    moved = jax.random.randint(jax.random.fold_in(stream_key, 1), (twos,), 0, 1 << 20) % (room + 1)
    tallies = tallies.at[1:1 + 2 * twos:2].set(donor - moved).at[2:2 + 2 * twos:2].set(taker + moved)
    return tallies[jax.random.permutation(jax.random.fold_in(stream_key, 2), amount)]


def gaussian(key, dims, deviation, most, cuts=(), kind=jnp.bfloat16):
    values = deviation * jax.random.normal(key, dims, jnp.float32)
    if cuts:
        values = values * block_levels(key, dims, cuts, -0.22, 0.18)
    return jnp.clip(values, -most, most).astype(kind)


def setup_inputs(seed: int = 0) -> dict:
    key_list = jax.random.split(jax.random.key(seed), 23)
    hidden = gaussian(key_list[0], (MB, SEQS, SEQ, D), 1.0, 6.0, ((1, 32),))
    encoder = gaussian(key_list[1], (MB, SEQS, ENC, D), 1.0, 6.0, ((1, 32),))
    cotangent = gaussian(key_list[2], (MB, SEQS, SEQ, D), 1.0, 6.0, ((1, 32),))
    segment_ids = jax.vmap(lambda own: jnp.searchsorted(jnp.cumsum(uneven_parts(own, DOCS, SEQ, SEQ // 2, 0)), jnp.arange(SEQ), side="right"))(jax.random.split(key_list[3], MB * SEQS)).reshape((MB, SEQS, SEQ)).astype(jnp.int32)
    rel_buckets = touch_ends(jax.random.randint(key_list[4], (MB, SEQS, SEQ), 0, NB), jax.random.fold_in(key_list[4], 1), 0, NB - 1).astype(jnp.int32)
    enc_rows = draw_enc_rows(jax.random.fold_in(key_list[22], 71), 0)
    dealing = jax.vmap(lambda own: jax.random.permutation(own, SEQS))(jax.random.split(key_list[6], MB)).reshape((MB, SEQS)).astype(jnp.int32)
    gain_self = jnp.clip(1.0 + 0.1 * jax.random.normal(key_list[7], (D,), jnp.float32), 0.5, 1.5).astype(jnp.bfloat16)
    gain_cross = jnp.clip(1.0 + 0.1 * jax.random.normal(key_list[8], (D,), jnp.float32), 0.5, 1.5).astype(jnp.bfloat16)
    gain_ffn = jnp.clip(1.0 + 0.1 * jax.random.normal(key_list[9], (D,), jnp.float32), 0.5, 1.5).astype(jnp.bfloat16)
    rel_bias = gaussian(key_list[10], (H * NB,), 1.0, 4.0, ((0, 32),))
    self_query = gaussian(key_list[11], (D, D), (D * 16) ** -0.5, 0.046875, ((0, 32),))
    self_key = gaussian(key_list[12], (D, D), D ** -0.5, 0.1875, ((0, 32),))
    self_value = gaussian(key_list[13], (D, D), D ** -0.5, 0.1875, ((0, 32),))
    self_out = gaussian(key_list[14], (D, D), (D // 8) ** -0.5, 0.5, ((0, 32),))
    cross_query = gaussian(key_list[15], (D, D), (D * 16) ** -0.5, 0.046875, ((0, 32),))
    cross_key = gaussian(key_list[16], (D, D), D ** -0.5, 0.1875, ((0, 32),))
    cross_value = gaussian(key_list[17], (D, D), D ** -0.5, 0.1875, ((0, 32),))
    cross_out = gaussian(key_list[18], (D, D), (D // 8) ** -0.5, 0.5, ((0, 32),))
    feed_gate = gaussian(key_list[19], (D, FF), D ** -0.5, 0.1875, ((0, 32),))
    feed_up = gaussian(key_list[20], (D, FF), D ** -0.5, 0.1875, ((0, 32),))
    feed_down = gaussian(key_list[21], (FF, D), (FF // 2) ** -0.5, 0.15625, ((0, 32),))
    return dict(hidden=hidden, encoder=encoder, cotangent=cotangent, segment_ids=segment_ids, rel_buckets=rel_buckets, enc_rows=enc_rows, dealing=dealing, gain_self=gain_self, gain_cross=gain_cross, gain_ffn=gain_ffn, rel_bias=rel_bias, self_query=self_query, self_key=self_key, self_value=self_value, self_out=self_out, cross_query=cross_query, cross_key=cross_key, cross_value=cross_value, cross_out=cross_out, feed_gate=feed_gate, feed_up=feed_up, feed_down=feed_down)


@jax.custom_vjp
def low(v):
    return lax.optimization_barrier(v.astype(jnp.bfloat16)).astype(jnp.float32)

@jax.custom_vjp
def low_back(v):
    return v

def low_keep(v):
    return (low(v), None)

def low_pass(kept, grad):
    return (grad,)

def back_keep(v):
    return (v, None)

def back_low(kept, grad):
    return (low(grad),)
low.defvjp(low_keep, low_pass)
low_back.defvjp(back_keep, back_low)
eps_norm = 1e-06
masked_score = -1000000000.0
highest = lax.Precision.HIGHEST

def product(left_side, right_side):
    return jnp.dot(left_side, right_side, precision=highest, preferred_element_type=jnp.float32)

def scaled_norm(values, gain_row):
    mean_square = lax.optimization_barrier(jnp.mean(values * values, axis=-1, keepdims=True))
    return values * lax.rsqrt(mean_square + eps_norm) * gain_row

def head_split(matrix):
    return matrix.reshape(matrix.shape[0], H, DH)

def attend(queries, keys_in, values, bias_grid, allowed):
    scores = jnp.einsum('ihd,jhd->hij', head_split(queries), head_split(keys_in), precision=highest) + bias_grid
    scores = jnp.where(allowed[None], low_back(scores), masked_score)
    largest = lax.optimization_barrier(jnp.max(scores, axis=2, keepdims=True))
    weights = jnp.exp(scores - largest)
    probs_low = low(weights / lax.optimization_barrier(jnp.sum(weights, axis=2, keepdims=True)))
    mixed_heads = jnp.einsum('hij,jhd->ihd', probs_low, head_split(values), precision=highest)
    return low(low_back(mixed_heads.reshape(queries.shape[0], D)))

def decoder_layer(params, hidden_in, encoder_in, seq_segments, seq_buckets, live_rows):
    gain_self, gain_cross, gain_ffn, bias_flat, self_query, self_key, self_value, self_out, cross_query, cross_key, cross_value, cross_out, feed_gate, feed_up, feed_down = params
    length = hidden_in.shape[0]
    enc_count = encoder_in.shape[0]
    positions = jnp.arange(length, dtype=jnp.int32)
    offsets = jnp.clip(positions[:, None] - positions[None, :], 0, length - 1).astype(jnp.int32)
    allowed = (positions[None, :] <= positions[:, None]) & (seq_segments[:, None] == seq_segments[None, :])
    bias_table = bias_flat.reshape(H, NB)
    bias_grid = bias_table[:, seq_buckets[offsets]]
    cross_allowed = jnp.broadcast_to(jnp.arange(enc_count, dtype=jnp.int32)[None, :] < live_rows, (length, enc_count))
    normed_one = low(scaled_norm(hidden_in, gain_self))
    queries = low(low_back(product(normed_one, self_query)))
    keys_self = low(low_back(product(normed_one, self_key)))
    values_self = low(low_back(product(normed_one, self_value)))
    mixed_self = attend(queries, keys_self, values_self, bias_grid, allowed)
    first_sum = hidden_in + low_back(product(mixed_self, self_out))
    normed_two = low(scaled_norm(first_sum, gain_cross))
    cross_queries = low(low_back(product(normed_two, cross_query)))
    cross_keys = low(low_back(product(encoder_in, cross_key)))
    cross_values = low(low_back(product(encoder_in, cross_value)))
    mixed_cross = attend(cross_queries, cross_keys, cross_values, 0.0, cross_allowed)
    second_sum = first_sum + low_back(product(mixed_cross, cross_out))
    normed_three = low(scaled_norm(second_sum, gain_ffn))
    gate_pre = low_back(product(normed_three, feed_gate))
    up_pre = low_back(product(normed_three, feed_up))
    hidden_units = low(jax.nn.gelu(gate_pre, approximate=True) * up_pre)
    return second_sum + low_back(product(hidden_units, feed_down))

def reference(hidden, encoder, cotangent, segment_ids, rel_buckets, enc_rows, dealing, gain_self, gain_cross, gain_ffn, rel_bias, self_query, self_key, self_value, self_out, cross_query, cross_key, cross_value, cross_out, feed_gate, feed_up, feed_down):
    params = tuple((weight.astype(jnp.float32) for weight in (gain_self, gain_cross, gain_ffn, rel_bias, self_query, self_key, self_value, self_out, cross_query, cross_key, cross_value, cross_out, feed_gate, feed_up, feed_down)))
    slot_count = MB * SEQS
    source = dealing.reshape(slot_count).astype(jnp.int32)

    def one_slot(running, slot_index):
        micro_step = slot_index // SEQS
        given_seq = source[slot_index]
        seq_hidden = hidden[micro_step, given_seq].astype(jnp.float32)
        seq_encoder = encoder[micro_step, given_seq].astype(jnp.float32)
        seq_segments = segment_ids[micro_step, given_seq]
        seq_buckets = rel_buckets[micro_step, given_seq]
        live_rows = enc_rows[micro_step, given_seq]

        def local_layer(weights_in, hidden_in, encoder_in):
            return decoder_layer(weights_in, hidden_in, encoder_in, seq_segments, seq_buckets, live_rows)
        result, pull_back = jax.vjp(local_layer, params, seq_hidden, seq_encoder)
        grad_params, grad_seq_hidden, grad_seq_encoder = pull_back(cotangent[micro_step, slot_index % SEQS].astype(jnp.float32))
        running = tuple((earlier + later for earlier, later in zip(running, grad_params)))
        return (running, (result.astype(jnp.bfloat16), grad_seq_hidden, grad_seq_encoder))
    zero_grads = tuple((jnp.zeros(weight.shape, jnp.float32) for weight in params))
    totals, (results, grad_work, grad_enc_work) = lax.scan(one_slot, zero_grads, jnp.arange(slot_count, dtype=jnp.int32))
    layer_out = results.reshape(MB, SEQS, SEQ, D)
    inverse = jnp.argsort(dealing, axis=1)
    grad_hidden = jnp.take_along_axis(grad_work.reshape(MB, SEQS, SEQ, D), inverse[:, :, None, None], axis=1)
    grad_encoder = jnp.take_along_axis(grad_enc_work.reshape(MB, SEQS, ENC, D), inverse[:, :, None, None], axis=1)
    return (layer_out, grad_hidden, grad_encoder, totals[0], totals[1], totals[2], totals[3], totals[4], totals[5], totals[6], totals[7], totals[8], totals[9], totals[10], totals[11], totals[12], totals[13], totals[14])
```

```python
import jax
import jax.numpy as jnp
from jax import lax
from jax.sharding import PartitionSpec as P

D = 1024
H = 16
DH = 64
NB = 32

AXIS = "fsdp"
eps_norm = 1e-06
masked_score = -1000000000.0
highest = lax.Precision.HIGHEST
f32 = jnp.float32
bf16 = jnp.bfloat16


def product(left_side, right_side):
    return jnp.dot(left_side, right_side, preferred_element_type=f32)


def product_left(left_side, right_side):
    return lax.dot_general(
        left_side, right_side, (((0,), (0,)), ((), ())), preferred_element_type=f32
    )


def product_right(left_side, right_side):
    return lax.dot_general(
        left_side, right_side, (((1,), (1,)), ((), ())), preferred_element_type=f32
    )


def inverse_rms(values):
    return lax.rsqrt(jnp.mean(values * values, axis=-1, keepdims=True) + eps_norm)


def norm_back(values, inverse, gain_row, grad):
    scaled = values * inverse
    weighted = grad * gain_row
    centre = jnp.mean(weighted * scaled, axis=-1, keepdims=True)
    return inverse * (weighted - scaled * centre), jnp.sum(grad * scaled, axis=0)


def gelu_parts(gate_pre):
    root = 0.7978845608028654
    inner = root * (gate_pre + 0.044715 * gate_pre * gate_pre * gate_pre)
    curve = jnp.tanh(inner)
    value = 0.5 * gate_pre * (1.0 + curve)
    slope = 0.5 * (1.0 + curve) + 0.5 * gate_pre * (1.0 - curve * curve) * root * (
        1.0 + 3 * 0.044715 * gate_pre * gate_pre
    )
    return value, slope


def toeplitz_expand(per_offset):
    head_count, length = per_offset.shape
    filler = jnp.zeros((head_count, 1), f32)
    pattern = jnp.concatenate(
        [per_offset[:, :1], filler, per_offset[:, ::-1][:, : length - 1]], axis=1
    )
    tiled_rows = jnp.broadcast_to(pattern[:, None, :], (head_count, length, length + 1))
    return tiled_rows.reshape(head_count, length * (length + 1))[:, : length * length].reshape(
        head_count, length, length
    )


def toeplitz_fold(score_grid):
    head_count, length = (score_grid.shape[0], score_grid.shape[1])
    flat_grid = score_grid.reshape(head_count, length * length)
    padded = jnp.concatenate([flat_grid, jnp.zeros((head_count, length), f32)], axis=1)
    columns = jnp.sum(padded.reshape(head_count, length, length + 1), axis=1)
    return jnp.concatenate([columns[:, :1], columns[:, 2:][:, ::-1]], axis=1)


def heads(matrix, blocks):
    return matrix.reshape(blocks, -1, H, DH)


def score_block(queries, keys_in, bias_grid, allowed):
    scores = jnp.einsum("bihd,bjhd->bhij", queries, keys_in, preferred_element_type=f32)
    if bias_grid is not None:
        scores = scores + bias_grid
    return jnp.where(allowed[:, None], scores, masked_score)


def attend(queries, keys_in, values, bias_grid, allowed):
    blocks = allowed.shape[0]
    scores = score_block(heads(queries, blocks), heads(keys_in, blocks), bias_grid, allowed)
    largest = jnp.max(scores, axis=3, keepdims=True)
    weights = jnp.exp(scores - largest)
    probs = weights / jnp.sum(weights, axis=3, keepdims=True)
    mixed = jnp.einsum(
        "bhij,bjhd->bihd", probs.astype(bf16), heads(values, blocks), preferred_element_type=f32
    )
    return mixed.reshape(queries.shape[0], D).astype(bf16), probs


def attend_back(queries, keys_in, values, probs, grad_mixed):
    blocks = probs.shape[0]
    grad_heads = heads(grad_mixed, blocks)
    grad_values = jnp.einsum(
        "bhij,bihd->bjhd", probs.astype(bf16), grad_heads, preferred_element_type=f32
    )
    grad_probs = jnp.einsum(
        "bihd,bjhd->bhij", grad_heads, heads(values, blocks), preferred_element_type=f32
    )
    grad_scores = (
        probs * (grad_probs - jnp.sum(probs * grad_probs, axis=3, keepdims=True))
    ).astype(bf16)
    grad_queries = jnp.einsum(
        "bhij,bjhd->bihd", grad_scores, heads(keys_in, blocks), preferred_element_type=f32
    )
    grad_keys = jnp.einsum(
        "bhij,bihd->bjhd", grad_scores, heads(queries, blocks), preferred_element_type=f32
    )
    return (
        grad_queries.reshape(-1, D).astype(bf16),
        grad_keys.reshape(-1, D).astype(bf16),
        grad_values.reshape(-1, D).astype(bf16),
        grad_scores,
    )


def redeal(blocks, source):
    micro, own, rows, width = blocks.shape
    count = source.shape[1] // own
    cut = blocks.reshape(micro, own, count, rows // count, width).transpose(2, 0, 1, 3, 4)
    spread = lax.all_to_all(cut, AXIS, split_axis=0, concat_axis=0, tiled=True)
    spread = spread.transpose(1, 0, 2, 3, 4).reshape(micro, count * own, rows // count, width)
    moved = jnp.take_along_axis(spread, source[:, :, None, None], axis=1)
    moved = moved.reshape(micro, count, own, rows // count, width).transpose(1, 0, 2, 3, 4)
    home = lax.all_to_all(moved, AXIS, split_axis=0, concat_axis=0, tiled=True)
    return home.transpose(1, 2, 0, 3, 4).reshape(micro, own, rows, width)


def gather_weights(wide, deep):
    packed = lax.all_gather(jnp.concatenate(wide, axis=1), AXIS, axis=0, tiled=True)
    whole, start = [], 0
    for part in wide:
        whole.append(packed[:, start : start + part.shape[1]])
        start += part.shape[1]
    return whole, lax.all_gather(deep, AXIS, axis=0, tiled=True)


def scatter_grads(wide, deep):
    packed = jnp.concatenate([part.astype(bf16) for part in wide], axis=1)
    packed = lax.psum_scatter(packed, AXIS, scatter_dimension=0, tiled=True).astype(f32)
    pieces, start = [], 0
    for part in wide:
        pieces.append(packed[:, start : start + part.shape[1]])
        start += part.shape[1]
    deep = lax.psum_scatter(deep.astype(bf16), AXIS, scatter_dimension=0, tiled=True)
    return pieces, deep.astype(f32)


def body(
    hidden,
    encoder,
    cotangent,
    segment_ids,
    rel_buckets,
    enc_rows,
    dealing,
    gain_self,
    gain_cross,
    gain_ffn,
    rel_bias,
    self_query,
    self_key,
    self_value,
    self_out,
    cross_query,
    cross_key,
    cross_value,
    cross_out,
    feed_gate,
    feed_up,
    feed_down,
):
    device = lax.axis_index(AXIS)
    micro, own, length, _ = hidden.shape
    enc_count = encoder.shape[2]
    blocks = micro * own
    first = device * own

    def mine(table):
        return lax.dynamic_slice_in_dim(table, first, own, axis=1).reshape(
            (blocks,) + table.shape[2:]
        )

    segments, buckets, live = mine(segment_ids), mine(rel_buckets), mine(enc_rows)
    grad_out = redeal(cotangent, jnp.argsort(dealing, axis=1)).reshape(blocks * length, D)

    small = jnp.concatenate([gain_self, gain_cross, gain_ffn, rel_bias])
    smalls = lax.all_gather(small, AXIS, axis=0)
    part = gain_self.shape[0]
    gain_one, gain_two, gain_three = [
        smalls[:, k * part : (k + 1) * part].reshape(D).astype(f32) for k in range(3)
    ]
    bias_table = smalls[:, 3 * part :].reshape(H, NB).astype(f32)
    (wq, wk, wv, wo, xq, xk, xv, xo, gate, up), down = gather_weights(
        (
            self_query,
            self_key,
            self_value,
            self_out,
            cross_query,
            cross_key,
            cross_value,
            cross_out,
            feed_gate,
            feed_up,
        ),
        feed_down,
    )

    positions = jnp.arange(length, dtype=jnp.int32)
    allowed = (positions[None, :] <= positions[:, None])[None] & (
        segments[:, :, None] == segments[:, None, :]
    )
    cross_allowed = jnp.broadcast_to(
        jnp.arange(enc_count, dtype=jnp.int32)[None, None, :] < live[:, None, None],
        (blocks, length, enc_count),
    )
    onehot = (buckets[:, :, None] == jnp.arange(NB, dtype=jnp.int32)).astype(f32)
    per_offset = jnp.einsum("hc,boc->bho", bias_table, onehot, precision=highest)
    bias_grid = toeplitz_expand(per_offset.reshape(blocks * H, length)).reshape(
        blocks, H, length, length
    )

    wide_in = hidden.reshape(blocks * length, D).astype(f32)
    enc_in = encoder.reshape(blocks * enc_count, D)
    inv_one = inverse_rms(wide_in)
    normed_one = (wide_in * inv_one * gain_one).astype(bf16)
    queries = product(normed_one, wq).astype(bf16)
    keys_self = product(normed_one, wk).astype(bf16)
    values_self = product(normed_one, wv).astype(bf16)
    mixed_self, probs_self = attend(queries, keys_self, values_self, bias_grid, allowed)
    first_sum = wide_in + product(mixed_self, wo)
    inv_two = inverse_rms(first_sum)
    normed_two = (first_sum * inv_two * gain_two).astype(bf16)
    cross_queries = product(normed_two, xq).astype(bf16)
    cross_keys = product(enc_in, xk).astype(bf16)
    cross_values = product(enc_in, xv).astype(bf16)
    mixed_cross, probs_cross = attend(
        cross_queries, cross_keys, cross_values, None, cross_allowed
    )
    second_sum = first_sum + product(mixed_cross, xo)
    inv_three = inverse_rms(second_sum)
    normed_three = (second_sum * inv_three * gain_three).astype(bf16)
    gate_pre = product(normed_three, gate)
    up_pre = product(normed_three, up)
    act, slope = gelu_parts(gate_pre)
    hidden_units = (act * up_pre).astype(bf16)
    result = (second_sum + product(hidden_units, down)).astype(bf16)
    layer_out = redeal(result.reshape(micro, own, length, D), dealing)

    g_down = product_left(hidden_units, grad_out)
    grad_units = product_right(grad_out, down)
    grad_gate = (grad_units * up_pre * slope).astype(bf16)
    grad_up = (grad_units * act).astype(bf16)
    g_gate = product_left(normed_three, grad_gate)
    g_up = product_left(normed_three, grad_up)
    grad_three = product_right(grad_gate, gate) + product_right(grad_up, up)
    back, g_gain_three = norm_back(second_sum, inv_three, gain_three, grad_three)
    grad_second = grad_out.astype(f32) + back
    grad_low = grad_second.astype(bf16)
    g_xo = product_left(mixed_cross, grad_low)
    grad_mixed = product_right(grad_low, xo).astype(bf16)
    grad_cq, grad_ck, grad_cv, _ = attend_back(
        cross_queries, cross_keys, cross_values, probs_cross, grad_mixed
    )
    g_xq = product_left(normed_two, grad_cq)
    g_xk = product_left(enc_in, grad_ck)
    g_xv = product_left(enc_in, grad_cv)
    grad_enc = product_right(grad_ck, xk) + product_right(grad_cv, xv)
    back, g_gain_two = norm_back(first_sum, inv_two, gain_two, product_right(grad_cq, xq))
    grad_first = grad_second + back
    grad_low = grad_first.astype(bf16)
    g_so = product_left(mixed_self, grad_low)
    grad_mixed = product_right(grad_low, wo).astype(bf16)
    grad_sq, grad_sk, grad_sv, grad_scores = attend_back(
        queries, keys_self, values_self, probs_self, grad_mixed
    )
    offsets = toeplitz_fold(
        grad_scores.astype(f32).reshape(blocks * H, length, length)
    ).reshape(blocks, H, length)
    g_bias = jnp.einsum("bho,boc->hc", offsets, onehot, precision=highest).reshape(H * NB)
    g_sq = product_left(normed_one, grad_sq)
    g_sk = product_left(normed_one, grad_sk)
    g_sv = product_left(normed_one, grad_sv)
    grad_one = (
        product_right(grad_sq, wq) + product_right(grad_sk, wk) + product_right(grad_sv, wv)
    )
    back, g_gain_one = norm_back(wide_in, inv_one, gain_one, grad_one)
    grad_in = grad_first + back

    pieces, piece_down = scatter_grads(
        (g_sq, g_sk, g_sv, g_so, g_xq, g_xk, g_xv, g_xo, g_gate, g_up), g_down
    )
    count = smalls.shape[0]
    small_grads = jnp.concatenate(
        [g.reshape(count, -1) for g in (g_gain_one, g_gain_two, g_gain_three, g_bias)], axis=1
    )
    small_sum = jnp.sum(
        lax.all_to_all(small_grads, AXIS, split_axis=0, concat_axis=0, tiled=True), axis=0
    )
    return (
        layer_out,
        grad_in.reshape(hidden.shape),
        grad_enc.reshape(encoder.shape),
        small_sum[:part],
        small_sum[part : 2 * part],
        small_sum[2 * part : 3 * part],
        small_sum[3 * part :],
        *pieces,
        piece_down,
    )


def solution(mesh):
    block = P(None, AXIS, None, None)
    row = P(AXIS)
    matrix = P(AXIS, None)
    return jax.shard_map(
        body,
        mesh=mesh,
        in_specs=(block,) * 3 + (P(),) * 4 + (row,) * 4 + (matrix,) * 11,
        out_specs=(block,) * 3 + (row,) * 4 + (matrix,) * 11,
        check_vma=False,
    )
```

```python
import functools

import jax
import jax.numpy as jnp
from jax import lax
from jax.experimental import pallas as pl
from jax.experimental.pallas import tpu as pltpu
from jax.sharding import PartitionSpec as P

D = 1024
H = 16
DH = 64
NB = 32

AXIS = "fsdp"
eps_norm = 1e-06
masked_score = -1000000000.0
highest = lax.Precision.HIGHEST
f32 = jnp.float32
bf16 = jnp.bfloat16


def product(left_side, right_side):
    return jnp.dot(left_side, right_side, preferred_element_type=f32)


def product_left(left_side, right_side):
    return lax.dot_general(
        left_side, right_side, (((0,), (0,)), ((), ())), preferred_element_type=f32
    )


def product_right(left_side, right_side):
    return lax.dot_general(
        left_side, right_side, (((1,), (1,)), ((), ())), preferred_element_type=f32
    )


def inverse_rms(values):
    return lax.rsqrt(jnp.mean(values * values, axis=-1, keepdims=True) + eps_norm)


def norm_back(values, inverse, gain_row, grad):
    scaled = values * inverse
    weighted = grad * gain_row
    centre = jnp.mean(weighted * scaled, axis=-1, keepdims=True)
    return inverse * (weighted - scaled * centre), jnp.sum(grad * scaled, axis=0)


def gelu_parts(gate_pre):
    root = 0.7978845608028654
    inner = root * (gate_pre + 0.044715 * gate_pre * gate_pre * gate_pre)
    curve = jnp.tanh(inner)
    value = 0.5 * gate_pre * (1.0 + curve)
    slope = 0.5 * (1.0 + curve) + 0.5 * gate_pre * (1.0 - curve * curve) * root * (
        1.0 + 3 * 0.044715 * gate_pre * gate_pre
    )
    return value, slope


def toeplitz_expand(per_offset):
    head_count, length = per_offset.shape
    filler = jnp.zeros((head_count, 1), f32)
    pattern = jnp.concatenate(
        [per_offset[:, :1], filler, per_offset[:, ::-1][:, : length - 1]], axis=1
    )
    tiled_rows = jnp.broadcast_to(pattern[:, None, :], (head_count, length, length + 1))
    return tiled_rows.reshape(head_count, length * (length + 1))[:, : length * length].reshape(
        head_count, length, length
    )


def toeplitz_fold(score_grid):
    head_count, length = (score_grid.shape[0], score_grid.shape[1])
    flat_grid = score_grid.reshape(head_count, length * length)
    padded = jnp.concatenate([flat_grid, jnp.zeros((head_count, length), f32)], axis=1)
    columns = jnp.sum(padded.reshape(head_count, length, length + 1), axis=1)
    return jnp.concatenate([columns[:, :1], columns[:, 2:][:, ::-1]], axis=1)


def heads(matrix, blocks):
    return matrix.reshape(blocks, -1, H, DH)


def score_block(queries, keys_in, bias_grid, allowed):
    scores = jnp.einsum("bihd,bjhd->bhij", queries, keys_in, preferred_element_type=f32)
    if bias_grid is not None:
        scores = scores + bias_grid
    return jnp.where(allowed[:, None], scores, masked_score)


def attend(queries, keys_in, values, bias_grid, allowed):
    blocks = allowed.shape[0]
    scores = score_block(heads(queries, blocks), heads(keys_in, blocks), bias_grid, allowed)
    largest = jnp.max(scores, axis=3, keepdims=True)
    weights = jnp.exp(scores - largest)
    probs = weights / jnp.sum(weights, axis=3, keepdims=True)
    mixed = jnp.einsum(
        "bhij,bjhd->bihd", probs.astype(bf16), heads(values, blocks), preferred_element_type=f32
    )
    return mixed.reshape(queries.shape[0], D).astype(bf16), probs


def attend_back(queries, keys_in, values, probs, grad_mixed):
    blocks = probs.shape[0]
    grad_heads = heads(grad_mixed, blocks)
    grad_values = jnp.einsum(
        "bhij,bihd->bjhd", probs.astype(bf16), grad_heads, preferred_element_type=f32
    )
    grad_probs = jnp.einsum(
        "bihd,bjhd->bhij", grad_heads, heads(values, blocks), preferred_element_type=f32
    )
    grad_scores = (
        probs * (grad_probs - jnp.sum(probs * grad_probs, axis=3, keepdims=True))
    ).astype(bf16)
    grad_queries = jnp.einsum(
        "bhij,bjhd->bihd", grad_scores, heads(keys_in, blocks), preferred_element_type=f32
    )
    grad_keys = jnp.einsum(
        "bhij,bihd->bjhd", grad_scores, heads(queries, blocks), preferred_element_type=f32
    )
    return (
        grad_queries.reshape(-1, D).astype(bf16),
        grad_keys.reshape(-1, D).astype(bf16),
        grad_values.reshape(-1, D).astype(bf16),
        grad_scores,
    )


def redeal(blocks, source):
    micro, own, rows, width = blocks.shape
    count = source.shape[1] // own
    cut = blocks.reshape(micro, own, count, rows // count, width).transpose(2, 0, 1, 3, 4)
    spread = lax.all_to_all(cut, AXIS, split_axis=0, concat_axis=0, tiled=True)
    spread = spread.transpose(1, 0, 2, 3, 4).reshape(micro, count * own, rows // count, width)
    moved = jnp.take_along_axis(spread, source[:, :, None, None], axis=1)
    moved = moved.reshape(micro, count, own, rows // count, width).transpose(1, 0, 2, 3, 4)
    home = lax.all_to_all(moved, AXIS, split_axis=0, concat_axis=0, tiled=True)
    return home.transpose(1, 2, 0, 3, 4).reshape(micro, own, rows, width)


def gather_weights(wide, deep):
    packed = lax.all_gather(jnp.concatenate(wide, axis=1), AXIS, axis=0, tiled=True)
    whole, start = [], 0
    for part in wide:
        whole.append(packed[:, start : start + part.shape[1]])
        start += part.shape[1]
    return whole, lax.all_gather(deep, AXIS, axis=0, tiled=True)


def scatter_grads(wide, deep):
    packed = jnp.concatenate([part.astype(bf16) for part in wide], axis=1)
    packed = lax.psum_scatter(packed, AXIS, scatter_dimension=0, tiled=True).astype(f32)
    pieces, start = [], 0
    for part in wide:
        pieces.append(packed[:, start : start + part.shape[1]])
        start += part.shape[1]
    deep = lax.psum_scatter(deep.astype(bf16), AXIS, scatter_dimension=0, tiled=True)
    return pieces, deep.astype(f32)


MESH = pl.DeviceIdType.MESH
RING = 3
SLOTS = 5


class Place:
    def __init__(self, depth):
        self.depth = depth
        self.count = depth * 8
        self.me = lax.axis_index(AXIS)
        self.core = self.me % 2
        self.x = (self.me // 2) % 2
        self.y = (self.me // 4) % 2
        self.z = self.me // 8
        self.twin = self.me + 1 - 2 * self.core
        self.over_x = self.me + 2 - 4 * self.x
        self.over_y = self.me + 4 - 8 * self.y
        self.far = [(self.z + d) % depth for d in range(1, depth)]
        self.over_z = [self.me + (z - self.z) * 8 for z in self.far]

    def greet(self):
        barrier = pltpu.get_barrier_semaphore()

        def hello(d, _):
            peer = (self.me + d) % self.count
            pl.semaphore_signal(barrier, inc=1, device_id=(peer,), device_id_type=MESH)
            return 0

        lax.fori_loop(1, self.count, hello, 0)
        pl.semaphore_wait(barrier, self.count - 1)


def remote(source, target, send, recv, index, device):
    return pltpu.make_async_remote_copy(
        src_ref=source,
        dst_ref=target,
        send_sem=send.at[index],
        recv_sem=recv.at[index],
        device_id=(device,),
        device_id_type=MESH,
    )


def columns(start, width):
    return pl.ds(pl.multiple_of(start, 128), width)


class Gather:
    def __init__(self, place, pieces, staged, wholes, local, send, recv):
        self.place, self.pieces = place, pieces
        self.staged, self.wholes = staged, wholes
        self.local, self.send, self.recv = local, send, recv
        self.steps = 1 + 2 * (place.depth + 2)
        self.sent = []

    def begin(self, copy):
        copy.start()
        self.sent.append(copy)

    def rows(self, kind):
        height = self.staged[kind].shape[0]
        p = self.place
        return self.wholes[kind].at[p.z, p.y, p.x, pl.ds(p.core * height, height)]

    def quarter(self, i, core, order):
        kind, start, width = self.pieces[i]
        return columns(start + core * (width // 2) + order * (width // 4), width // 4)

    def copy(self, source, target, i, step, device):
        return remote(source, target, self.send, self.recv, i * self.steps + step, device)

    def to_twin(self, i):
        kind, start, width = self.pieces[i]
        cols = columns(start + (1 - self.place.core) * (width // 2), width // 2)
        return self.copy(
            self.staged[kind].at[:, cols], self.rows(kind).at[:, cols], i, 0, self.place.twin
        )

    def own(self, i):
        kind, start, width = self.pieces[i]
        cols = columns(start + self.place.core * (width // 2), width // 2)
        return pltpu.make_async_copy(
            self.staged[kind].at[:, cols], self.rows(kind).at[:, cols], self.local.at[i]
        )

    def along_z(self, i, order, d):
        p = self.place
        ref = self.wholes[self.pieces[i][0]].at[p.z, p.y, p.x, :, self.quarter(i, p.core, order)]
        return self.copy(ref, ref, i, 1 + order * (p.depth + 2) + d, p.over_z[d])

    def plane(self, i, order, second):
        p = self.place
        whole = self.wholes[self.pieces[i][0]]
        cols = self.quarter(i, p.core, order)
        if second:
            ref = whole.at[:, :, p.x, :, cols] if order else whole.at[:, p.y, :, :, cols]
        else:
            ref = whole.at[:, p.y, p.x, :, cols]
        device = p.over_x if order == second else p.over_y
        return self.copy(ref, ref, i, 1 + order * (p.depth + 2) + p.depth - 1 + second, device)

    def across(self, i, order):
        p = self.place
        whole = self.wholes[self.pieces[i][0]]
        ref = whole.at[:, :, :, :, self.quarter(i, p.core, order)]
        return self.copy(ref, ref, i, 1 + order * (p.depth + 2) + p.depth + 1, p.twin)

    def open(self):
        for i in range(len(self.pieces)):
            self.begin(self.to_twin(i))
        for i in range(len(self.pieces)):
            self.own(i).start()
        for i in range(len(self.pieces)):
            self.own(i).wait()
        for i in range(len(self.pieces)):
            self.to_twin(i).wait_recv()
            for d in range(self.place.depth - 1):
                for order in (0, 1):
                    self.begin(self.along_z(i, order, d))

    def advance(self, i, stage):
        if not 0 <= i < len(self.pieces):
            return
        for order in (0, 1):
            if stage == 0:
                for d in range(self.place.depth - 1):
                    self.along_z(i, order, d).wait_recv()
                self.begin(self.plane(i, order, 0))
            elif stage == 1:
                self.plane(i, order, 0).wait_recv()
                self.begin(self.plane(i, order, 1))
            elif stage == 2:
                self.plane(i, order, 1).wait_recv()
                self.begin(self.across(i, order))
            else:
                self.across(i, order).wait_recv()

    def turn(self, t):
        for stage in (3, 2, 1, 0):
            self.advance(t - stage, stage)

    def close(self):
        for copy in self.sent:
            copy.wait_send()


class Scatter:
    def __init__(self, place, pieces, blocks, outs, scratch):
        self.place, self.pieces, self.blocks, self.outs = place, pieces, blocks, outs
        self.grads, self.got, self.final, (self.local, self.send, self.recv) = (
            scratch[0],
            scratch[1:5],
            scratch[5],
            scratch[6:9],
        )
        self.steps = 1 + 2 * (place.depth + 2)
        self.time = 0

    @staticmethod
    def scratch(pieces, depth, blocks):
        tall = max(blocks[kind] * (width // 512) for kind, _, width in pieces)
        copies = len(pieces) * (1 + 2 * (depth + 2))
        return [
            pltpu.VMEM((SLOTS, 2, 2, depth, 2, 2, tall, 128), bf16),
            pltpu.VMEM((RING, 2, depth, 2, 2, tall, 128), bf16),
            pltpu.VMEM((RING, 2, depth, 2, tall, 128), bf16),
            pltpu.VMEM((RING, 2, depth, tall, 128), bf16),
            pltpu.VMEM((RING, 2, depth - 1, tall, 128), bf16),
            pltpu.VMEM((RING, 2, 2, tall // 2, 128), f32),
            pltpu.SemaphoreType.DMA((2 * len(pieces),)),
            pltpu.SemaphoreType.DMA((copies,)),
            pltpu.SemaphoreType.DMA((copies,)),
        ]

    def size(self, i):
        kind, start, width = self.pieces[i]
        return kind, start // 128, width // 512, self.blocks[kind]

    def rows(self, i):
        _, _, tiles, block = self.size(i)
        return pl.ds(0, tiles * block)

    def cut(self, ref, i):
        return ref.at[(slice(None),) * (len(ref.shape) - 2) + (self.rows(i),)]

    def mine(self, i, half, *quarter):
        return self.cut(self.grads.at[(i % SLOTS, half) + quarter], i)

    def theirs(self, level, i, *index):
        return self.cut(self.got[level].at[(i % RING,) + index], i)

    def copy(self, source, target, i, step, device):
        return remote(source, target, self.send, self.recv, i * self.steps + step, device)

    def to_twin(self, i):
        return self.copy(
            self.mine(i, 1 - self.place.core), self.theirs(0, i), i, 0, self.place.twin
        )

    def plane(self, i, order, second):
        p = self.place
        ref = self.mine(i, p.core, order)
        if second:
            ref = ref.at[:, p.y, 1 - p.x] if order else ref.at[:, 1 - p.y, p.x]
        else:
            ref = ref.at[:, 1 - p.y] if order else ref.at[:, :, 1 - p.x]
        device = p.over_x if order == second else p.over_y
        step = 1 + order * (p.depth + 2) + second
        return self.copy(ref, self.theirs(1 + second, i, order), i, step, device)

    def along_z(self, i, order, d):
        p = self.place
        ref = self.mine(i, p.core, order).at[p.far[d], p.y, p.x]
        step = 1 + order * (p.depth + 2) + 2 + d
        return self.copy(ref, self.theirs(3, i, order, d), i, step, p.over_z[d])

    def ends(self, i, order, core):
        kind, first, tiles, block = self.size(i)
        count = tiles * block // 2
        row = (first + (2 * self.place.core + order) * tiles) * (block // 2)
        source = self.final.at[i % RING, order, core, pl.ds(0, count)]
        return source, self.outs[kind].at[pl.ds(pl.multiple_of(row, 8), count)]

    def rest(self, i, order):
        p = self.place
        source, target = self.ends(i, order, 1 - p.core)
        return self.copy(source, target, i, 1 + order * (p.depth + 2) + p.depth + 1, p.twin)

    def keep(self, i, order):
        source, target = self.ends(i, order, self.place.core)
        return pltpu.make_async_copy(source, target, self.local.at[2 * i + order])

    def add(self, i, order, level, spots):
        rows = self.rows(i)
        slot, ring, core = i % SLOTS, i % RING, self.place.core

        def layer(z, _):
            for there, here in spots:
                at = (slot, core, order, z) + here + (rows,)
                total = self.grads[at].astype(f32)
                total = total + self.got[level][(ring, order, z) + there + (rows,)].astype(f32)
                self.grads[at] = total.astype(bf16)
            return 0

        lax.fori_loop(0, self.place.depth, layer, 0)

    def advance(self, i, stage):
        if not 0 <= i < len(self.pieces):
            return
        p = self.place
        if stage == 1:
            self.to_twin(i).wait_recv()
            for order in (0, 1):
                self.add(i, order, 0, [((y, x), (y, x)) for y in (0, 1) for x in (0, 1)])
                self.plane(i, order, 0).start()
        elif stage == 2:
            for order in (0, 1):
                self.plane(i, order, 0).wait_recv()
                self.add(
                    i, order, 1, [((k,), (p.y, k) if order else (k, p.x)) for k in (0, 1)]
                )
                self.plane(i, order, 1).start()
        elif stage == 3:
            for order in (0, 1):
                self.plane(i, order, 1).wait_recv()
                self.add(i, order, 2, [((), (p.y, p.x))])
                for d in range(p.depth - 1):
                    self.along_z(i, order, d).start()
        elif stage == 4:
            if i >= RING:
                self.settle(i - RING)
            _, _, tiles, block = self.size(i)
            rows, half = self.rows(i), block // 2
            for order in (0, 1):
                for d in range(p.depth - 1):
                    self.along_z(i, order, d).wait_recv()
                total = self.grads[i % SLOTS, p.core, order, p.z, p.y, p.x, rows].astype(f32)
                for d in range(p.depth - 1):
                    total = total + self.got[3][i % RING, order, d, rows].astype(f32)
                for tile in range(tiles):
                    for core in (0, 1):
                        row = tile * block + core * half
                        self.final[i % RING, order, core, pl.ds(tile * half, half)] = total[
                            row : row + half
                        ]
                self.rest(i, order).start()
                self.keep(i, order).start()
        else:
            self.to_twin(i).wait_send()
            for order in (0, 1):
                self.plane(i, order, 0).wait_send()
                self.plane(i, order, 1).wait_send()
                for d in range(p.depth - 1):
                    self.along_z(i, order, d).wait_send()
                self.rest(i, order).wait_recv()

    def settle(self, i):
        for order in (0, 1):
            self.rest(i, order).wait_send()
            self.keep(i, order).wait()

    def turn(self):
        for stage in (5, 4, 3, 2, 1):
            self.advance(self.time - stage, stage)
        self.time += 1

    def produce(self, left, right, column):
        i = self.time
        self.turn()
        _, _, tiles, block = self.size(i)
        slot = i % SLOTS
        group = 1 if block % 32 == 0 else 2
        turns = self.place.depth // group
        high = 4 * block * group

        def chunk(k, _):
            n, first = k // turns, (k % turns) * group
            part = transposed(
                left[:, columns(k % turns * high, high)], right[:, columns(column + 256 * n, 256)]
            ).astype(bf16)
            for tile in (0, 1):
                for b in range(4 * group):
                    spot = first + b // 4, b // 2 % 2, b % 2
                    piece = part[b * block : b * block + block, tile * 128 : tile * 128 + 128]
                    if tiles == 2:
                        at = (slot, n // 2, n % 2) + spot + (pl.ds(tile * block, block),)
                    else:
                        at = (slot, n, tile) + spot + (pl.ds(0, block),)
                    self.grads[at] = piece
            return 0

        lax.fori_loop(0, 2 * tiles * turns, chunk, 0)
        self.to_twin(i).start()

    def close(self):
        while self.time < len(self.pieces) + 5:
            self.turn()
        for i in range(max(0, len(self.pieces) - RING), len(self.pieces)):
            self.settle(i)


class Redeal:
    def __init__(self, place, given, spread, moved, wanted, send, recv):
        self.place, self.given, self.spread, self.moved = place, given, spread, moved
        self.wanted, self.send, self.recv = wanted, send, recv
        self.high, self.wide = spread.shape[2:]

    def spot(self, ref, j):
        depth = self.place.depth
        rows = pl.ds(pl.multiple_of((j // depth) * self.high, self.high), self.high)
        return ref.at[:, rows, columns((j % depth) * self.wide, self.wide)]

    def peer(self, d):
        return (self.place.me + d) % self.place.count

    def out(self, d):
        target = self.spread.at[self.place.me]
        peer = self.peer(d)
        return remote(self.spot(self.given, peer), target, self.send, self.recv, d - 1, peer)

    def home(self, d):
        peer, count = self.peer(d), self.place.count
        target = self.spot(self.wanted, self.place.me)
        return remote(
            self.moved.at[peer], target, self.send, self.recv, count - 1 + d - 1, peer
        )

    def each(self, act):
        def one(d, _):
            act(d)
            return 0

        lax.fori_loop(1, self.place.count, one, 0)

    def own(self, ref):
        j = self.place.me
        depth = self.place.depth
        rows = pl.ds(pl.multiple_of((j // depth) * self.high, self.high), self.high)
        return slice(None), rows, columns((j % depth) * self.wide, self.wide)

    def begin(self):
        self.each(lambda d: self.out(d).start())
        self.spread[self.place.me] = self.given[self.own(self.given)]

    def middle(self, source):
        self.each(lambda d: self.out(d).wait())

        def one(j, _):
            for m in range(self.moved.shape[1]):
                self.moved[j, m] = self.spread[source[m, j], m]
            return 0

        lax.fori_loop(0, self.place.count, one, 0)
        self.each(lambda d: self.home(d).start())
        self.wanted[self.own(self.wanted)] = self.moved[self.place.me]

    def end(self):
        self.each(lambda d: self.home(d).wait())


def spread_small(place, tile, table, send, recv):
    table[place.me] = tile[...]

    def out(d, _):
        remote(
            tile, table.at[place.me], send, recv, d - 1, (place.me + d) % place.count
        ).start()
        return 0

    lax.fori_loop(1, place.count, out, 0)


def collect_small(place, tile, table, send, recv):
    def back(d, _):
        copy = remote(
            tile,
            table.at[(place.me + place.count - d) % place.count],
            send,
            recv,
            d - 1,
            (place.me + d) % place.count,
        )
        copy.wait()
        return 0

    lax.fori_loop(1, place.count, back, 0)


def cut_columns(widths, start=0):
    pieces = []
    for width in widths:
        pieces.append((0, start, width))
        start += width
    return pieces


def kernel_depth(count, wide, deep):
    fits = count % 8 == 0 and wide.shape[0] % 8 == 0 and deep.shape[0] % 8 == 0
    return count // 8 if fits else 0


def transposed(left, right):
    return lax.dot_general(
        left, right, (((0,), (0,)), ((), ())), preferred_element_type=f32
    )


def against(left, right):
    return lax.dot_general(
        left, right, (((1,), (1,)), ((), ())), preferred_element_type=f32
    )


class Stream:
    def __init__(self, refs, tiles, slots, sems):
        self.refs, self.tiles, self.slots, self.sems = refs, tiles, slots, sems
        self.next, self.begun = 0, 0

    def copy(self, k):
        kind, start, size = self.tiles[k]
        slot = k % self.slots.shape[0]
        cut = pl.ds(0, size)
        if kind:
            source, target = self.refs[1].at[pl.ds(start, size)], self.slots.at[slot, cut]
        else:
            source, target = self.refs[0].at[:, pl.ds(start, size)], self.slots.at[slot, :, cut]
        return pltpu.make_async_copy(source, target, self.sems.at[slot])

    def take(self):
        ahead = min(len(self.tiles), self.next + self.slots.shape[0])
        while self.begun < ahead:
            self.copy(self.begun).start()
            self.begun += 1
        k = self.next
        self.copy(k).wait()
        self.next += 1
        return self.slots.at[k % self.slots.shape[0]]


def back_into(total, left, start, size, tile, fresh):
    def chunk(n, _):
        cols = columns(n * 256, 256)
        part = against(left[:, start : start + size], tile[cols, 0:size])
        rows = pl.ds(0, left.shape[0])
        total[rows, cols] = part if fresh else total[rows, cols] + part
        return 0

    lax.fori_loop(0, D // 256, chunk, 0)


def back_rounded(out, left, tile):
    def chunk(n, _):
        cols = columns(n * 256, 256)
        out[:, cols] = against(left[...], tile[cols, :]).astype(bf16)
        return 0

    lax.fori_loop(0, D // 256, chunk, 0)


def self_scores(bias, scores, block, head):
    marked = bias[block, head].astype(f32)
    return jnp.where(marked < -1e29, masked_score, scores + marked)


def cross_scores(live, scores, block, head):
    return jnp.where(live[block, 0:1, :] > 0.0, scores, masked_score)


def pair_loop(count, body_of):
    def one(index, _):
        body_of(index // (H // 2), index % (H // 2))
        return 0

    lax.fori_loop(0, count * (H // 2), one, 0)


def softmax_rows(scores):
    weights = jnp.exp(scores - jnp.max(scores, axis=1, keepdims=True))
    return weights / jnp.sum(weights, axis=1, keepdims=True)


def attend_back_pairs(refs, grads, marks, mask, folded):
    q, k, v, da = refs
    dq, dk, dv = grads
    rows_q = 128
    tall = k.shape[0] // (q.shape[0] // rows_q)
    even = lax.broadcasted_iota(jnp.int32, (1, 128), 1) < DH
    down, right = [lax.broadcasted_iota(jnp.int32, (rows_q, rows_q), k) for k in (0, 1)]
    mirror = jnp.where(down + right == rows_q - 1, 1.0, 0.0).astype(bf16)

    def pair(block, p):
        rows = pl.ds(pl.multiple_of(block * rows_q, rows_q), rows_q)
        keys = pl.ds(pl.multiple_of(block * tall, tall), tall)
        cols = columns(p * 128, 128)
        q2, k2, v2, da2 = q[rows, cols], k[keys, cols], v[keys, cols], da[rows, cols]
        sums = [None, None, None]
        for e in (0, 1):
            keep = even if e == 0 else jnp.logical_not(even)

            def half(value):
                return jnp.where(keep, value.astype(f32), 0.0).astype(bf16)

            qe, dae, ke = half(q2), half(da2), half(k2)
            head = 2 * p + e
            probs = softmax_rows(mask(marks, against(qe, k2), block, head))
            dp = against(dae, v2)
            centre = jnp.sum(probs * dp, axis=1, keepdims=True)
            ds = (probs * (dp - centre)).astype(bf16)
            terms = (
                jnp.dot(ds, ke, preferred_element_type=f32),
                transposed(ds, qe),
                transposed(probs.astype(bf16), dae),
            )
            sums = [t if s is None else s + t for s, t in zip(sums, terms)]
            if folded is not None:
                upside = jnp.dot(mirror, ds, preferred_element_type=f32)
                turned = pltpu.roll(upside, 0, 1, stride=1, stride_axis=0)
                folded[block * H + head] = jnp.sum(turned, axis=0, keepdims=True)
        dq[rows, cols] = sums[0].astype(bf16)
        dk[keys, cols] = sums[1].astype(bf16)
        dv[keys, cols] = sums[2].astype(bf16)

    pair_loop(q.shape[0] // rows_q, pair)


def norm_back_rows(values, gain_row, grad, base, out, total):
    total[...] = jnp.zeros_like(total)

    def chunk(k, _):
        rows = pl.ds(pl.multiple_of(k * 64, 64), 64)
        v = values[rows, :].astype(f32)
        inverse = inverse_rms(v)
        scaled = v * inverse
        g = grad[rows, :]
        weighted = g * gain_row[...]
        centre = jnp.mean(weighted * scaled, axis=-1, keepdims=True)
        out[rows, :] = base[rows, :].astype(f32) + inverse * (weighted - scaled * centre)
        total[...] += jnp.sum(g * scaled, axis=0, keepdims=True)
        return 0

    lax.fori_loop(0, values.shape[0] // 64, chunk, 0)


BACK_INPUTS = (
    "result", "dy", "hd", "n3", "r2", "ac", "cq", "ck", "cv", "n2",
    "enc", "r1", "mixed", "q", "k", "v", "n1", "x", "bias", "pre",
)
BACK_ORDER = ("xo", "xk", "xv", "xq", "o", "q", "k", "v")
SCATTER_ORDER = ("xo", "xq", "xk", "xv", "o", "q", "k", "v")


def backward_kernel(pieces, depth, blocks, *refs):
    refs = list(refs)

    def pop(count):
        return [refs.pop(0) for _ in range(count)]

    whole, down, source, live, gains = pop(5)
    ins = dict(zip(BACK_INPUTS, pop(len(BACK_INPUTS))))
    out, out_deep, layer_out, grad_in, grad_enc, gain_sums, folded = pop(7)
    held = dict(zip(BACK_INPUTS[:-1], pop(len(BACK_INPUTS) - 1)))
    load_sems, slots, slot_sems, pre, pre_sems, out_sems = pop(6)
    dgu, acc, dr2, dr1, low, dmix, dq, dk, dv, dck, dcv = pop(11)
    spread, moved, wanted, deal_send, deal_recv = pop(5)
    place = Place(depth)
    scatter = Scatter(place, pieces, blocks, (out, out_deep), refs)
    units = held["hd"].shape[1]
    rows = held["dy"].shape[0]

    loads = {
        name: pltpu.make_async_copy(ins[name], held[name], load_sems.at[i])
        for i, name in enumerate(BACK_INPUTS[:-1])
    }
    for load in loads.values():
        load.start()

    def need(*names):
        for name in names:
            loads.pop(name).wait()

    tiles = [(1, start, min(1024, units - start)) for start in range(0, units, 1024)]
    tiles += [(0, 8 * D + k, min(1024, 2 * units - k)) for k in range(0, 2 * units, 1024)]
    tiles += [(0, D * LEFT.index(w), D) for w in BACK_ORDER]
    stream = Stream((whole, down), tiles, slots, slot_sems)

    def ahead(k):
        return [
            pltpu.make_async_copy(
                ins["pre"].at[:, columns(j * units + k * 256, 256)],
                pre.at[k % 2, j],
                pre_sems.at[k % 2, j],
            )
            for j in (0, 1)
        ]

    for load in ahead(0):
        load.start()
    place.greet()
    redeal = Redeal(place, held["result"], spread, moved, wanted, deal_send, deal_recv)
    need("result")
    redeal.begin()

    need("dy", "hd")
    dy = held["dy"]
    scatter.produce(held["hd"], dy, 0)
    scatter.produce(held["hd"], dy, 512)
    for start in range(0, units, 1024):
        tile = stream.take()

        def chunk(n, _):
            k = start // 256 + n

            @pl.when(k + 1 < units // 256)
            def _():
                for load in ahead(k + 1):
                    load.start()

            for load in ahead(k):
                load.wait()
            part = against(dy[...], tile[pl.ds(pl.multiple_of(n * 256, 256), 256), :])
            act, slope = gelu_parts(pre[k % 2, 0])
            dgu[:, columns(k * 256, 256)] = (part * pre[k % 2, 1] * slope).astype(bf16)
            dgu[:, columns(units + k * 256, 256)] = (part * act).astype(bf16)
            return 0

        lax.fori_loop(0, min(1024, units - start) // 256, chunk, 0)
    need("n3")
    for start in range(0, 2 * units, 1024):
        scatter.produce(held["n3"], dgu, start)
        back_into(acc, dgu, start, min(1024, 2 * units - start), stream.take(), start == 0)
        if start == 2048:
            redeal.middle(source)
    need("r2")
    norm_back_rows(held["r2"], gains.at[2], acc, dy, dr2, gain_sums.at[2])
    low[...] = dr2[...].astype(bf16)
    need("ac")
    scatter.produce(held["ac"], low, 0)
    back_rounded(dmix, low, stream.take())
    need("cq", "ck", "cv")
    attend_back_pairs(
        (held["cq"], held["ck"], held["cv"], dmix), (dq, dck, dcv), live, cross_scores, None
    )
    need("n2", "enc")
    scatter.produce(held["n2"], dq, 0)
    scatter.produce(held["enc"], dck, 0)
    scatter.produce(held["enc"], dcv, 0)
    back_into(acc, dck, 0, D, stream.take(), True)
    back_into(acc, dcv, 0, D, stream.take(), False)
    enc_out = pltpu.make_async_copy(acc, grad_enc, out_sems.at[0])
    enc_out.start()
    enc_out.wait()
    back_into(acc, dq, 0, D, stream.take(), True)
    need("r1")
    norm_back_rows(held["r1"], gains.at[1], acc, dr2, dr1, gain_sums.at[1])
    low[...] = dr1[...].astype(bf16)
    need("mixed")
    scatter.produce(held["mixed"], low, 0)
    back_rounded(dmix, low, stream.take())
    need("q", "k", "v", "bias")
    attend_back_pairs(
        (held["q"], held["k"], held["v"], dmix),
        (dq, dk, dv),
        held["bias"],
        self_scores,
        folded,
    )
    need("n1")
    for grad in (dq, dk, dv):
        scatter.produce(held["n1"], grad, 0)
    for index, grad in enumerate((dq, dk, dv)):
        back_into(acc, grad, 0, D, stream.take(), index == 0)
    need("x")
    norm_back_rows(held["x"], gains.at[0], acc, dr1, dr2, gain_sums.at[0])
    in_out = pltpu.make_async_copy(dr2, grad_in, out_sems.at[1])
    in_out.start()
    redeal.end()
    deal_out = pltpu.make_async_copy(wanted, layer_out, out_sems.at[2])
    deal_out.start()
    scatter.close()
    in_out.wait()
    deal_out.wait()


def backward_all(whole, down, source, live, gains, acts, depth):
    tall, width = whole.shape
    tall_deep = down.shape[0]
    blocks = (tall // (4 * depth), tall_deep // (4 * depth))
    micro, length = acts["result"].shape[:2]
    rows, keys = micro * length, acts["enc"].shape[0]
    units, count = tall_deep, 8 * depth
    pieces = [(1, 0, 512), (1, 512, 512)]
    pieces += [(0, 8 * D + k, min(1024, 2 * units - k)) for k in range(0, 2 * units, 1024)]
    pieces += [(0, D * LEFT.index(w), D) for w in SCATTER_ORDER]
    anywhere = pl.BlockSpec(memory_space=pl.ANY)
    inside = pl.BlockSpec(memory_space=pltpu.VMEM)
    arrays = [acts[name] for name in BACK_INPUTS]
    spots = (micro, length // 8, D // depth)
    held = [pltpu.VMEM(a.shape, a.dtype) for a in arrays[:-1]]
    square = [pltpu.VMEM((rows, D), f32)] * 2 + [pltpu.VMEM((rows, D), bf16)] * 5
    return pl.pallas_call(
        functools.partial(backward_kernel, pieces, depth, blocks),
        out_shape=(
            jax.ShapeDtypeStruct((width // 128 * (blocks[0] // 2), 128), f32),
            jax.ShapeDtypeStruct((D // 128 * (blocks[1] // 2), 128), f32),
            jax.ShapeDtypeStruct((micro, length, D), bf16),
            jax.ShapeDtypeStruct((rows, D), f32),
            jax.ShapeDtypeStruct((keys, D), f32),
            jax.ShapeDtypeStruct((3, 1, D), f32),
            jax.ShapeDtypeStruct((micro * H, 1, length), f32),
        ),
        in_specs=[anywhere] * 2
        + [pl.BlockSpec(memory_space=pltpu.SMEM)]
        + [inside] * 2
        + [anywhere] * len(arrays),
        out_specs=(anywhere,) * 5 + (inside,) * 2,
        scratch_shapes=held
        + [
            pltpu.SemaphoreType.DMA((len(held),)),
            pltpu.VMEM((3, D, 1024), bf16),
            pltpu.SemaphoreType.DMA((3,)),
            pltpu.VMEM((2, 2, rows, 256), f32),
            pltpu.SemaphoreType.DMA((2, 2)),
            pltpu.SemaphoreType.DMA((3,)),
            pltpu.VMEM((rows, 2 * units), bf16),
            pltpu.VMEM((keys, D), f32),
        ]
        + square
        + [pltpu.VMEM((keys, D), bf16)] * 2
        + [
            pltpu.VMEM((count,) + spots, bf16),
            pltpu.VMEM((count,) + spots, bf16),
            pltpu.VMEM((micro, length, D), bf16),
            pltpu.SemaphoreType.DMA((2 * (count - 1),)),
            pltpu.SemaphoreType.DMA((2 * (count - 1),)),
        ]
        + Scatter.scratch(pieces, depth, blocks),
        compiler_params=pltpu.CompilerParams(
            collective_id=1, has_side_effects=True, vmem_limit_bytes=67043328
        ),
        name="backward",
    )(whole, down, source, live, gains, *arrays)


ACTS = ("hd", "n3", "r2", "ac", "cq", "ck", "cv", "n2", "r1", "mixed", "q", "k", "v", "n1", "bias")
LEFT = ("xk", "xv", "q", "k", "v", "o", "xq", "xo")


def norm_rows(values, gain_row, out):
    def chunk(k, _):
        rows = pl.ds(pl.multiple_of(k * 64, 64), 64)
        v = values[rows, :].astype(f32)
        out[rows, :] = (v * inverse_rms(v) * gain_row[...]).astype(bf16)
        return 0

    lax.fori_loop(0, values.shape[0] // 64, chunk, 0)


def by_columns(left, tile, width, put):
    def chunk(k, _):
        part = tile[:, :, :, :, columns(k * 256, 256)].reshape(-1, 256)
        put(k, jnp.dot(left[...], part, preferred_element_type=f32))
        return 0

    lax.fori_loop(0, width // 256, chunk, 0)


def attend_pairs(refs, out, marks, mask):
    q, k, v = refs
    rows_q = 128
    tall = k.shape[0] // (q.shape[0] // rows_q)
    even = lax.broadcasted_iota(jnp.int32, (1, 128), 1) < DH

    def pair(block, p):
        rows = pl.ds(pl.multiple_of(block * rows_q, rows_q), rows_q)
        keys = pl.ds(pl.multiple_of(block * tall, tall), tall)
        cols = columns(p * 128, 128)
        q2, k2, v2 = q[rows, cols], k[keys, cols], v[keys, cols]
        total = None
        for e in (0, 1):
            keep = even if e == 0 else jnp.logical_not(even)

            def half(value):
                return jnp.where(keep, value.astype(f32), 0.0).astype(bf16)

            probs = softmax_rows(mask(marks, against(half(q2), k2), block, 2 * p + e))
            term = jnp.dot(probs.astype(bf16), half(v2), preferred_element_type=f32)
            total = term if total is None else total + term
        out[rows, cols] = total.astype(bf16)

    pair_loop(q.shape[0] // rows_q, pair)


def gain_rows(table, gains, count):
    each = D // count
    values = jnp.sum(table[...], axis=1).astype(bf16)
    lane = lax.broadcasted_iota(jnp.int32, (128, D), 0)
    col = lax.broadcasted_iota(jnp.int32, (128, D), 1)
    device = lax.broadcasted_iota(jnp.int32, (count, D), 0)
    owner = lax.broadcasted_iota(jnp.int32, (count, D), 1) // each
    for k in range(3):
        pick = jnp.where(lane == k * each + col % each, 1.0, 0.0).astype(bf16)
        spread = jnp.dot(values, pick, preferred_element_type=f32)
        gains[k] = jnp.sum(jnp.where(device == owner, spread, 0.0), axis=0, keepdims=True)


def bias_blocks(table, buckets, allowed, by_offset, bias, count):
    first, share = 3 * (D // count), H * NB // count
    split = NB // share
    values = jnp.sum(table[...], axis=1).astype(bf16)
    lane = lax.broadcasted_iota(jnp.int32, (128, 128), 0) - first
    for block in range(bias.shape[0]):
        for part in range(split):
            hit = (lane + part * share == buckets[block, 0:1, :]) & (lane >= 0) & (lane < share)
            pick = jnp.where(hit, 1.0, 0.0).astype(bf16)
            found = jnp.dot(values, pick, preferred_element_type=f32)
            for device in range(count):
                by_offset[part, device] = found[device : device + 1]

        def head_bias(head, _):
            row = by_offset[0, head * split]
            for part in range(1, split):
                row = row + by_offset[part, head * split + part]
            grid = pltpu.roll(
                jnp.broadcast_to(row, (128, 128)), 0, 1, stride=1, stride_axis=0
            )
            bias[block, head] = jnp.where(allowed[block] > 0.0, grid, -1e30).astype(bf16)
            return 0

        lax.fori_loop(0, H, head_bias, 0)


def forward_kernel(pieces, depth, widths, *refs):
    refs = list(refs)

    def pop(count):
        return [refs.pop(0) for _ in range(count)]

    wide = pop(len(widths))
    (deep, tile, source, live, allowed, buckets, hidden, encoder, cotangent) = pop(9)
    whole, whole_deep, gains, dy, result, pre = pop(6)
    outs = dict(zip(ACTS, pop(len(ACTS))))
    staged, staged_deep, table, by_offset, x, enc, cot = pop(7)
    held = dict(zip(ACTS, pop(len(ACTS))))
    pre_held, result_held, slots, slot_sems, down_slot, spread, moved, wanted = pop(8)
    stage_sems, load_sems, out_sems, own_sems, send, recv, small_send, small_recv = pop(8)
    deal_send, deal_recv = pop(2)
    place = Place(depth)
    count = place.count
    rows, units = x.shape[0], held["hd"].shape[1]
    gather = Gather(
        place, pieces, (staged, staged_deep), (whole, whole_deep), own_sems, send, recv
    )
    staging, start = [], 0
    for i, width in enumerate(widths):
        target = staged.at[:, pl.ds(start, width)]
        staging.append(pltpu.make_async_copy(wide[i], target, stage_sems.at[i]))
        start += width
    staging.append(pltpu.make_async_copy(deep, staged_deep, stage_sems.at[len(widths)]))
    loads = [
        pltpu.make_async_copy(a, b, load_sems.at[i])
        for i, (a, b) in enumerate(((cotangent, cot), (hidden, x), (encoder, enc)))
    ]
    for copy in staging + loads:
        copy.start()
    place.greet()
    spread_small(place, tile, table, small_send, small_recv)
    for copy in staging:
        copy.wait()
    gather.open()
    redeal = Redeal(place, cot, spread, moved, wanted, deal_send, deal_recv)
    loads[0].wait()
    redeal.begin()
    collect_small(place, tile, table, small_send, small_recv)
    gain_rows(table, gains, count)
    loads[1].wait()
    loads[2].wait()
    norm_rows(x, gains.at[0], held["n1"])
    bias_blocks(table, buckets, allowed, by_offset, held["bias"], count)

    leaving = []

    def leave(name, source_ref=None, target=None):
        copy = pltpu.make_async_copy(
            held[name] if source_ref is None else source_ref,
            outs[name] if target is None else target,
            out_sems.at[len(leaving)],
        )
        copy.start()
        leaving.append(copy)

    leave("n1")
    leave("bias")

    tiles = [(D * k, D) for k in range(len(LEFT))]
    tiles += [(8 * D + k, min(1024, 2 * units - k)) for k in range(0, 2 * units, 1024)]

    def fetch(k):
        start, width = tiles[k]
        slot = k % slots.shape[0]
        return pltpu.make_async_copy(
            whole.at[:, :, :, :, pl.ds(start, width)],
            slots.at[slot, :, :, :, :, pl.ds(0, width)],
            slot_sems.at[slot],
        )

    def rounded(out):
        def put(k, part):
            out[:, columns(k * 256, 256)] = part.astype(bf16)

        return put

    def added(base, out):
        def put(k, part):
            cols = columns(k * 256, 256)
            out[:, cols] = base[:, cols].astype(f32) + part

        return put

    def units_of(k, tile_ref):
        start, width = tiles[k][0] - 8 * D, tiles[k][1]

        def put(n, part):
            at = start // 256 + n
            pre_held[:, columns(at * 256, 256)] = part

            @pl.when(at >= units // 256)
            def _():
                cols = columns((at - units // 256) * 256, 256)
                act, _ = gelu_parts(pre_held[:, cols])
                held["hd"][:, cols] = (act * part).astype(bf16)

        by_columns(held["n3"], tile_ref, width, put)

    def use(k):
        ref = slots.at[k % slots.shape[0]]
        name = LEFT[k] if k < len(LEFT) else ""
        if name in ("xk", "xv"):
            by_columns(enc, ref, D, rounded(held["c" + name[1]]))
            leave("c" + name[1])
        elif name in ("q", "k", "v"):
            by_columns(held["n1"], ref, D, rounded(held[name]))
            leave(name)
            if name == "v":
                attend_pairs(
                    (held["q"], held["k"], held["v"]),
                    held["mixed"],
                    held["bias"],
                    self_scores,
                )
                leave("mixed")
        elif name == "o":
            by_columns(held["mixed"], ref, D, added(x, held["r1"]))
            norm_rows(held["r1"], gains.at[1], held["n2"])
            leave("r1")
            leave("n2")
        elif name == "xq":
            by_columns(held["n2"], ref, D, rounded(held["cq"]))
            leave("cq")
            attend_pairs((held["cq"], held["ck"], held["cv"]), held["ac"], live, cross_scores)
            leave("ac")
        elif name == "xo":
            by_columns(held["ac"], ref, D, added(held["r1"], held["r2"]))
            norm_rows(held["r2"], gains.at[2], held["n3"])
            leave("r2")
            leave("n3")
        else:
            units_of(k, ref)

    done, fetched = 0, 0
    for t in range(len(pieces) + 3):
        gather.turn(t)
        if t < 3:
            continue
        kind, first, width = pieces[t - 3]
        if kind:
            copy = pltpu.make_async_copy(whole_deep, down_slot, slot_sems.at[0])
            copy.start()
            copy.wait()
            continue
        here = [k for k, (s, w) in enumerate(tiles) if first < s + w <= first + width]
        while fetched < len(tiles) and tiles[fetched][0] + tiles[fetched][1] <= first + width:
            if fetched >= done + slots.shape[0]:
                break
            fetch(fetched).start()
            fetched += 1
        for k in here:
            if k >= fetched:
                fetch(k).start()
                fetched += 1
            fetch(k).wait()
            use(k)
            done += 1
        if t == 4:
            redeal.middle(source)
    leave("", pre_held, pre)
    leave("hd")

    def last(k, part):
        cols = columns(k * 256, 256)
        result_held[:, cols] = (held["r2"][:, cols] + part).astype(bf16)

    by_columns(held["hd"], down_slot, D, last)
    leave("", result_held, result)
    redeal.end()
    leave("", wanted, dy)
    for copy in leaving:
        copy.wait()
    gather.close()


def forward_all(wide, deep, small, source, live, allowed, buckets, hidden, encoder, cotangent, depth):
    widths = [part.shape[1] for part in wide]
    width, tall = sum(widths), wide[0].shape[0]
    tall_deep, units = deep.shape[0], widths[-1]
    rows, keys = hidden.shape[0], encoder.shape[0]
    micro, length = cotangent.shape[:2]
    pieces = cut_columns([1024] + [2048] * 5)
    pieces.append((0, 11264, width - 11264))
    pieces.append((1, 0, D))
    copies = len(pieces) * (1 + 2 * (depth + 2))
    count = 8 * depth
    tile = jnp.zeros((8, 128), f32).at[0, : small.shape[0]].set(small.astype(f32))
    anywhere = pl.BlockSpec(memory_space=pl.ANY)
    inside = pl.BlockSpec(memory_space=pltpu.VMEM)
    spots = (micro, length // 8, D // depth)
    kinds = dict(
        hd=((rows, units), bf16),
        n3=((rows, D), bf16),
        r2=((rows, D), f32),
        ac=((rows, D), bf16),
        cq=((rows, D), bf16),
        ck=((keys, D), bf16),
        cv=((keys, D), bf16),
        n2=((rows, D), bf16),
        r1=((rows, D), f32),
        mixed=((rows, D), bf16),
        q=((rows, D), bf16),
        k=((rows, D), bf16),
        v=((rows, D), bf16),
        n1=((rows, D), bf16),
        bias=((micro, H, length, length), bf16),
    )
    results = pl.pallas_call(
        functools.partial(forward_kernel, pieces, depth, widths),
        out_shape=(
            jax.ShapeDtypeStruct((depth, 2, 2, 2 * tall, width), bf16),
            jax.ShapeDtypeStruct((depth, 2, 2, 2 * tall_deep, D), bf16),
            jax.ShapeDtypeStruct((3, 1, D), f32),
            jax.ShapeDtypeStruct((micro, length, D), bf16),
            jax.ShapeDtypeStruct((rows, D), bf16),
            jax.ShapeDtypeStruct((rows, 2 * units), f32),
        )
        + tuple(jax.ShapeDtypeStruct(*kinds[name]) for name in ACTS),
        in_specs=[anywhere] * (len(wide) + 1)
        + [inside, pl.BlockSpec(memory_space=pltpu.SMEM)]
        + [inside] * 3
        + [anywhere] * 3,
        out_specs=(anywhere,) * 2 + (inside,) + (anywhere,) * (3 + len(ACTS)),
        scratch_shapes=[
            pltpu.VMEM((tall, width), bf16),
            pltpu.VMEM((tall_deep, D), bf16),
            pltpu.VMEM((count, 8, 128), f32),
            pltpu.VMEM((2, count, 1, 128), f32),
            pltpu.VMEM((rows, D), bf16),
            pltpu.VMEM((keys, D), bf16),
            pltpu.VMEM((micro, length, D), bf16),
        ]
        + [pltpu.VMEM(*kinds[name]) for name in ACTS]
        + [
            pltpu.VMEM((rows, 2 * units), f32),
            pltpu.VMEM((rows, D), bf16),
            pltpu.VMEM((4, depth, 2, 2, 2 * tall, 1024), bf16),
            pltpu.SemaphoreType.DMA((4,)),
            pltpu.VMEM((depth, 2, 2, 2 * tall_deep, D), bf16),
            pltpu.VMEM((count,) + spots, bf16),
            pltpu.VMEM((count,) + spots, bf16),
            pltpu.VMEM((micro, length, D), bf16),
            pltpu.SemaphoreType.DMA((len(wide) + 1,)),
            pltpu.SemaphoreType.DMA((3,)),
            pltpu.SemaphoreType.DMA((len(ACTS) + 3,)),
            pltpu.SemaphoreType.DMA((len(pieces),)),
            pltpu.SemaphoreType.DMA((copies,)),
            pltpu.SemaphoreType.DMA((copies,)),
            pltpu.SemaphoreType.DMA((count - 1,)),
            pltpu.SemaphoreType.DMA((count - 1,)),
            pltpu.SemaphoreType.DMA((2 * (count - 1),)),
            pltpu.SemaphoreType.DMA((2 * (count - 1),)),
        ],
        compiler_params=pltpu.CompilerParams(
            collective_id=0, has_side_effects=True, vmem_limit_bytes=67043328
        ),
        name="forward",
    )(*wide, deep, tile, source, live, allowed, buckets, hidden, encoder, cotangent)
    whole, whole_deep, gains, dy, result, pre = results[:6]
    acts = dict(zip(ACTS, results[6:]))
    acts.update(
        dy=dy.reshape(rows, D),
        result=result.reshape(micro, length, D),
        pre=pre,
        x=hidden,
        enc=encoder,
    )
    return whole.reshape(-1, width), whole_deep.reshape(-1, D), gains, acts


def fused(
    depth,
    hidden,
    encoder,
    cotangent,
    segments,
    buckets,
    live,
    dealing,
    small,
    wide,
    feed_down,
):
    micro, _, length, _ = hidden.shape
    enc_count = encoder.shape[2]
    count = 8 * depth
    slots = jnp.arange(count, dtype=jnp.int32)
    inverse = jnp.sum(
        jnp.where(dealing[:, None, :] == slots[:, None], slots, 0), axis=2, dtype=jnp.int32
    )
    positions = jnp.arange(length, dtype=jnp.int32)
    allowed = (positions[None, :] <= positions[:, None])[None] & (
        segments[:, :, None] == segments[:, None, :]
    )
    turned = jnp.concatenate([buckets[:, :1], buckets[:, :0:-1]], axis=1)
    live_rows = jnp.arange(enc_count, dtype=jnp.int32)[None, None, :] < live[:, None, None]
    live_rows = jnp.broadcast_to(live_rows, (micro, 8, enc_count)).astype(f32)
    whole, down, gains, acts = forward_all(
        wide,
        feed_down,
        small,
        inverse,
        live_rows,
        allowed.astype(f32),
        jnp.broadcast_to(turned[:, None], (micro, 8, length)),
        hidden.reshape(micro * length, D),
        encoder.reshape(micro * enc_count, D),
        cotangent.reshape(micro, length, D),
        depth,
    )
    sums, piece_down, layer_out, grad_in, grad_enc, gain_sums, folded = backward_all(
        whole, down, dealing, live_rows, gains, acts, depth
    )
    offsets = folded.reshape(micro, H, length)[:, :, ::-1]
    onehot = (buckets[:, :, None] == jnp.arange(NB, dtype=jnp.int32)).astype(f32)
    g_bias = jnp.einsum("bho,boc->hc", offsets, onehot, precision=highest)
    small_grads = jnp.concatenate(
        [gain_sums[k, 0].reshape(count, -1) for k in range(3)] + [g_bias.reshape(count, -1)],
        axis=1,
    )
    small_sum = jnp.sum(
        lax.all_to_all(small_grads, AXIS, split_axis=0, concat_axis=0, tiled=True), axis=0
    )
    tall, tall_deep = wide[0].shape[0], feed_down.shape[0]
    sums = sums.reshape(-1, tall, 128)
    piece_down = piece_down.reshape(-1, tall_deep, 128)

    def unpack(tiles):
        return tiles.transpose(1, 0, 2).reshape(tiles.shape[1], -1)

    grads, start = [], 0
    for part in wide:
        tiles = part.shape[1] // 128
        grads.append(unpack(sums[start : start + tiles]))
        start += tiles
    part = D // count
    return (
        layer_out.reshape(hidden.shape),
        grad_in.reshape(hidden.shape),
        grad_enc.reshape(encoder.shape),
        small_sum[:part],
        small_sum[part : 2 * part],
        small_sum[2 * part : 3 * part],
        small_sum[3 * part :],
        *[grads[k] for k in (2, 3, 4, 5, 6, 0, 1, 7, 8, 9)],
        unpack(piece_down),
    )


def body(
    hidden,
    encoder,
    cotangent,
    segment_ids,
    rel_buckets,
    enc_rows,
    dealing,
    gain_self,
    gain_cross,
    gain_ffn,
    rel_bias,
    self_query,
    self_key,
    self_value,
    self_out,
    cross_query,
    cross_key,
    cross_value,
    cross_out,
    feed_gate,
    feed_up,
    feed_down,
):
    device = lax.axis_index(AXIS)
    micro, own, length, _ = hidden.shape
    enc_count = encoder.shape[2]
    blocks = micro * own
    first = device * own

    def mine(table):
        return lax.dynamic_slice_in_dim(table, first, own, axis=1).reshape(
            (blocks,) + table.shape[2:]
        )

    segments, buckets, live = mine(segment_ids), mine(rel_buckets), mine(enc_rows)
    small = jnp.concatenate([gain_self, gain_cross, gain_ffn, rel_bias])
    wide = (
        cross_key,
        cross_value,
        self_query,
        self_key,
        self_value,
        self_out,
        cross_query,
        cross_out,
        feed_gate,
        feed_up,
    )
    depth = kernel_depth(lax.axis_size(AXIS), self_query, feed_down) if own == 1 else 0
    if depth:
        return fused(
            depth,
            hidden,
            encoder,
            cotangent,
            segments,
            buckets,
            live,
            dealing,
            small,
            wide,
            feed_down,
        )
    grad_out = redeal(cotangent, jnp.argsort(dealing, axis=1)).reshape(blocks * length, D)

    smalls = lax.all_gather(small, AXIS, axis=0)
    part = gain_self.shape[0]
    gain_one, gain_two, gain_three = [
        smalls[:, k * part : (k + 1) * part].reshape(D).astype(f32) for k in range(3)
    ]
    bias_table = smalls[:, 3 * part :].reshape(H, NB).astype(f32)
    (wq, wk, wv, wo, xq, xk, xv, xo, gate, up), down = gather_weights(
        (
            self_query,
            self_key,
            self_value,
            self_out,
            cross_query,
            cross_key,
            cross_value,
            cross_out,
            feed_gate,
            feed_up,
        ),
        feed_down,
    )

    positions = jnp.arange(length, dtype=jnp.int32)
    allowed = (positions[None, :] <= positions[:, None])[None] & (
        segments[:, :, None] == segments[:, None, :]
    )
    cross_allowed = jnp.broadcast_to(
        jnp.arange(enc_count, dtype=jnp.int32)[None, None, :] < live[:, None, None],
        (blocks, length, enc_count),
    )
    onehot = (buckets[:, :, None] == jnp.arange(NB, dtype=jnp.int32)).astype(f32)
    per_offset = jnp.einsum("hc,boc->bho", bias_table, onehot, precision=highest)
    bias_grid = toeplitz_expand(per_offset.reshape(blocks * H, length)).reshape(
        blocks, H, length, length
    )

    wide_in = hidden.reshape(blocks * length, D).astype(f32)
    enc_in = encoder.reshape(blocks * enc_count, D)
    inv_one = inverse_rms(wide_in)
    normed_one = (wide_in * inv_one * gain_one).astype(bf16)
    queries = product(normed_one, wq).astype(bf16)
    keys_self = product(normed_one, wk).astype(bf16)
    values_self = product(normed_one, wv).astype(bf16)
    mixed_self, probs_self = attend(queries, keys_self, values_self, bias_grid, allowed)
    first_sum = wide_in + product(mixed_self, wo)
    inv_two = inverse_rms(first_sum)
    normed_two = (first_sum * inv_two * gain_two).astype(bf16)
    cross_queries = product(normed_two, xq).astype(bf16)
    cross_keys = product(enc_in, xk).astype(bf16)
    cross_values = product(enc_in, xv).astype(bf16)
    mixed_cross, probs_cross = attend(
        cross_queries, cross_keys, cross_values, None, cross_allowed
    )
    second_sum = first_sum + product(mixed_cross, xo)
    inv_three = inverse_rms(second_sum)
    normed_three = (second_sum * inv_three * gain_three).astype(bf16)
    gate_pre = product(normed_three, gate)
    up_pre = product(normed_three, up)
    act, slope = gelu_parts(gate_pre)
    hidden_units = (act * up_pre).astype(bf16)
    result = (second_sum + product(hidden_units, down)).astype(bf16)
    layer_out = redeal(result.reshape(micro, own, length, D), dealing)

    g_down = product_left(hidden_units, grad_out)
    grad_units = product_right(grad_out, down)
    grad_gate = (grad_units * up_pre * slope).astype(bf16)
    grad_up = (grad_units * act).astype(bf16)
    g_gate = product_left(normed_three, grad_gate)
    g_up = product_left(normed_three, grad_up)
    grad_three = product_right(grad_gate, gate) + product_right(grad_up, up)
    back, g_gain_three = norm_back(second_sum, inv_three, gain_three, grad_three)
    grad_second = grad_out.astype(f32) + back
    grad_low = grad_second.astype(bf16)
    g_xo = product_left(mixed_cross, grad_low)
    grad_mixed = product_right(grad_low, xo).astype(bf16)
    grad_cq, grad_ck, grad_cv, _ = attend_back(
        cross_queries, cross_keys, cross_values, probs_cross, grad_mixed
    )
    g_xq = product_left(normed_two, grad_cq)
    g_xk = product_left(enc_in, grad_ck)
    g_xv = product_left(enc_in, grad_cv)
    grad_enc = product_right(grad_ck, xk) + product_right(grad_cv, xv)
    back, g_gain_two = norm_back(first_sum, inv_two, gain_two, product_right(grad_cq, xq))
    grad_first = grad_second + back
    grad_low = grad_first.astype(bf16)
    g_so = product_left(mixed_self, grad_low)
    grad_mixed = product_right(grad_low, wo).astype(bf16)
    grad_sq, grad_sk, grad_sv, grad_scores = attend_back(
        queries, keys_self, values_self, probs_self, grad_mixed
    )
    offsets = toeplitz_fold(
        grad_scores.astype(f32).reshape(blocks * H, length, length)
    ).reshape(blocks, H, length)
    g_bias = jnp.einsum("bho,boc->hc", offsets, onehot, precision=highest).reshape(H * NB)
    g_sq = product_left(normed_one, grad_sq)
    g_sk = product_left(normed_one, grad_sk)
    g_sv = product_left(normed_one, grad_sv)
    grad_one = (
        product_right(grad_sq, wq) + product_right(grad_sk, wk) + product_right(grad_sv, wv)
    )
    back, g_gain_one = norm_back(wide_in, inv_one, gain_one, grad_one)
    grad_in = grad_first + back

    pieces, piece_down = scatter_grads(
        (g_sq, g_sk, g_sv, g_so, g_xq, g_xk, g_xv, g_xo, g_gate, g_up), g_down
    )
    count = smalls.shape[0]
    small_grads = jnp.concatenate(
        [g.reshape(count, -1) for g in (g_gain_one, g_gain_two, g_gain_three, g_bias)], axis=1
    )
    small_sum = jnp.sum(
        lax.all_to_all(small_grads, AXIS, split_axis=0, concat_axis=0, tiled=True), axis=0
    )
    return (
        layer_out,
        grad_in.reshape(hidden.shape),
        grad_enc.reshape(encoder.shape),
        small_sum[:part],
        small_sum[part : 2 * part],
        small_sum[2 * part : 3 * part],
        small_sum[3 * part :],
        *pieces,
        piece_down,
    )


def solution(mesh):
    block = P(None, AXIS, None, None)
    row = P(AXIS)
    matrix = P(AXIS, None)
    return jax.shard_map(
        body,
        mesh=mesh,
        in_specs=(block,) * 3 + (P(),) * 4 + (row,) * 4 + (matrix,) * 11,
        out_specs=(block,) * 3 + (row,) * 4 + (matrix,) * 11,
        check_vma=False,
    )
```

```python
import functools

import jax
import jax.numpy as jnp
from jax import lax
from jax.experimental import pallas as pl
from jax.experimental.pallas import tpu as pltpu
from jax.sharding import PartitionSpec as P

D = 1024
H = 16
DH = 64
NB = 32

AXIS = "fsdp"
eps_norm = 1e-06
masked_score = -1000000000.0
highest = lax.Precision.HIGHEST
f32 = jnp.float32
bf16 = jnp.bfloat16


def product(left_side, right_side):
    return jnp.dot(left_side, right_side, preferred_element_type=f32)


def product_left(left_side, right_side):
    return lax.dot_general(
        left_side, right_side, (((0,), (0,)), ((), ())), preferred_element_type=f32
    )


def product_right(left_side, right_side):
    return lax.dot_general(
        left_side, right_side, (((1,), (1,)), ((), ())), preferred_element_type=f32
    )


def inverse_rms(values):
    return lax.rsqrt(jnp.mean(values * values, axis=-1, keepdims=True) + eps_norm)


def norm_back(values, inverse, gain_row, grad):
    scaled = values * inverse
    weighted = grad * gain_row
    centre = jnp.mean(weighted * scaled, axis=-1, keepdims=True)
    return inverse * (weighted - scaled * centre), jnp.sum(grad * scaled, axis=0)


def gelu_parts(gate_pre):
    root = 0.7978845608028654
    inner = root * (gate_pre + 0.044715 * gate_pre * gate_pre * gate_pre)
    curve = jnp.tanh(inner)
    value = 0.5 * gate_pre * (1.0 + curve)
    slope = 0.5 * (1.0 + curve) + 0.5 * gate_pre * (1.0 - curve * curve) * root * (
        1.0 + 3 * 0.044715 * gate_pre * gate_pre
    )
    return value, slope


def toeplitz_expand(per_offset):
    head_count, length = per_offset.shape
    filler = jnp.zeros((head_count, 1), f32)
    pattern = jnp.concatenate(
        [per_offset[:, :1], filler, per_offset[:, ::-1][:, : length - 1]], axis=1
    )
    tiled_rows = jnp.broadcast_to(pattern[:, None, :], (head_count, length, length + 1))
    return tiled_rows.reshape(head_count, length * (length + 1))[:, : length * length].reshape(
        head_count, length, length
    )


def toeplitz_fold(score_grid):
    head_count, length = (score_grid.shape[0], score_grid.shape[1])
    flat_grid = score_grid.reshape(head_count, length * length)
    padded = jnp.concatenate([flat_grid, jnp.zeros((head_count, length), f32)], axis=1)
    columns = jnp.sum(padded.reshape(head_count, length, length + 1), axis=1)
    return jnp.concatenate([columns[:, :1], columns[:, 2:][:, ::-1]], axis=1)


def heads(matrix, blocks):
    return matrix.reshape(blocks, -1, H, DH)


def score_block(queries, keys_in, bias_grid, allowed):
    scores = jnp.einsum("bihd,bjhd->bhij", queries, keys_in, preferred_element_type=f32)
    if bias_grid is not None:
        scores = scores + bias_grid
    return jnp.where(allowed[:, None], scores, masked_score)


def attend(queries, keys_in, values, bias_grid, allowed):
    blocks = allowed.shape[0]
    scores = score_block(heads(queries, blocks), heads(keys_in, blocks), bias_grid, allowed)
    largest = jnp.max(scores, axis=3, keepdims=True)
    weights = jnp.exp(scores - largest)
    probs = weights / jnp.sum(weights, axis=3, keepdims=True)
    mixed = jnp.einsum(
        "bhij,bjhd->bihd", probs.astype(bf16), heads(values, blocks), preferred_element_type=f32
    )
    return mixed.reshape(queries.shape[0], D).astype(bf16), probs


def attend_back(queries, keys_in, values, probs, grad_mixed):
    blocks = probs.shape[0]
    grad_heads = heads(grad_mixed, blocks)
    grad_values = jnp.einsum(
        "bhij,bihd->bjhd", probs.astype(bf16), grad_heads, preferred_element_type=f32
    )
    grad_probs = jnp.einsum(
        "bihd,bjhd->bhij", grad_heads, heads(values, blocks), preferred_element_type=f32
    )
    grad_scores = (
        probs * (grad_probs - jnp.sum(probs * grad_probs, axis=3, keepdims=True))
    ).astype(bf16)
    grad_queries = jnp.einsum(
        "bhij,bjhd->bihd", grad_scores, heads(keys_in, blocks), preferred_element_type=f32
    )
    grad_keys = jnp.einsum(
        "bhij,bihd->bjhd", grad_scores, heads(queries, blocks), preferred_element_type=f32
    )
    return (
        grad_queries.reshape(-1, D).astype(bf16),
        grad_keys.reshape(-1, D).astype(bf16),
        grad_values.reshape(-1, D).astype(bf16),
        grad_scores,
    )


def redeal(blocks, source):
    micro, own, rows, width = blocks.shape
    count = source.shape[1] // own
    cut = blocks.reshape(micro, own, count, rows // count, width).transpose(2, 0, 1, 3, 4)
    spread = lax.all_to_all(cut, AXIS, split_axis=0, concat_axis=0, tiled=True)
    spread = spread.transpose(1, 0, 2, 3, 4).reshape(micro, count * own, rows // count, width)
    moved = jnp.take_along_axis(spread, source[:, :, None, None], axis=1)
    moved = moved.reshape(micro, count, own, rows // count, width).transpose(1, 0, 2, 3, 4)
    home = lax.all_to_all(moved, AXIS, split_axis=0, concat_axis=0, tiled=True)
    return home.transpose(1, 2, 0, 3, 4).reshape(micro, own, rows, width)


def gather_weights(wide, deep):
    packed = lax.all_gather(jnp.concatenate(wide, axis=1), AXIS, axis=0, tiled=True)
    whole, start = [], 0
    for part in wide:
        whole.append(packed[:, start : start + part.shape[1]])
        start += part.shape[1]
    return whole, lax.all_gather(deep, AXIS, axis=0, tiled=True)


def scatter_grads(wide, deep):
    packed = jnp.concatenate([part.astype(bf16) for part in wide], axis=1)
    packed = lax.psum_scatter(packed, AXIS, scatter_dimension=0, tiled=True).astype(f32)
    pieces, start = [], 0
    for part in wide:
        pieces.append(packed[:, start : start + part.shape[1]])
        start += part.shape[1]
    deep = lax.psum_scatter(deep.astype(bf16), AXIS, scatter_dimension=0, tiled=True)
    return pieces, deep.astype(f32)


MESH = pl.DeviceIdType.MESH
RING = 3
SLOTS = 7
DRAIN = (1,) * 6
GATHER_LAGS = (0, 2, 4, 5)
SCATTER_LAGS = (0, 1, 2, 2, 1, 1)


class Place:
    def __init__(self, depth):
        self.depth = depth
        self.count = depth * 8
        self.me = lax.axis_index(AXIS)
        self.core = self.me % 2
        self.x = (self.me // 2) % 2
        self.y = (self.me // 4) % 2
        self.z = self.me // 8
        self.twin = self.me + 1 - 2 * self.core
        self.over_x = self.me + 2 - 4 * self.x
        self.over_y = self.me + 4 - 8 * self.y
        self.far = [(self.z + d) % depth for d in range(1, depth)]
        self.over_z = [self.me + (z - self.z) * 8 for z in self.far]

    def greet(self):
        barrier = pltpu.get_barrier_semaphore()

        def hello(d, _):
            peer = (self.me + d) % self.count
            pl.semaphore_signal(barrier, inc=1, device_id=(peer,), device_id_type=MESH)
            return 0

        lax.fori_loop(1, self.count, hello, 0)
        pl.semaphore_wait(barrier, self.count - 1)


def remote(source, target, send, recv, index, device):
    return pltpu.make_async_remote_copy(
        src_ref=source,
        dst_ref=target,
        send_sem=send.at[index],
        recv_sem=recv.at[index],
        device_id=(device,),
        device_id_type=MESH,
    )


def columns(start, width):
    return pl.ds(pl.multiple_of(start, 128), width)


class Gather:
    def __init__(self, place, pieces, staged, wholes, local, send, recv):
        self.place, self.pieces = place, pieces
        self.staged, self.wholes = staged, wholes
        self.local, self.send, self.recv = local, send, recv
        self.steps = 1 + 2 * (place.depth + 2)
        self.sent = []

    def begin(self, copy):
        copy.start()
        self.sent.append(copy)

    def rows(self, kind):
        height = self.staged[kind].shape[0]
        p = self.place
        return self.wholes[kind].at[p.z, p.y, p.x, pl.ds(p.core * height, height)]

    def quarter(self, i, core, order):
        kind, start, width = self.pieces[i]
        return columns(start + core * (width // 2) + order * (width // 4), width // 4)

    def copy(self, source, target, i, step, device):
        return remote(source, target, self.send, self.recv, i * self.steps + step, device)

    def to_twin(self, i):
        kind, start, width = self.pieces[i]
        cols = columns(start + (1 - self.place.core) * (width // 2), width // 2)
        return self.copy(
            self.staged[kind].at[:, cols], self.rows(kind).at[:, cols], i, 0, self.place.twin
        )

    def own(self, i):
        kind, start, width = self.pieces[i]
        cols = columns(start + self.place.core * (width // 2), width // 2)
        return pltpu.make_async_copy(
            self.staged[kind].at[:, cols], self.rows(kind).at[:, cols], self.local.at[i]
        )

    def along_z(self, i, order, d):
        p = self.place
        ref = self.wholes[self.pieces[i][0]].at[p.z, p.y, p.x, :, self.quarter(i, p.core, order)]
        return self.copy(ref, ref, i, 1 + order * (p.depth + 2) + d, p.over_z[d])

    def plane(self, i, order, second):
        p = self.place
        whole = self.wholes[self.pieces[i][0]]
        cols = self.quarter(i, p.core, order)
        if second:
            ref = whole.at[:, :, p.x, :, cols] if order else whole.at[:, p.y, :, :, cols]
        else:
            ref = whole.at[:, p.y, p.x, :, cols]
        device = p.over_x if order == second else p.over_y
        return self.copy(ref, ref, i, 1 + order * (p.depth + 2) + p.depth - 1 + second, device)

    def across(self, i, order):
        p = self.place
        whole = self.wholes[self.pieces[i][0]]
        ref = whole.at[:, :, :, :, self.quarter(i, p.core, order)]
        return self.copy(ref, ref, i, 1 + order * (p.depth + 2) + p.depth + 1, p.twin)

    def open(self):
        for i in range(len(self.pieces)):
            self.begin(self.to_twin(i))
        for i in range(len(self.pieces)):
            self.own(i).start()
        for i in range(len(self.pieces)):
            self.own(i).wait()
        for i in range(len(self.pieces)):
            self.to_twin(i).wait_recv()
            for d in range(self.place.depth - 1):
                for order in (0, 1):
                    self.begin(self.along_z(i, order, d))

    def advance(self, i, stage):
        if not 0 <= i < len(self.pieces):
            return
        for order in (0, 1):
            if stage == 0:
                for d in range(self.place.depth - 1):
                    self.along_z(i, order, d).wait_recv()
                self.begin(self.plane(i, order, 0))
            elif stage == 1:
                self.plane(i, order, 0).wait_recv()
                self.begin(self.plane(i, order, 1))
            elif stage == 2:
                self.plane(i, order, 1).wait_recv()
                self.begin(self.across(i, order))
            else:
                self.across(i, order).wait_recv()

    def turn(self, t):
        for stage in (3, 2, 1, 0):
            self.advance(t - GATHER_LAGS[stage], stage)

    def close(self):
        for copy in self.sent:
            copy.wait_send()


class Scatter:
    def __init__(self, place, pieces, blocks, outs, scratch):
        self.place, self.pieces, self.blocks, self.outs = place, pieces, blocks, outs
        self.grads, self.got, self.final, (self.local, self.send, self.recv) = (
            scratch[0],
            scratch[1:5],
            scratch[5],
            scratch[6:9],
        )
        self.steps = 1 + 2 * (place.depth + 2)
        self.done = [0] * 6

    @staticmethod
    def scratch(pieces, depth, blocks):
        tall = max(blocks[kind] * (width // 512) for kind, _, width in pieces)
        copies = len(pieces) * (1 + 2 * (depth + 2))
        return [
            pltpu.VMEM((SLOTS, 2, 2, depth, 2, 2, tall, 128), bf16),
            pltpu.VMEM((RING, 2, depth, 2, 2, tall, 128), bf16),
            pltpu.VMEM((RING + 1, 2, depth, 2, tall, 128), bf16),
            pltpu.VMEM((RING + 1, 2, depth, tall, 128), bf16),
            pltpu.VMEM((RING, 2, depth - 1, tall, 128), bf16),
            pltpu.VMEM((RING, 2, 2, tall // 2, 128), f32),
            pltpu.SemaphoreType.DMA((2 * len(pieces),)),
            pltpu.SemaphoreType.DMA((copies,)),
            pltpu.SemaphoreType.DMA((copies,)),
        ]

    def size(self, i):
        kind, start, width = self.pieces[i]
        return kind, start // 128, width // 512, self.blocks[kind]

    def rows(self, i):
        _, _, tiles, block = self.size(i)
        return pl.ds(0, tiles * block)

    def cut(self, ref, i):
        return ref.at[(slice(None),) * (len(ref.shape) - 2) + (self.rows(i),)]

    def mine(self, i, half, *quarter):
        return self.cut(self.grads.at[(i % SLOTS, half) + quarter], i)

    def theirs(self, level, i, *index):
        return self.cut(self.got[level].at[(i % self.got[level].shape[0],) + index], i)

    def copy(self, source, target, i, step, device):
        return remote(source, target, self.send, self.recv, i * self.steps + step, device)

    def to_twin(self, i):
        return self.copy(
            self.mine(i, 1 - self.place.core), self.theirs(0, i), i, 0, self.place.twin
        )

    def plane(self, i, order, second):
        p = self.place
        ref = self.mine(i, p.core, order)
        if second:
            ref = ref.at[:, p.y, 1 - p.x] if order else ref.at[:, 1 - p.y, p.x]
        else:
            ref = ref.at[:, 1 - p.y] if order else ref.at[:, :, 1 - p.x]
        device = p.over_x if order == second else p.over_y
        step = 1 + order * (p.depth + 2) + second
        return self.copy(ref, self.theirs(1 + second, i, order), i, step, device)

    def along_z(self, i, order, d):
        p = self.place
        ref = self.mine(i, p.core, order).at[p.far[d], p.y, p.x]
        step = 1 + order * (p.depth + 2) + 2 + d
        return self.copy(ref, self.theirs(3, i, order, d), i, step, p.over_z[d])

    def ends(self, i, order, core):
        kind, first, tiles, block = self.size(i)
        count = tiles * block // 2
        row = (first + (2 * self.place.core + order) * tiles) * (block // 2)
        source = self.final.at[i % RING, order, core, pl.ds(0, count)]
        return source, self.outs[kind].at[pl.ds(pl.multiple_of(row, 8), count)]

    def rest(self, i, order):
        p = self.place
        source, target = self.ends(i, order, 1 - p.core)
        return self.copy(source, target, i, 1 + order * (p.depth + 2) + p.depth + 1, p.twin)

    def keep(self, i, order):
        source, target = self.ends(i, order, self.place.core)
        return pltpu.make_async_copy(source, target, self.local.at[2 * i + order])

    def add(self, i, order, level, spots):
        rows = self.rows(i)
        slot, ring, core = i % SLOTS, i % self.got[level].shape[0], self.place.core

        def layer(z, _):
            for there, here in spots:
                at = (slot, core, order, z) + here + (rows,)
                total = self.grads[at].astype(f32)
                total = total + self.got[level][(ring, order, z) + there + (rows,)].astype(f32)
                self.grads[at] = total.astype(bf16)
            return 0

        lax.fori_loop(0, self.place.depth, layer, 0)

    def advance(self, i, stage):
        if not 0 <= i < len(self.pieces):
            return
        p = self.place
        if stage == 1:
            self.to_twin(i).wait_recv()
            for order in (0, 1):
                self.add(i, order, 0, [((y, x), (y, x)) for y in (0, 1) for x in (0, 1)])
                self.plane(i, order, 0).start()
        elif stage == 2:
            for order in (0, 1):
                self.plane(i, order, 0).wait_recv()
                self.add(
                    i, order, 1, [((k,), (p.y, k) if order else (k, p.x)) for k in (0, 1)]
                )
                self.plane(i, order, 1).start()
        elif stage == 3:
            for order in (0, 1):
                self.plane(i, order, 1).wait_recv()
                self.add(i, order, 2, [((), (p.y, p.x))])
                for d in range(p.depth - 1):
                    self.along_z(i, order, d).start()
        elif stage == 4:
            if i >= RING:
                self.settle(i - RING)
            _, _, tiles, block = self.size(i)
            rows, half = self.rows(i), block // 2
            for order in (0, 1):
                for d in range(p.depth - 1):
                    self.along_z(i, order, d).wait_recv()
                total = self.grads[i % SLOTS, p.core, order, p.z, p.y, p.x, rows].astype(f32)
                for d in range(p.depth - 1):
                    total = total + self.got[3][i % RING, order, d, rows].astype(f32)
                for tile in range(tiles):
                    for core in (0, 1):
                        row = tile * block + core * half
                        self.final[i % RING, order, core, pl.ds(tile * half, half)] = total[
                            row : row + half
                        ]
                self.rest(i, order).start()
                self.keep(i, order).start()
        else:
            self.to_twin(i).wait_send()
            for order in (0, 1):
                self.plane(i, order, 0).wait_send()
                self.plane(i, order, 1).wait_send()
                for d in range(p.depth - 1):
                    self.along_z(i, order, d).wait_send()
                self.rest(i, order).wait_recv()

    def settle(self, i):
        for order in (0, 1):
            self.rest(i, order).wait_send()
            self.keep(i, order).wait()

    def pump(self, lags=SCATTER_LAGS):
        for stage in (5, 4, 3, 2, 1):
            if self.done[stage] + lags[stage] <= self.done[stage - 1]:
                self.advance(self.done[stage], stage)
                self.done[stage] += 1

    def produce(self, left, right, column):
        i = self.done[0]
        self.pump()
        while self.done[5] <= i - SLOTS:
            self.pump()
        self.done[0] += 1
        _, _, tiles, block = self.size(i)
        slot = i % SLOTS
        group = 1 if block % 32 == 0 else 2
        turns = self.place.depth // group
        high = 4 * block * group

        def chunk(k, _):
            n, first = k // turns, (k % turns) * group
            part = transposed(
                left[:, columns(k % turns * high, high)], right[:, columns(column + 256 * n, 256)]
            ).astype(bf16)
            for tile in (0, 1):
                for b in range(4 * group):
                    spot = first + b // 4, b // 2 % 2, b % 2
                    piece = part[b * block : b * block + block, tile * 128 : tile * 128 + 128]
                    if tiles == 2:
                        at = (slot, n // 2, n % 2) + spot + (pl.ds(tile * block, block),)
                    else:
                        at = (slot, n, tile) + spot + (pl.ds(0, block),)
                    self.grads[at] = piece
            return 0

        lax.fori_loop(0, 2 * tiles * turns, chunk, 0)
        self.to_twin(i).start()

    def close(self):
        while self.done[5] < len(self.pieces):
            self.pump(DRAIN)
        for i in range(max(0, len(self.pieces) - RING), len(self.pieces)):
            self.settle(i)


class Redeal:
    def __init__(self, place, given, spread, moved, wanted, send, recv):
        self.place, self.given, self.spread, self.moved = place, given, spread, moved
        self.wanted, self.send, self.recv = wanted, send, recv
        self.high, self.wide = spread.shape[2:]

    def spot(self, ref, j):
        depth = self.place.depth
        rows = pl.ds(pl.multiple_of((j // depth) * self.high, self.high), self.high)
        return ref.at[:, rows, columns((j % depth) * self.wide, self.wide)]

    def peer(self, d):
        return (self.place.me + d) % self.place.count

    def out(self, d):
        target = self.spread.at[self.place.me]
        peer = self.peer(d)
        return remote(self.spot(self.given, peer), target, self.send, self.recv, d - 1, peer)

    def home(self, d):
        peer, count = self.peer(d), self.place.count
        target = self.spot(self.wanted, self.place.me)
        return remote(
            self.moved.at[peer], target, self.send, self.recv, count - 1 + d - 1, peer
        )

    def each(self, act):
        def one(d, _):
            act(d)
            return 0

        lax.fori_loop(1, self.place.count, one, 0)

    def own(self, ref):
        j = self.place.me
        depth = self.place.depth
        rows = pl.ds(pl.multiple_of((j // depth) * self.high, self.high), self.high)
        return slice(None), rows, columns((j % depth) * self.wide, self.wide)

    def begin(self):
        self.each(lambda d: self.out(d).start())
        self.spread[self.place.me] = self.given[self.own(self.given)]

    def middle(self, source):
        self.each(lambda d: self.out(d).wait())

        def one(j, _):
            for m in range(self.moved.shape[1]):
                self.moved[j, m] = self.spread[source[m, j], m]
            return 0

        lax.fori_loop(0, self.place.count, one, 0)
        self.each(lambda d: self.home(d).start())
        self.wanted[self.own(self.wanted)] = self.moved[self.place.me]

    def end(self):
        self.each(lambda d: self.home(d).wait())


def spread_small(place, tile, table, send, recv):
    table[place.me] = tile[...]

    def out(d, _):
        remote(
            tile, table.at[place.me], send, recv, d - 1, (place.me + d) % place.count
        ).start()
        return 0

    lax.fori_loop(1, place.count, out, 0)


def collect_small(place, tile, table, send, recv):
    def back(d, _):
        copy = remote(
            tile,
            table.at[(place.me + place.count - d) % place.count],
            send,
            recv,
            d - 1,
            (place.me + d) % place.count,
        )
        copy.wait()
        return 0

    lax.fori_loop(1, place.count, back, 0)


def cut_columns(widths, start=0):
    pieces = []
    for width in widths:
        pieces.append((0, start, width))
        start += width
    return pieces


def kernel_depth(count, wide, deep):
    fits = count % 8 == 0 and wide.shape[0] % 8 == 0 and deep.shape[0] % 8 == 0
    return count // 8 if fits else 0


def transposed(left, right):
    return lax.dot_general(
        left, right, (((0,), (0,)), ((), ())), preferred_element_type=f32
    )


def against(left, right):
    return lax.dot_general(
        left, right, (((1,), (1,)), ((), ())), preferred_element_type=f32
    )


class Stream:
    def __init__(self, refs, tiles, slots, sems):
        self.refs, self.tiles, self.slots, self.sems = refs, tiles, slots, sems
        self.next, self.begun = 0, 0

    def copy(self, k):
        kind, start, size = self.tiles[k]
        slot = k % self.slots.shape[0]
        cut = pl.ds(0, size)
        if kind:
            source, target = self.refs[1].at[pl.ds(start, size)], self.slots.at[slot, cut]
        else:
            source, target = self.refs[0].at[:, pl.ds(start, size)], self.slots.at[slot, :, cut]
        return pltpu.make_async_copy(source, target, self.sems.at[slot])

    def take(self):
        ahead = min(len(self.tiles), self.next + self.slots.shape[0])
        while self.begun < ahead:
            self.copy(self.begun).start()
            self.begun += 1
        k = self.next
        self.copy(k).wait()
        self.next += 1
        return self.slots.at[k % self.slots.shape[0]]


def back_into(total, left, start, size, tile, fresh):
    def chunk(n, _):
        cols = columns(n * 256, 256)
        part = against(left[:, start : start + size], tile[cols, 0:size])
        rows = pl.ds(0, left.shape[0])
        total[rows, cols] = part if fresh else total[rows, cols] + part
        return 0

    lax.fori_loop(0, D // 256, chunk, 0)


def back_rounded(out, left, tile):
    def chunk(n, _):
        cols = columns(n * 256, 256)
        out[:, cols] = against(left[...], tile[cols, :]).astype(bf16)
        return 0

    lax.fori_loop(0, D // 256, chunk, 0)


def self_scores(bias, scores, block, head):
    marked = bias[block, head].astype(f32)
    return jnp.where(marked < -1e29, masked_score, scores + marked)


def cross_scores(live, scores, block, head):
    return jnp.where(live[block, 0:1, :] > 0.0, scores, masked_score)


def pair_loop(first, last, body_of):
    def one(index, _):
        body_of(index // (H // 2), index % (H // 2))
        return 0

    lax.fori_loop(first, last, one, 0)


def softmax_rows(scores):
    weights = jnp.exp(scores - jnp.max(scores, axis=1, keepdims=True))
    return weights / jnp.sum(weights, axis=1, keepdims=True)


def attend_back_pairs(refs, grads, marks, mask, folded, first, last):
    q, k, v, da = refs
    dq, dk, dv = grads
    rows_q = 128
    tall = k.shape[0] // (q.shape[0] // rows_q)
    even = lax.broadcasted_iota(jnp.int32, (1, 128), 1) < DH
    down, right = [lax.broadcasted_iota(jnp.int32, (rows_q, rows_q), k) for k in (0, 1)]
    mirror = jnp.where(down + right == rows_q - 1, 1.0, 0.0).astype(bf16)

    def pair(block, p):
        rows = pl.ds(pl.multiple_of(block * rows_q, rows_q), rows_q)
        keys = pl.ds(pl.multiple_of(block * tall, tall), tall)
        cols = columns(p * 128, 128)
        q2, k2, v2, da2 = q[rows, cols], k[keys, cols], v[keys, cols], da[rows, cols]
        sums = [None, None, None]
        for e in (0, 1):
            keep = even if e == 0 else jnp.logical_not(even)

            def half(value):
                return jnp.where(keep, value.astype(f32), 0.0).astype(bf16)

            qe, dae, ke = half(q2), half(da2), half(k2)
            head = 2 * p + e
            probs = softmax_rows(mask(marks, against(qe, k2), block, head))
            dp = against(dae, v2)
            centre = jnp.sum(probs * dp, axis=1, keepdims=True)
            ds = (probs * (dp - centre)).astype(bf16)
            terms = (
                jnp.dot(ds, ke, preferred_element_type=f32),
                transposed(ds, qe),
                transposed(probs.astype(bf16), dae),
            )
            sums = [t if s is None else s + t for s, t in zip(sums, terms)]
            if folded is not None:
                upside = jnp.dot(mirror, ds, preferred_element_type=f32)
                turned = pltpu.roll(upside, 0, 1, stride=1, stride_axis=0)
                folded[block * H + head] = jnp.sum(turned, axis=0, keepdims=True)
        dq[rows, cols] = sums[0].astype(bf16)
        dk[keys, cols] = sums[1].astype(bf16)
        dv[keys, cols] = sums[2].astype(bf16)

    pair_loop(first, last, pair)


def norm_back_rows(values, gain_row, grad, base, out, total):
    total[...] = jnp.zeros_like(total)

    def chunk(k, _):
        rows = pl.ds(pl.multiple_of(k * 64, 64), 64)
        v = values[rows, :].astype(f32)
        inverse = inverse_rms(v)
        scaled = v * inverse
        g = grad[rows, :]
        weighted = g * gain_row[...]
        centre = jnp.mean(weighted * scaled, axis=-1, keepdims=True)
        out[rows, :] = base[rows, :].astype(f32) + inverse * (weighted - scaled * centre)
        total[...] += jnp.sum(g * scaled, axis=0, keepdims=True)
        return 0

    lax.fori_loop(0, values.shape[0] // 64, chunk, 0)


def small_tables(gain_sums, folded, buckets, tables, count):
    each, share = D // count, H * NB // count
    split, micro = NB // share, folded.shape[0] // H
    lane = lax.broadcasted_iota(jnp.int32, (D, 128), 1)
    col = lax.broadcasted_iota(jnp.int32, (D, 128), 0)
    device = lax.broadcasted_iota(jnp.int32, (count, D), 0)
    owner = lax.broadcasted_iota(jnp.int32, (count, D), 1) // each
    total = jnp.zeros((count, 128), f32)
    for k in range(3):
        pick = jnp.where(lane == k * each + col % each, 1.0, 0.0)
        mine = jnp.where(device == owner, gain_sums[k], 0.0)
        total = total + jnp.dot(mine, pick, precision=highest, preferred_element_type=f32)
    spot = lax.broadcasted_iota(jnp.int32, (128, 128), 1) - 3 * each
    inside = (spot >= 0) & (spot < share)
    for part in range(split):
        found = jnp.zeros((H, 128), f32)
        for block in range(micro):
            hit = inside & (buckets[block] == spot + part * share)
            rows = jnp.concatenate([folded[block * H + h] for h in range(H)], axis=0)
            found = found + jnp.dot(
                rows, jnp.where(hit, 1.0, 0.0), precision=highest, preferred_element_type=f32
            )
        for h in range(H):
            j = h * split + part
            row = total[j : j + 1] + found[h : h + 1]
            tables[j] = jnp.broadcast_to(row, (8, 128))


def swap_small(place, tables, got, send, recv, act):
    def one(d, _):
        peer = (place.me + d) % place.count
        act(remote(tables.at[peer], got.at[place.me], send, recv, d - 1, peer))
        return 0

    lax.fori_loop(1, place.count, one, 0)


BACK_INPUTS = (
    "result", "dy", "hd", "n3", "r2", "ac", "cq", "ck", "cv", "n2",
    "enc", "r1", "mixed", "q", "k", "v", "n1", "x", "bias", "pre",
)
BACK_ORDER = ("xo", "xq", "o", "xk", "xv", "q", "k", "v")
SCATTER_ORDER = ("xo", "xq", "xk", "xv", "o", "q", "k", "v")


def backward_kernel(pieces, depth, blocks, *refs):
    refs = list(refs)

    def pop(count):
        return [refs.pop(0) for _ in range(count)]

    whole, down, source, live, buckets, gains = pop(6)
    ins = dict(zip(BACK_INPUTS, pop(len(BACK_INPUTS))))
    out, out_deep, layer_out, grad_in, grad_enc, small_out = pop(6)
    held = dict(zip(BACK_INPUTS[:-1], pop(len(BACK_INPUTS) - 1)))
    load_sems, slots, slot_sems, pre, pre_sems, out_sems = pop(6)
    dgu, acc, dr2, dr1, low, dmix, dq, dk, dv, dck, dcv = pop(11)
    spread, moved, wanted, deal_send, deal_recv = pop(5)
    gain_sums, folded, tables, got, small_send, small_recv = pop(6)
    place = Place(depth)
    scatter = Scatter(place, pieces, blocks, (out, out_deep), refs)
    units = held["hd"].shape[1]
    rows = held["dy"].shape[0]

    loads = {
        name: pltpu.make_async_copy(ins[name], held[name], load_sems.at[i])
        for i, name in enumerate(BACK_INPUTS[:-1])
    }
    for load in loads.values():
        load.start()

    def need(*names):
        for name in names:
            loads.pop(name).wait()

    tiles = [(1, start, min(1024, units - start)) for start in range(0, units, 1024)]
    tiles += [(0, 8 * D + k, min(1024, 2 * units - k)) for k in range(0, 2 * units, 1024)]
    tiles += [(0, D * LEFT.index(w), D) for w in BACK_ORDER]
    stream = Stream((whole, down), tiles, slots, slot_sems)

    def ahead(k):
        return [
            pltpu.make_async_copy(
                ins["pre"].at[:, columns(j * units + k * 256, 256)],
                pre.at[k % 2, j],
                pre_sems.at[k % 2, j],
            )
            for j in (0, 1)
        ]

    for load in ahead(0):
        load.start()
    place.greet()
    redeal = Redeal(place, held["result"], spread, moved, wanted, deal_send, deal_recv)
    need("result")
    redeal.begin()

    need("dy", "hd")
    dy = held["dy"]
    scatter.produce(held["hd"], dy, 0)
    scatter.produce(held["hd"], dy, 512)
    for start in range(0, units, 1024):
        tile = stream.take()

        def chunk(n, _):
            k = start // 256 + n

            @pl.when(k + 1 < units // 256)
            def _():
                for load in ahead(k + 1):
                    load.start()

            for load in ahead(k):
                load.wait()
            part = against(dy[...], tile[pl.ds(pl.multiple_of(n * 256, 256), 256), :])
            act, slope = gelu_parts(pre[k % 2, 0])
            dgu[:, columns(k * 256, 256)] = (part * pre[k % 2, 1] * slope).astype(bf16)
            dgu[:, columns(units + k * 256, 256)] = (part * act).astype(bf16)
            return 0

        lax.fori_loop(0, min(1024, units - start) // 256, chunk, 0)
        scatter.pump()
    starts = list(range(0, 2 * units, 1024))
    halves = rows // 128 * (H // 2)
    quarter = halves // 4

    def cross(part):
        attend_back_pairs(
            (held["cq"], held["ck"], held["cv"], dmix),
            (dq, dck, dcv),
            live,
            cross_scores,
            None,
            part * quarter,
            part * quarter + quarter,
        )

    def within(part):
        attend_back_pairs(
            (held["q"], held["k"], held["v"], dmix),
            (dq, dk, dv),
            held["bias"],
            self_scores,
            folded,
            part * quarter,
            part * quarter + quarter,
        )

    def feed():
        start = starts.pop(0)
        scatter.produce(held["n3"], dgu, start)

    need("n3")
    feed()
    for k, start in enumerate(range(0, 2 * units, 1024)):
        back_into(acc, dgu, start, min(1024, 2 * units - start), stream.take(), k == 0)
        if k == 2:
            feed()
    need("r2")
    norm_back_rows(held["r2"], gains.at[2], acc, dy, dr2, gain_sums.at[2])
    low[...] = dr2[...].astype(bf16)
    back_rounded(dmix, low, stream.take())
    feed()
    need("cq", "ck", "cv")
    for part in range(4):
        cross(part)
        if starts:
            feed()
        else:
            scatter.pump()
    while starts:
        feed()
    redeal.middle(source)
    need("ac")
    scatter.produce(held["ac"], low, 0)
    back_into(acc, dq, 0, D, stream.take(), True)
    need("r1")
    norm_back_rows(held["r1"], gains.at[1], acc, dr2, dr1, gain_sums.at[1])
    low[...] = dr1[...].astype(bf16)
    back_rounded(dmix, low, stream.take())
    need("n2", "enc")
    scatter.produce(held["n2"], dq, 0)
    need("q", "k", "v", "bias")
    within(0)
    within(1)
    scatter.produce(held["enc"], dck, 0)
    within(2)
    within(3)
    scatter.produce(held["enc"], dcv, 0)
    back_into(acc, dck, 0, D, stream.take(), True)
    back_into(acc, dcv, 0, D, stream.take(), False)
    enc_out = pltpu.make_async_copy(acc, grad_enc, out_sems.at[0])
    enc_out.start()
    need("mixed")
    scatter.produce(held["mixed"], low, 0)
    need("n1")
    for grad in (dq, dk, dv):
        scatter.produce(held["n1"], grad, 0)
    scatter.produce(held["n1"], dv, 512)
    enc_out.wait()
    for index, grad in enumerate((dq, dk, dv)):
        back_into(acc, grad, 0, D, stream.take(), index == 0)
        scatter.pump(DRAIN)
    need("x")
    norm_back_rows(held["x"], gains.at[0], acc, dr1, dr2, gain_sums.at[0])
    in_out = pltpu.make_async_copy(dr2, grad_in, out_sems.at[1])
    in_out.start()
    scatter.pump(DRAIN)
    small_tables(gain_sums, folded, buckets, tables, place.count)
    swap_small(place, tables, got, small_send, small_recv, lambda copy: copy.start())
    got[place.me] = tables[place.me]
    scatter.pump(DRAIN)
    redeal.end()
    deal_out = pltpu.make_async_copy(wanted, layer_out, out_sems.at[2])
    deal_out.start()
    scatter.close()
    swap_small(place, tables, got, small_send, small_recv, lambda copy: copy.wait())
    small_out[...] = jnp.sum(got[...], axis=0)
    in_out.wait()
    deal_out.wait()


def backward_all(whole, down, source, live, buckets, gains, acts, depth):
    tall, width = whole.shape
    tall_deep = down.shape[0]
    blocks = (tall // (4 * depth), tall_deep // (4 * depth))
    micro, length = acts["result"].shape[:2]
    rows, keys = micro * length, acts["enc"].shape[0]
    units, count = tall_deep, 8 * depth
    pieces = [(1, 0, 512), (1, 512, 512)]
    pieces += [(0, 8 * D + k, min(1024, 2 * units - k)) for k in range(0, 2 * units, 1024)]
    pieces += [(0, D * LEFT.index(w), D) for w in SCATTER_ORDER[:-1]]
    pieces += [(0, D * LEFT.index(SCATTER_ORDER[-1]) + k, 512) for k in (0, 512)]
    anywhere = pl.BlockSpec(memory_space=pl.ANY)
    inside = pl.BlockSpec(memory_space=pltpu.VMEM)
    arrays = [acts[name] for name in BACK_INPUTS]
    spots = (micro, length // 8, D // depth)
    held = [pltpu.VMEM(a.shape, a.dtype) for a in arrays[:-1]]
    square = [pltpu.VMEM((rows, D), f32)] * 2 + [pltpu.VMEM((rows, D), bf16)] * 5
    return pl.pallas_call(
        functools.partial(backward_kernel, pieces, depth, blocks),
        out_shape=(
            jax.ShapeDtypeStruct((width // 128 * (blocks[0] // 2), 128), f32),
            jax.ShapeDtypeStruct((D // 128 * (blocks[1] // 2), 128), f32),
            jax.ShapeDtypeStruct((micro, length, D), bf16),
            jax.ShapeDtypeStruct((rows, D), f32),
            jax.ShapeDtypeStruct((keys, D), f32),
            jax.ShapeDtypeStruct((8, 128), f32),
        ),
        in_specs=[anywhere] * 2
        + [pl.BlockSpec(memory_space=pltpu.SMEM)]
        + [inside] * 3
        + [anywhere] * len(arrays),
        out_specs=(anywhere,) * 5 + (inside,),
        scratch_shapes=held
        + [
            pltpu.SemaphoreType.DMA((len(held),)),
            pltpu.VMEM((2, D, 1024), bf16),
            pltpu.SemaphoreType.DMA((2,)),
            pltpu.VMEM((2, 2, rows, 256), f32),
            pltpu.SemaphoreType.DMA((2, 2)),
            pltpu.SemaphoreType.DMA((3,)),
            pltpu.VMEM((rows, 2 * units), bf16),
            pltpu.VMEM((keys, D), f32),
        ]
        + square
        + [pltpu.VMEM((keys, D), bf16)] * 2
        + [
            pltpu.VMEM((count,) + spots, bf16),
            pltpu.VMEM((count,) + spots, bf16),
            pltpu.VMEM((micro, length, D), bf16),
            pltpu.SemaphoreType.DMA((2 * (count - 1),)),
            pltpu.SemaphoreType.DMA((2 * (count - 1),)),
            pltpu.VMEM((3, 1, D), f32),
            pltpu.VMEM((micro * H, 1, length), f32),
            pltpu.VMEM((count, 8, 128), f32),
            pltpu.VMEM((count, 8, 128), f32),
            pltpu.SemaphoreType.DMA((count - 1,)),
            pltpu.SemaphoreType.DMA((count - 1,)),
        ]
        + Scatter.scratch(pieces, depth, blocks),
        compiler_params=pltpu.CompilerParams(
            collective_id=1, has_side_effects=True, vmem_limit_bytes=67043328
        ),
        name="backward",
    )(whole, down, source, live, buckets, gains, *arrays)


ACTS = ("hd", "n3", "r2", "ac", "cq", "ck", "cv", "n2", "r1", "mixed", "q", "k", "v", "n1", "bias")
LEFT = ("xk", "xv", "q", "k", "v", "o", "xq", "xo")


def norm_rows(values, gain_row, out):
    def chunk(k, _):
        rows = pl.ds(pl.multiple_of(k * 64, 64), 64)
        v = values[rows, :].astype(f32)
        out[rows, :] = (v * inverse_rms(v) * gain_row[...]).astype(bf16)
        return 0

    lax.fori_loop(0, values.shape[0] // 64, chunk, 0)


def by_columns(left, tile, width, put):
    def chunk(k, _):
        part = tile[:, :, :, :, columns(k * 256, 256)].reshape(-1, 256)
        put(k, jnp.dot(left[...], part, preferred_element_type=f32))
        return 0

    lax.fori_loop(0, width // 256, chunk, 0)


def attend_pairs(refs, out, marks, mask, first, last):
    q, k, v = refs
    rows_q = 128
    tall = k.shape[0] // (q.shape[0] // rows_q)
    even = lax.broadcasted_iota(jnp.int32, (1, 128), 1) < DH

    def pair(block, p):
        rows = pl.ds(pl.multiple_of(block * rows_q, rows_q), rows_q)
        keys = pl.ds(pl.multiple_of(block * tall, tall), tall)
        cols = columns(p * 128, 128)
        q2, k2, v2 = q[rows, cols], k[keys, cols], v[keys, cols]
        total = None
        for e in (0, 1):
            keep = even if e == 0 else jnp.logical_not(even)

            def half(value):
                return jnp.where(keep, value.astype(f32), 0.0).astype(bf16)

            probs = softmax_rows(mask(marks, against(half(q2), k2), block, 2 * p + e))
            term = jnp.dot(probs.astype(bf16), half(v2), preferred_element_type=f32)
            total = term if total is None else total + term
        out[rows, cols] = total.astype(bf16)

    pair_loop(first, last, pair)


def gain_rows(table, gains, count):
    each = D // count
    values = jnp.sum(table[...], axis=1).astype(bf16)
    lane = lax.broadcasted_iota(jnp.int32, (128, D), 0)
    col = lax.broadcasted_iota(jnp.int32, (128, D), 1)
    device = lax.broadcasted_iota(jnp.int32, (count, D), 0)
    owner = lax.broadcasted_iota(jnp.int32, (count, D), 1) // each
    for k in range(3):
        pick = jnp.where(lane == k * each + col % each, 1.0, 0.0).astype(bf16)
        spread = jnp.dot(values, pick, preferred_element_type=f32)
        gains[k] = jnp.sum(jnp.where(device == owner, spread, 0.0), axis=0, keepdims=True)


def bias_block(table, buckets, allowed, by_offset, bias, count, block):
    first, share = 3 * (D // count), H * NB // count
    split = NB // share
    values = jnp.sum(table[...], axis=1).astype(bf16)
    lane = lax.broadcasted_iota(jnp.int32, (128, 128), 0) - first
    for part in range(split):
        hit = (lane + part * share == buckets[block, 0:1, :]) & (lane >= 0) & (lane < share)
        pick = jnp.where(hit, 1.0, 0.0).astype(bf16)
        found = jnp.dot(values, pick, preferred_element_type=f32)
        for device in range(count):
            by_offset[part, device] = found[device : device + 1]

    def head_bias(head, _):
        row = by_offset[0, head * split]
        for part in range(1, split):
            row = row + by_offset[part, head * split + part]
        grid = pltpu.roll(
            jnp.broadcast_to(row, (128, 128)), 0, 1, stride=1, stride_axis=0
        )
        bias[block, head] = jnp.where(allowed[block] > 0.0, grid, -1e30).astype(bf16)
        return 0

    lax.fori_loop(0, H, head_bias, 0)


def forward_kernel(pieces, depth, widths, *refs):
    refs = list(refs)

    def pop(count):
        return [refs.pop(0) for _ in range(count)]

    wide = pop(len(widths))
    (deep, tile, source, live, allowed, buckets, hidden, encoder, cotangent) = pop(9)
    whole, whole_deep, gains, dy, result, pre = pop(6)
    outs = dict(zip(ACTS, pop(len(ACTS))))
    staged, staged_deep, table, by_offset, x, enc, cot = pop(7)
    held = dict(zip(ACTS, pop(len(ACTS))))
    pre_held, result_held, slots, slot_sems, down_sems, down_slot, spread, moved, wanted = pop(9)
    stage_sems, load_sems, out_sems, own_sems, send, recv, small_send, small_recv = pop(8)
    deal_send, deal_recv = pop(2)
    place = Place(depth)
    count = place.count
    rows, units = x.shape[0], held["hd"].shape[1]
    gather = Gather(
        place, pieces, (staged, staged_deep), (whole, whole_deep), own_sems, send, recv
    )
    staging, start = [], 0
    for i, width in enumerate(widths):
        target = staged.at[:, pl.ds(start, width)]
        staging.append(pltpu.make_async_copy(wide[i], target, stage_sems.at[i]))
        start += width
    staging.append(pltpu.make_async_copy(deep, staged_deep, stage_sems.at[len(widths)]))
    loads = [
        pltpu.make_async_copy(a, b, load_sems.at[i])
        for i, (a, b) in enumerate(((cotangent, cot), (hidden, x), (encoder, enc)))
    ]
    for copy in staging + loads:
        copy.start()
    place.greet()
    spread_small(place, tile, table, small_send, small_recv)
    redeal = Redeal(place, cot, spread, moved, wanted, deal_send, deal_recv)
    loads[0].wait()
    redeal.begin()
    for copy in staging:
        copy.wait()
    gather.open()
    collect_small(place, tile, table, small_send, small_recv)
    loads[1].wait()
    loads[2].wait()

    leaving = []

    def leave(name, source_ref=None, target=None):
        copy = pltpu.make_async_copy(
            held[name] if source_ref is None else source_ref,
            outs[name] if target is None else target,
            out_sems.at[len(leaving)],
        )
        copy.start()
        leaving.append(copy)

    tiles = [(D * k, D) for k in range(len(LEFT))]
    tiles += [(8 * D + k, min(1024, 2 * units - k)) for k in range(0, 2 * units, 1024)]

    def fetch(k):
        start, width = tiles[k]
        slot = k % slots.shape[0]
        return pltpu.make_async_copy(
            whole.at[:, :, :, :, pl.ds(start, width)],
            slots.at[slot, :, :, :, :, pl.ds(0, width)],
            slot_sems.at[slot],
        )

    def rounded(out):
        def put(k, part):
            out[:, columns(k * 256, 256)] = part.astype(bf16)

        return put

    def added(base, out):
        def put(k, part):
            cols = columns(k * 256, 256)
            out[:, cols] = base[:, cols].astype(f32) + part

        return put

    def units_of(k, tile_ref):
        start, width = tiles[k][0] - 8 * D, tiles[k][1]

        def put(n, part):
            at = start // 256 + n
            pre_held[:, columns(at * 256, 256)] = part

            @pl.when(at >= units // 256)
            def _():
                cols = columns((at - units // 256) * 256, 256)
                act, _ = gelu_parts(pre_held[:, cols])
                held["hd"][:, cols] = (act * part).astype(bf16)

        by_columns(held["n3"], tile_ref, width, put)

    whole_pairs = rows // 128 * (H // 2)
    work = []

    def piece_of(k):
        kind, end = (1, 0) if k is None else (0, sum(tiles[k]))
        ends = [s + w if kd == 0 else 0 for kd, s, w in pieces]
        return next(i for i, e in enumerate(ends) if e >= end)

    def with_tile(k, cost, act):
        def run():
            if k not in fetched:
                fetch(k).start()
                fetched.append(k)
            fetch(k).wait()
            act(slots.at[k % slots.shape[0]])
            used.append(k)

        work.append((piece_of(k), cost, run))

    def then(cost, act):
        work.append((0, cost, act))

    fetched, used = [], []

    def encoded(name):
        def act(ref):
            by_columns(enc, ref, D, rounded(held[name]))
            leave(name)

        return act

    def projected(name, left):
        def act(ref):
            by_columns(held[left], ref, D, rounded(held[name]))
            leave(name)

        return act

    def summed(left, base, total, gain, normed):
        def act(ref):
            by_columns(held[left], ref, D, added(base, held[total]))
            norm_rows(held[total], gains.at[gain], held[normed])
            leave(total)
            leave(normed)

        return act

    def attention(cost, names, out, marks, mask):
        for part in range(4):

            def act(part=part):
                attend_pairs(
                    [held[name] for name in names],
                    held[out],
                    marks,
                    mask,
                    part * whole_pairs // 4,
                    (part + 1) * whole_pairs // 4,
                )
                if part == 3:
                    leave(out)

            then(cost, act)

    def first_norm():
        gain_rows(table, gains, count)
        norm_rows(x, gains.at[0], held["n1"])
        leave("n1")

    work.append((-count, 3, first_norm))
    for block in range(held["bias"].shape[0]):

        def biases(block=block):
            bias_block(table, buckets, allowed, by_offset, held["bias"], count, block)
            if block == held["bias"].shape[0] - 1:
                leave("bias")

        work.append((-count, 3, biases))
    for k, name in enumerate(("ck", "cv")):
        with_tile(k, 4, encoded(name))
    for k, name in enumerate(("q", "k", "v")):
        with_tile(2 + k, 2, projected(name, "n1"))
    attention(2, ("q", "k", "v"), "mixed", held["bias"], self_scores)
    with_tile(5, 3, summed("mixed", x, "r1", 1, "n2"))
    with_tile(6, 2, projected("cq", "n2"))
    attention(3, ("cq", "ck", "cv"), "ac", live, cross_scores)
    with_tile(7, 3, summed("ac", held["r1"], "r2", 2, "n3"))
    for k in range(len(LEFT), len(tiles)):
        with_tile(k, 3, functools.partial(units_of, k))

    deep_pieces = [i for i, piece in enumerate(pieces) if piece[0]]
    downs = []
    for number, i in enumerate(deep_pieces):
        cut = pl.ds(pieces[i][1], pieces[i][2])
        downs.append(
            pltpu.make_async_copy(
                whole_deep.at[:, :, :, :, cut],
                down_slot.at[:, :, :, :, cut],
                down_sems.at[number],
            )
        )

    def last(k, part):
        cols = columns(k * 256, 256)
        result_held[:, cols] = (held["r2"][:, cols] + part).astype(bf16)

    for t in range(len(pieces) + GATHER_LAGS[3]):
        gather.turn(t)
        ready = t - GATHER_LAGS[3]
        if ready in deep_pieces:
            downs[deep_pieces.index(ready)].start()
        while len(fetched) < len(tiles) and piece_of(len(fetched)) <= ready:
            if len(fetched) >= len(used) + slots.shape[0]:
                break
            fetch(len(fetched)).start()
            fetched.append(len(fetched))
        if t == 6:
            redeal.middle(source)
        spent = 0
        while work and spent < 6 and work[0][0] <= ready:
            _, cost, run = work.pop(0)
            run()
            spent += cost
    while work:
        work.pop(0)[2]()
    leave("", pre_held, pre)
    leave("hd")
    for down in downs:
        down.wait()
    by_columns(held["hd"], down_slot, D, last)
    leave("", result_held, result)
    redeal.end()
    leave("", wanted, dy)
    for copy in leaving:
        copy.wait()
    gather.close()


def forward_all(wide, deep, small, source, live, allowed, buckets, hidden, encoder, cotangent, depth):
    widths = [part.shape[1] for part in wide]
    width, tall = sum(widths), wide[0].shape[0]
    tall_deep, units = deep.shape[0], widths[-1]
    rows, keys = hidden.shape[0], encoder.shape[0]
    micro, length = cotangent.shape[:2]
    pieces = cut_columns([512, 512] + [1024] * 7)
    pieces += [(0, k, min(1024, width - k)) for k in range(8 * D, width, 1024)]
    pieces += [(1, 0, 512), (1, 512, 512)]
    copies = len(pieces) * (1 + 2 * (depth + 2))
    count = 8 * depth
    tile = jnp.zeros((8, 128), f32).at[0, : small.shape[0]].set(small.astype(f32))
    anywhere = pl.BlockSpec(memory_space=pl.ANY)
    inside = pl.BlockSpec(memory_space=pltpu.VMEM)
    spots = (micro, length // 8, D // depth)
    kinds = dict(
        hd=((rows, units), bf16),
        n3=((rows, D), bf16),
        r2=((rows, D), f32),
        ac=((rows, D), bf16),
        cq=((rows, D), bf16),
        ck=((keys, D), bf16),
        cv=((keys, D), bf16),
        n2=((rows, D), bf16),
        r1=((rows, D), f32),
        mixed=((rows, D), bf16),
        q=((rows, D), bf16),
        k=((rows, D), bf16),
        v=((rows, D), bf16),
        n1=((rows, D), bf16),
        bias=((micro, H, length, length), bf16),
    )
    results = pl.pallas_call(
        functools.partial(forward_kernel, pieces, depth, widths),
        out_shape=(
            jax.ShapeDtypeStruct((depth, 2, 2, 2 * tall, width), bf16),
            jax.ShapeDtypeStruct((depth, 2, 2, 2 * tall_deep, D), bf16),
            jax.ShapeDtypeStruct((3, 1, D), f32),
            jax.ShapeDtypeStruct((micro, length, D), bf16),
            jax.ShapeDtypeStruct((rows, D), bf16),
            jax.ShapeDtypeStruct((rows, 2 * units), f32),
        )
        + tuple(jax.ShapeDtypeStruct(*kinds[name]) for name in ACTS),
        in_specs=[anywhere] * (len(wide) + 1)
        + [inside, pl.BlockSpec(memory_space=pltpu.SMEM)]
        + [inside] * 3
        + [anywhere] * 3,
        out_specs=(anywhere,) * 2 + (inside,) + (anywhere,) * (3 + len(ACTS)),
        scratch_shapes=[
            pltpu.VMEM((tall, width), bf16),
            pltpu.VMEM((tall_deep, D), bf16),
            pltpu.VMEM((count, 8, 128), f32),
            pltpu.VMEM((2, count, 1, 128), f32),
            pltpu.VMEM((rows, D), bf16),
            pltpu.VMEM((keys, D), bf16),
            pltpu.VMEM((micro, length, D), bf16),
        ]
        + [pltpu.VMEM(*kinds[name]) for name in ACTS]
        + [
            pltpu.VMEM((rows, 2 * units), f32),
            pltpu.VMEM((rows, D), bf16),
            pltpu.VMEM((5, depth, 2, 2, 2 * tall, 1024), bf16),
            pltpu.SemaphoreType.DMA((5,)),
            pltpu.SemaphoreType.DMA((2,)),
            pltpu.VMEM((depth, 2, 2, 2 * tall_deep, D), bf16),
            pltpu.VMEM((count,) + spots, bf16),
            pltpu.VMEM((count,) + spots, bf16),
            pltpu.VMEM((micro, length, D), bf16),
            pltpu.SemaphoreType.DMA((len(wide) + 1,)),
            pltpu.SemaphoreType.DMA((3,)),
            pltpu.SemaphoreType.DMA((len(ACTS) + 3,)),
            pltpu.SemaphoreType.DMA((len(pieces),)),
            pltpu.SemaphoreType.DMA((copies,)),
            pltpu.SemaphoreType.DMA((copies,)),
            pltpu.SemaphoreType.DMA((count - 1,)),
            pltpu.SemaphoreType.DMA((count - 1,)),
            pltpu.SemaphoreType.DMA((2 * (count - 1),)),
            pltpu.SemaphoreType.DMA((2 * (count - 1),)),
        ],
        compiler_params=pltpu.CompilerParams(
            collective_id=0, has_side_effects=True, vmem_limit_bytes=67043328
        ),
        name="forward",
    )(*wide, deep, tile, source, live, allowed, buckets, hidden, encoder, cotangent)
    whole, whole_deep, gains, dy, result, pre = results[:6]
    acts = dict(zip(ACTS, results[6:]))
    acts.update(
        dy=dy.reshape(rows, D),
        result=result.reshape(micro, length, D),
        pre=pre,
        x=hidden,
        enc=encoder,
    )
    return whole.reshape(-1, width), whole_deep.reshape(-1, D), gains, acts


def fused(
    depth,
    hidden,
    encoder,
    cotangent,
    segments,
    buckets,
    live,
    dealing,
    small,
    wide,
    feed_down,
):
    micro, _, length, _ = hidden.shape
    enc_count = encoder.shape[2]
    count = 8 * depth
    slots = jnp.arange(count, dtype=jnp.int32)
    inverse = jnp.sum(
        jnp.where(dealing[:, None, :] == slots[:, None], slots, 0), axis=2, dtype=jnp.int32
    )
    positions = jnp.arange(length, dtype=jnp.int32)
    allowed = (positions[None, :] <= positions[:, None])[None] & (
        segments[:, :, None] == segments[:, None, :]
    )
    turned = jnp.concatenate([buckets[:, :1], buckets[:, :0:-1]], axis=1)
    live_rows = jnp.arange(enc_count, dtype=jnp.int32)[None, None, :] < live[:, None, None]
    live_rows = jnp.broadcast_to(live_rows, (micro, 8, enc_count)).astype(f32)
    whole, down, gains, acts = forward_all(
        wide,
        feed_down,
        small,
        inverse,
        live_rows,
        allowed.astype(f32),
        jnp.broadcast_to(turned[:, None], (micro, 8, length)),
        hidden.reshape(micro * length, D),
        encoder.reshape(micro * enc_count, D),
        cotangent.reshape(micro, length, D),
        depth,
    )
    flipped = jnp.broadcast_to(buckets[:, ::-1, None], (micro, length, 128))
    sums, piece_down, layer_out, grad_in, grad_enc, small_sum = backward_all(
        whole, down, dealing, live_rows, flipped, gains, acts, depth
    )
    small_sum = small_sum[0]
    tall, tall_deep = wide[0].shape[0], feed_down.shape[0]
    sums = sums.reshape(-1, tall, 128)
    piece_down = piece_down.reshape(-1, tall_deep, 128)

    def unpack(tiles):
        return tiles.transpose(1, 0, 2).reshape(tiles.shape[1], -1)

    grads, start = [], 0
    for part in wide:
        tiles = part.shape[1] // 128
        grads.append(unpack(sums[start : start + tiles]))
        start += tiles
    part = D // count
    return (
        layer_out.reshape(hidden.shape),
        grad_in.reshape(hidden.shape),
        grad_enc.reshape(encoder.shape),
        small_sum[:part],
        small_sum[part : 2 * part],
        small_sum[2 * part : 3 * part],
        small_sum[3 * part : 3 * part + H * NB // count],
        *[grads[k] for k in (2, 3, 4, 5, 6, 0, 1, 7, 8, 9)],
        unpack(piece_down),
    )


def body(
    hidden,
    encoder,
    cotangent,
    segment_ids,
    rel_buckets,
    enc_rows,
    dealing,
    gain_self,
    gain_cross,
    gain_ffn,
    rel_bias,
    self_query,
    self_key,
    self_value,
    self_out,
    cross_query,
    cross_key,
    cross_value,
    cross_out,
    feed_gate,
    feed_up,
    feed_down,
):
    device = lax.axis_index(AXIS)
    micro, own, length, _ = hidden.shape
    enc_count = encoder.shape[2]
    blocks = micro * own
    first = device * own

    def mine(table):
        return lax.dynamic_slice_in_dim(table, first, own, axis=1).reshape(
            (blocks,) + table.shape[2:]
        )

    segments, buckets, live = mine(segment_ids), mine(rel_buckets), mine(enc_rows)
    small = jnp.concatenate([gain_self, gain_cross, gain_ffn, rel_bias])
    wide = (
        cross_key,
        cross_value,
        self_query,
        self_key,
        self_value,
        self_out,
        cross_query,
        cross_out,
        feed_gate,
        feed_up,
    )
    depth = kernel_depth(lax.axis_size(AXIS), self_query, feed_down) if own == 1 else 0
    if depth:
        return fused(
            depth,
            hidden,
            encoder,
            cotangent,
            segments,
            buckets,
            live,
            dealing,
            small,
            wide,
            feed_down,
        )
    grad_out = redeal(cotangent, jnp.argsort(dealing, axis=1)).reshape(blocks * length, D)

    smalls = lax.all_gather(small, AXIS, axis=0)
    part = gain_self.shape[0]
    gain_one, gain_two, gain_three = [
        smalls[:, k * part : (k + 1) * part].reshape(D).astype(f32) for k in range(3)
    ]
    bias_table = smalls[:, 3 * part :].reshape(H, NB).astype(f32)
    (wq, wk, wv, wo, xq, xk, xv, xo, gate, up), down = gather_weights(
        (
            self_query,
            self_key,
            self_value,
            self_out,
            cross_query,
            cross_key,
            cross_value,
            cross_out,
            feed_gate,
            feed_up,
        ),
        feed_down,
    )

    positions = jnp.arange(length, dtype=jnp.int32)
    allowed = (positions[None, :] <= positions[:, None])[None] & (
        segments[:, :, None] == segments[:, None, :]
    )
    cross_allowed = jnp.broadcast_to(
        jnp.arange(enc_count, dtype=jnp.int32)[None, None, :] < live[:, None, None],
        (blocks, length, enc_count),
    )
    onehot = (buckets[:, :, None] == jnp.arange(NB, dtype=jnp.int32)).astype(f32)
    per_offset = jnp.einsum("hc,boc->bho", bias_table, onehot, precision=highest)
    bias_grid = toeplitz_expand(per_offset.reshape(blocks * H, length)).reshape(
        blocks, H, length, length
    )

    wide_in = hidden.reshape(blocks * length, D).astype(f32)
    enc_in = encoder.reshape(blocks * enc_count, D)
    inv_one = inverse_rms(wide_in)
    normed_one = (wide_in * inv_one * gain_one).astype(bf16)
    queries = product(normed_one, wq).astype(bf16)
    keys_self = product(normed_one, wk).astype(bf16)
    values_self = product(normed_one, wv).astype(bf16)
    mixed_self, probs_self = attend(queries, keys_self, values_self, bias_grid, allowed)
    first_sum = wide_in + product(mixed_self, wo)
    inv_two = inverse_rms(first_sum)
    normed_two = (first_sum * inv_two * gain_two).astype(bf16)
    cross_queries = product(normed_two, xq).astype(bf16)
    cross_keys = product(enc_in, xk).astype(bf16)
    cross_values = product(enc_in, xv).astype(bf16)
    mixed_cross, probs_cross = attend(
        cross_queries, cross_keys, cross_values, None, cross_allowed
    )
    second_sum = first_sum + product(mixed_cross, xo)
    inv_three = inverse_rms(second_sum)
    normed_three = (second_sum * inv_three * gain_three).astype(bf16)
    gate_pre = product(normed_three, gate)
    up_pre = product(normed_three, up)
    act, slope = gelu_parts(gate_pre)
    hidden_units = (act * up_pre).astype(bf16)
    result = (second_sum + product(hidden_units, down)).astype(bf16)
    layer_out = redeal(result.reshape(micro, own, length, D), dealing)

    g_down = product_left(hidden_units, grad_out)
    grad_units = product_right(grad_out, down)
    grad_gate = (grad_units * up_pre * slope).astype(bf16)
    grad_up = (grad_units * act).astype(bf16)
    g_gate = product_left(normed_three, grad_gate)
    g_up = product_left(normed_three, grad_up)
    grad_three = product_right(grad_gate, gate) + product_right(grad_up, up)
    back, g_gain_three = norm_back(second_sum, inv_three, gain_three, grad_three)
    grad_second = grad_out.astype(f32) + back
    grad_low = grad_second.astype(bf16)
    g_xo = product_left(mixed_cross, grad_low)
    grad_mixed = product_right(grad_low, xo).astype(bf16)
    grad_cq, grad_ck, grad_cv, _ = attend_back(
        cross_queries, cross_keys, cross_values, probs_cross, grad_mixed
    )
    g_xq = product_left(normed_two, grad_cq)
    g_xk = product_left(enc_in, grad_ck)
    g_xv = product_left(enc_in, grad_cv)
    grad_enc = product_right(grad_ck, xk) + product_right(grad_cv, xv)
    back, g_gain_two = norm_back(first_sum, inv_two, gain_two, product_right(grad_cq, xq))
    grad_first = grad_second + back
    grad_low = grad_first.astype(bf16)
    g_so = product_left(mixed_self, grad_low)
    grad_mixed = product_right(grad_low, wo).astype(bf16)
    grad_sq, grad_sk, grad_sv, grad_scores = attend_back(
        queries, keys_self, values_self, probs_self, grad_mixed
    )
    offsets = toeplitz_fold(
        grad_scores.astype(f32).reshape(blocks * H, length, length)
    ).reshape(blocks, H, length)
    g_bias = jnp.einsum("bho,boc->hc", offsets, onehot, precision=highest).reshape(H * NB)
    g_sq = product_left(normed_one, grad_sq)
    g_sk = product_left(normed_one, grad_sk)
    g_sv = product_left(normed_one, grad_sv)
    grad_one = (
        product_right(grad_sq, wq) + product_right(grad_sk, wk) + product_right(grad_sv, wv)
    )
    back, g_gain_one = norm_back(wide_in, inv_one, gain_one, grad_one)
    grad_in = grad_first + back

    pieces, piece_down = scatter_grads(
        (g_sq, g_sk, g_sv, g_so, g_xq, g_xk, g_xv, g_xo, g_gate, g_up), g_down
    )
    count = smalls.shape[0]
    small_grads = jnp.concatenate(
        [g.reshape(count, -1) for g in (g_gain_one, g_gain_two, g_gain_three, g_bias)], axis=1
    )
    small_sum = jnp.sum(
        lax.all_to_all(small_grads, AXIS, split_axis=0, concat_axis=0, tiled=True), axis=0
    )
    return (
        layer_out,
        grad_in.reshape(hidden.shape),
        grad_enc.reshape(encoder.shape),
        small_sum[:part],
        small_sum[part : 2 * part],
        small_sum[2 * part : 3 * part],
        small_sum[3 * part :],
        *pieces,
        piece_down,
    )


def solution(mesh):
    block = P(None, AXIS, None, None)
    row = P(AXIS)
    matrix = P(AXIS, None)
    return jax.shard_map(
        body,
        mesh=mesh,
        in_specs=(block,) * 3 + (P(),) * 4 + (row,) * 4 + (matrix,) * 11,
        out_specs=(block,) * 3 + (row,) * 4 + (matrix,) * 11,
        check_vma=False,
    )
```

```python
import functools

import jax
import jax.numpy as jnp
from jax import lax
from jax.experimental import pallas as pl
from jax.experimental.pallas import tpu as pltpu
from jax.sharding import PartitionSpec as P

D = 1024
H = 16
DH = 64
NB = 32

AXIS = "fsdp"
eps_norm = 1e-06
masked_score = -1000000000.0
highest = lax.Precision.HIGHEST
f32 = jnp.float32
bf16 = jnp.bfloat16


def product(left_side, right_side):
    return jnp.dot(left_side, right_side, preferred_element_type=f32)


def product_left(left_side, right_side):
    return lax.dot_general(
        left_side, right_side, (((0,), (0,)), ((), ())), preferred_element_type=f32
    )


def product_right(left_side, right_side):
    return lax.dot_general(
        left_side, right_side, (((1,), (1,)), ((), ())), preferred_element_type=f32
    )


def inverse_rms(values):
    return lax.rsqrt(jnp.mean(values * values, axis=-1, keepdims=True) + eps_norm)


def norm_back(values, inverse, gain_row, grad):
    scaled = values * inverse
    weighted = grad * gain_row
    centre = jnp.mean(weighted * scaled, axis=-1, keepdims=True)
    return inverse * (weighted - scaled * centre), jnp.sum(grad * scaled, axis=0)


def gelu_parts(gate_pre):
    root = 0.7978845608028654
    inner = root * (gate_pre + 0.044715 * gate_pre * gate_pre * gate_pre)
    curve = jnp.tanh(inner)
    value = 0.5 * gate_pre * (1.0 + curve)
    slope = 0.5 * (1.0 + curve) + 0.5 * gate_pre * (1.0 - curve * curve) * root * (
        1.0 + 3 * 0.044715 * gate_pre * gate_pre
    )
    return value, slope


def toeplitz_expand(per_offset):
    head_count, length = per_offset.shape
    filler = jnp.zeros((head_count, 1), f32)
    pattern = jnp.concatenate(
        [per_offset[:, :1], filler, per_offset[:, ::-1][:, : length - 1]], axis=1
    )
    tiled_rows = jnp.broadcast_to(pattern[:, None, :], (head_count, length, length + 1))
    return tiled_rows.reshape(head_count, length * (length + 1))[:, : length * length].reshape(
        head_count, length, length
    )


def toeplitz_fold(score_grid):
    head_count, length = (score_grid.shape[0], score_grid.shape[1])
    flat_grid = score_grid.reshape(head_count, length * length)
    padded = jnp.concatenate([flat_grid, jnp.zeros((head_count, length), f32)], axis=1)
    columns = jnp.sum(padded.reshape(head_count, length, length + 1), axis=1)
    return jnp.concatenate([columns[:, :1], columns[:, 2:][:, ::-1]], axis=1)


def heads(matrix, blocks):
    return matrix.reshape(blocks, -1, H, DH)


def score_block(queries, keys_in, bias_grid, allowed):
    scores = jnp.einsum("bihd,bjhd->bhij", queries, keys_in, preferred_element_type=f32)
    if bias_grid is not None:
        scores = scores + bias_grid
    return jnp.where(allowed[:, None], scores, masked_score)


def attend(queries, keys_in, values, bias_grid, allowed):
    blocks = allowed.shape[0]
    scores = score_block(heads(queries, blocks), heads(keys_in, blocks), bias_grid, allowed)
    largest = jnp.max(scores, axis=3, keepdims=True)
    weights = jnp.exp(scores - largest)
    probs = weights / jnp.sum(weights, axis=3, keepdims=True)
    mixed = jnp.einsum(
        "bhij,bjhd->bihd", probs.astype(bf16), heads(values, blocks), preferred_element_type=f32
    )
    return mixed.reshape(queries.shape[0], D).astype(bf16), probs


def attend_back(queries, keys_in, values, probs, grad_mixed):
    blocks = probs.shape[0]
    grad_heads = heads(grad_mixed, blocks)
    grad_values = jnp.einsum(
        "bhij,bihd->bjhd", probs.astype(bf16), grad_heads, preferred_element_type=f32
    )
    grad_probs = jnp.einsum(
        "bihd,bjhd->bhij", grad_heads, heads(values, blocks), preferred_element_type=f32
    )
    grad_scores = (
        probs * (grad_probs - jnp.sum(probs * grad_probs, axis=3, keepdims=True))
    ).astype(bf16)
    grad_queries = jnp.einsum(
        "bhij,bjhd->bihd", grad_scores, heads(keys_in, blocks), preferred_element_type=f32
    )
    grad_keys = jnp.einsum(
        "bhij,bihd->bjhd", grad_scores, heads(queries, blocks), preferred_element_type=f32
    )
    return (
        grad_queries.reshape(-1, D).astype(bf16),
        grad_keys.reshape(-1, D).astype(bf16),
        grad_values.reshape(-1, D).astype(bf16),
        grad_scores,
    )


def redeal(blocks, source):
    micro, own, rows, width = blocks.shape
    count = source.shape[1] // own
    cut = blocks.reshape(micro, own, count, rows // count, width).transpose(2, 0, 1, 3, 4)
    spread = lax.all_to_all(cut, AXIS, split_axis=0, concat_axis=0, tiled=True)
    spread = spread.transpose(1, 0, 2, 3, 4).reshape(micro, count * own, rows // count, width)
    moved = jnp.take_along_axis(spread, source[:, :, None, None], axis=1)
    moved = moved.reshape(micro, count, own, rows // count, width).transpose(1, 0, 2, 3, 4)
    home = lax.all_to_all(moved, AXIS, split_axis=0, concat_axis=0, tiled=True)
    return home.transpose(1, 2, 0, 3, 4).reshape(micro, own, rows, width)


def gather_weights(wide, deep):
    packed = lax.all_gather(jnp.concatenate(wide, axis=1), AXIS, axis=0, tiled=True)
    whole, start = [], 0
    for part in wide:
        whole.append(packed[:, start : start + part.shape[1]])
        start += part.shape[1]
    return whole, lax.all_gather(deep, AXIS, axis=0, tiled=True)


def scatter_grads(wide, deep):
    packed = jnp.concatenate([part.astype(bf16) for part in wide], axis=1)
    packed = lax.psum_scatter(packed, AXIS, scatter_dimension=0, tiled=True).astype(f32)
    pieces, start = [], 0
    for part in wide:
        pieces.append(packed[:, start : start + part.shape[1]])
        start += part.shape[1]
    deep = lax.psum_scatter(deep.astype(bf16), AXIS, scatter_dimension=0, tiled=True)
    return pieces, deep.astype(f32)


MESH = pl.DeviceIdType.MESH


def late_in_z(count):
    return set(range(count - 5, count - 2))


RING = 3
SLOTS = 7
DRAIN = (1,) * 5
GATHER_LAGS = (0, 2, 4, 5)
SCATTER_LAGS = (0, 1, 2, 2, 1)


class Place:
    def __init__(self, depth):
        self.depth = depth
        self.count = depth * 8
        self.me = lax.axis_index(AXIS)
        self.core = self.me % 2
        self.x = (self.me // 2) % 2
        self.y = (self.me // 4) % 2
        self.z = self.me // 8
        self.twin = self.me + 1 - 2 * self.core
        self.over_x = self.me + 2 - 4 * self.x
        self.over_y = self.me + 4 - 8 * self.y
        self.far = [(self.z + d) % depth for d in range(1, depth)]
        self.over_z = [self.me + (z - self.z) * 8 for z in self.far]

    def greet(self):
        barrier = pltpu.get_barrier_semaphore()

        def hello(d, _):
            peer = (self.me + d) % self.count
            pl.semaphore_signal(barrier, inc=1, device_id=(peer,), device_id_type=MESH)
            return 0

        lax.fori_loop(1, self.count, hello, 0)
        pl.semaphore_wait(barrier, self.count - 1)


def remote(source, target, send, recv, index, device):
    return pltpu.make_async_remote_copy(
        src_ref=source,
        dst_ref=target,
        send_sem=send.at[index],
        recv_sem=recv.at[index],
        device_id=(device,),
        device_id_type=MESH,
    )


def columns(start, width):
    return pl.ds(pl.multiple_of(start, 128), width)


class Gather:
    def __init__(self, place, pieces, staged, wholes, local, send, recv):
        self.place, self.pieces = place, pieces
        self.staged, self.wholes = staged, wholes
        self.local, self.send, self.recv = local, send, recv
        self.steps = 1 + 2 * (place.depth + 2)
        self.sent = []
        self.plane_first = late_in_z(len(pieces))

    def begin(self, copy):
        copy.start()
        self.sent.append(copy)

    def rows(self, kind):
        height = self.staged[kind].shape[0]
        p = self.place
        return self.wholes[kind].at[p.z, p.y, p.x, pl.ds(p.core * height, height)]

    def quarter(self, i, core, order):
        kind, start, width = self.pieces[i]
        return columns(start + core * (width // 2) + order * (width // 4), width // 4)

    def copy(self, source, target, i, step, device):
        return remote(source, target, self.send, self.recv, i * self.steps + step, device)

    def to_twin(self, i):
        kind, start, width = self.pieces[i]
        cols = columns(start + (1 - self.place.core) * (width // 2), width // 2)
        return self.copy(
            self.staged[kind].at[:, cols], self.rows(kind).at[:, cols], i, 0, self.place.twin
        )

    def own(self, i):
        kind, start, width = self.pieces[i]
        cols = columns(start + self.place.core * (width // 2), width // 2)
        return pltpu.make_async_copy(
            self.staged[kind].at[:, cols], self.rows(kind).at[:, cols], self.local.at[i]
        )

    def along_z(self, i, order, d):
        p = self.place
        whole, cols = self.wholes[self.pieces[i][0]], self.quarter(i, p.core, order)
        if i in self.plane_first:
            ref = whole.at[p.z, :, :, :, cols]
        else:
            ref = whole.at[p.z, p.y, p.x, :, cols]
        return self.copy(ref, ref, i, 1 + order * (p.depth + 2) + d, p.over_z[d])

    def plane(self, i, order, second):
        p = self.place
        whole = self.wholes[self.pieces[i][0]]
        cols = self.quarter(i, p.core, order)
        layers = p.z if i in self.plane_first else slice(None)
        if second:
            ref = whole.at[layers, :, p.x, :, cols] if order else whole.at[layers, p.y, :, :, cols]
        else:
            ref = whole.at[layers, p.y, p.x, :, cols]
        device = p.over_x if order == second else p.over_y
        return self.copy(ref, ref, i, 1 + order * (p.depth + 2) + p.depth - 1 + second, device)

    def across(self, i, order):
        p = self.place
        whole = self.wholes[self.pieces[i][0]]
        ref = whole.at[:, :, :, :, self.quarter(i, p.core, order)]
        return self.copy(ref, ref, i, 1 + order * (p.depth + 2) + p.depth + 1, p.twin)

    def open(self):
        for i in range(len(self.pieces)):
            self.begin(self.to_twin(i))
        for i in range(len(self.pieces)):
            self.own(i).start()
        for i in range(len(self.pieces)):
            self.own(i).wait()
        for i in sorted(self.plane_first):
            self.to_twin(i).wait_recv()
            for order in (0, 1):
                self.begin(self.plane(i, order, 0))
        for i in range(len(self.pieces)):
            if i not in self.plane_first:
                self.to_twin(i).wait_recv()
                self.all_z(i)

    def all_z(self, i):
        for d in range(self.place.depth - 1):
            for order in (0, 1):
                self.begin(self.along_z(i, order, d))

    def early(self, t):
        for i in sorted(self.plane_first):
            for order in (0, 1):
                if t == 1:
                    self.plane(i, order, 0).wait_recv()
                    self.begin(self.plane(i, order, 1))
                elif t == 3:
                    self.plane(i, order, 1).wait_recv()
            if t == 3:
                self.all_z(i)

    def advance(self, i, stage):
        if not 0 <= i < len(self.pieces):
            return
        late = i in self.plane_first
        for order in (0, 1):
            if late and stage < 2:
                continue
            if stage == 0 or late and stage == 2:
                for d in range(self.place.depth - 1):
                    self.along_z(i, order, d).wait_recv()
            if stage == 0:
                self.begin(self.plane(i, order, 0))
            elif stage == 1:
                self.plane(i, order, 0).wait_recv()
                self.begin(self.plane(i, order, 1))
            elif stage == 2:
                if not late:
                    self.plane(i, order, 1).wait_recv()
                self.begin(self.across(i, order))
            else:
                self.across(i, order).wait_recv()

    def turn(self, t):
        self.early(t)
        for stage in (3, 2, 1, 0):
            self.advance(t - GATHER_LAGS[stage], stage)

    def close(self):
        for copy in self.sent:
            copy.wait_send()


class Scatter:
    def __init__(self, place, pieces, blocks, outs, scratch):
        self.place, self.pieces, self.blocks, self.outs = place, pieces, blocks, outs
        self.grads, self.got, self.final, (self.local, self.send, self.recv) = (
            scratch[0],
            scratch[1:5],
            scratch[5],
            scratch[6:9],
        )
        self.steps = 1 + 2 * (place.depth + 2)
        self.done = [0] * 5

    @staticmethod
    def scratch(pieces, depth, blocks):
        tall = max(blocks[kind] * (width // 512) for kind, _, width in pieces)
        copies = len(pieces) * (1 + 2 * (depth + 2))
        return [
            pltpu.VMEM((SLOTS, 2, 2, depth, 2, 2, tall, 128), bf16),
            pltpu.VMEM((RING, 2, depth, 2, 2, tall, 128), bf16),
            pltpu.VMEM((2 * SCATTER_LAGS[2], 2, depth, 2, tall, 128), bf16),
            pltpu.VMEM((2 * SCATTER_LAGS[3], 2, depth, tall, 128), bf16),
            pltpu.VMEM((RING, 2, depth - 1, tall, 128), bf16),
            pltpu.VMEM((RING, 2, 2, tall // 2, 128), f32),
            pltpu.SemaphoreType.DMA((2 * len(pieces),)),
            pltpu.SemaphoreType.DMA((copies,)),
            pltpu.SemaphoreType.DMA((copies,)),
        ]

    def size(self, i):
        kind, start, width = self.pieces[i]
        return kind, start // 128, width // 512, self.blocks[kind]

    def rows(self, i):
        _, _, tiles, block = self.size(i)
        return pl.ds(0, tiles * block)

    def cut(self, ref, i):
        return ref.at[(slice(None),) * (len(ref.shape) - 2) + (self.rows(i),)]

    def mine(self, i, half, *quarter):
        return self.cut(self.grads.at[(i % SLOTS, half) + quarter], i)

    def theirs(self, level, i, *index):
        return self.cut(self.got[level].at[(i % self.got[level].shape[0],) + index], i)

    def copy(self, source, target, i, step, device):
        return remote(source, target, self.send, self.recv, i * self.steps + step, device)

    def to_twin(self, i):
        return self.copy(
            self.mine(i, 1 - self.place.core), self.theirs(0, i), i, 0, self.place.twin
        )

    def plane(self, i, order, second):
        p = self.place
        ref = self.mine(i, p.core, order)
        if second:
            ref = ref.at[:, p.y, 1 - p.x] if order else ref.at[:, 1 - p.y, p.x]
        else:
            ref = ref.at[:, 1 - p.y] if order else ref.at[:, :, 1 - p.x]
        device = p.over_x if order == second else p.over_y
        step = 1 + order * (p.depth + 2) + second
        return self.copy(ref, self.theirs(1 + second, i, order), i, step, device)

    def along_z(self, i, order, d):
        p = self.place
        ref = self.mine(i, p.core, order).at[p.far[d], p.y, p.x]
        step = 1 + order * (p.depth + 2) + 2 + d
        return self.copy(ref, self.theirs(3, i, order, d), i, step, p.over_z[d])

    def ends(self, i, order, core):
        kind, first, tiles, block = self.size(i)
        count = tiles * block // 2
        row = (first + (2 * self.place.core + order) * tiles) * (block // 2)
        source = self.final.at[i % RING, order, core, pl.ds(0, count)]
        return source, self.outs[kind].at[pl.ds(pl.multiple_of(row, 8), count)]

    def rest(self, i, order):
        p = self.place
        source, target = self.ends(i, order, 1 - p.core)
        return self.copy(source, target, i, 1 + order * (p.depth + 2) + p.depth + 1, p.twin)

    def keep(self, i, order):
        source, target = self.ends(i, order, self.place.core)
        return pltpu.make_async_copy(source, target, self.local.at[2 * i + order])

    def add(self, i, order, level, spots):
        rows = self.rows(i)
        slot, ring, core = i % SLOTS, i % self.got[level].shape[0], self.place.core

        def layer(z, _):
            for there, here in spots:
                at = (slot, core, order, z) + here + (rows,)
                total = self.grads[at].astype(f32)
                total = total + self.got[level][(ring, order, z) + there + (rows,)].astype(f32)
                self.grads[at] = total.astype(bf16)
            return 0

        lax.fori_loop(0, self.place.depth, layer, 0)

    def advance(self, i, stage):
        if not 0 <= i < len(self.pieces):
            return
        p = self.place
        if stage == 1:
            self.to_twin(i).wait_recv()
            for order in (0, 1):
                self.add(i, order, 0, [((y, x), (y, x)) for y in (0, 1) for x in (0, 1)])
                self.plane(i, order, 0).start()
        elif stage == 2:
            for order in (0, 1):
                self.plane(i, order, 0).wait_recv()
                self.add(
                    i, order, 1, [((k,), (p.y, k) if order else (k, p.x)) for k in (0, 1)]
                )
                self.plane(i, order, 1).start()
        elif stage == 3:
            for order in (0, 1):
                self.plane(i, order, 1).wait_recv()
                self.add(i, order, 2, [((), (p.y, p.x))])
                for d in range(p.depth - 1):
                    self.along_z(i, order, d).start()
        elif stage == 4:
            if i >= RING:
                self.settle(i - RING)
            _, _, tiles, block = self.size(i)
            rows, half = self.rows(i), block // 2
            for order in (0, 1):
                for d in range(p.depth - 1):
                    self.along_z(i, order, d).wait_recv()
                total = self.grads[i % SLOTS, p.core, order, p.z, p.y, p.x, rows].astype(f32)
                for d in range(p.depth - 1):
                    total = total + self.got[3][i % RING, order, d, rows].astype(f32)
                for tile in range(tiles):
                    for core in (0, 1):
                        row = tile * block + core * half
                        self.final[i % RING, order, core, pl.ds(tile * half, half)] = total[
                            row : row + half
                        ]
                self.rest(i, order).start()
                self.keep(i, order).start()
            self.to_twin(i).wait_send()
            for order in (0, 1):
                self.plane(i, order, 0).wait_send()
                self.plane(i, order, 1).wait_send()
                for d in range(p.depth - 1):
                    self.along_z(i, order, d).wait_send()

    def settle(self, i):
        for order in (0, 1):
            self.rest(i, order).wait()
            self.keep(i, order).wait()

    def pump(self, lags=SCATTER_LAGS):
        for stage in (4, 3, 2, 1):
            if self.done[stage] + lags[stage] <= self.done[stage - 1]:
                self.advance(self.done[stage], stage)
                self.done[stage] += 1

    def produce(self, left, right, column):
        i = self.done[0]
        self.pump()
        while self.done[4] <= i - SLOTS:
            self.pump()
        self.done[0] += 1
        _, _, tiles, block = self.size(i)
        slot = i % SLOTS
        group = 1 if block % 32 == 0 else 2
        turns = self.place.depth // group
        high = 4 * block * group

        def chunk(k, _):
            n, first = k // turns, (k % turns) * group
            part = transposed(
                left[:, columns(k % turns * high, high)], right[:, columns(column + 256 * n, 256)]
            ).astype(bf16)
            for tile in (0, 1):
                for b in range(4 * group):
                    spot = first + b // 4, b // 2 % 2, b % 2
                    piece = part[b * block : b * block + block, tile * 128 : tile * 128 + 128]
                    if tiles == 2:
                        at = (slot, n // 2, n % 2) + spot + (pl.ds(tile * block, block),)
                    else:
                        at = (slot, n, tile) + spot + (pl.ds(0, block),)
                    self.grads[at] = piece
            return 0

        lax.fori_loop(0, 2 * tiles * turns, chunk, 0)
        self.to_twin(i).start()

    def close(self):
        while self.done[4] < len(self.pieces):
            self.pump(DRAIN)
        for i in range(max(0, len(self.pieces) - RING), len(self.pieces)):
            self.settle(i)


class Redeal:
    def __init__(self, place, given, spread, moved, wanted, send, recv):
        self.place, self.given, self.spread, self.moved = place, given, spread, moved
        self.wanted, self.send, self.recv = wanted, send, recv
        self.high, self.wide = spread.shape[2:]

    def spot(self, ref, j):
        depth = self.place.depth
        rows = pl.ds(pl.multiple_of((j // depth) * self.high, self.high), self.high)
        return ref.at[:, rows, columns((j % depth) * self.wide, self.wide)]

    def peer(self, d):
        return (self.place.me + d) % self.place.count

    def out(self, d):
        target = self.spread.at[self.place.me]
        peer = self.peer(d)
        return remote(self.spot(self.given, peer), target, self.send, self.recv, d - 1, peer)

    def home(self, d):
        peer, count = self.peer(d), self.place.count
        target = self.spot(self.wanted, self.place.me)
        return remote(
            self.moved.at[peer], target, self.send, self.recv, count - 1 + d - 1, peer
        )

    def each(self, act):
        def one(d, _):
            act(d)
            return 0

        lax.fori_loop(1, self.place.count, one, 0)

    def own(self, ref):
        j = self.place.me
        depth = self.place.depth
        rows = pl.ds(pl.multiple_of((j // depth) * self.high, self.high), self.high)
        return slice(None), rows, columns((j % depth) * self.wide, self.wide)

    def begin(self):
        self.each(lambda d: self.out(d).start())
        self.spread[self.place.me] = self.given[self.own(self.given)]

    def middle(self, source):
        self.each(lambda d: self.out(d).wait())

        def one(j, _):
            for m in range(self.moved.shape[1]):
                self.moved[j, m] = self.spread[source[m, j], m]
            return 0

        lax.fori_loop(0, self.place.count, one, 0)
        self.each(lambda d: self.home(d).start())
        self.wanted[self.own(self.wanted)] = self.moved[self.place.me]

    def end(self):
        self.each(lambda d: self.home(d).wait())


def spread_small(place, tile, table, send, recv):
    table[place.me] = tile[...]

    def out(d, _):
        remote(
            tile, table.at[place.me], send, recv, d - 1, (place.me + d) % place.count
        ).start()
        return 0

    lax.fori_loop(1, place.count, out, 0)


def collect_small(place, tile, table, send, recv):
    def back(d, _):
        copy = remote(
            tile,
            table.at[(place.me + place.count - d) % place.count],
            send,
            recv,
            d - 1,
            (place.me + d) % place.count,
        )
        copy.wait()
        return 0

    lax.fori_loop(1, place.count, back, 0)


def cut_columns(widths, start=0):
    pieces = []
    for width in widths:
        pieces.append((0, start, width))
        start += width
    return pieces


def kernel_depth(count, wide, deep):
    fits = count % 8 == 0 and wide.shape[0] % 8 == 0 and deep.shape[0] % 8 == 0
    return count // 8 if fits else 0


def transposed(left, right):
    return lax.dot_general(
        left, right, (((0,), (0,)), ((), ())), preferred_element_type=f32
    )


def against(left, right):
    return lax.dot_general(
        left, right, (((1,), (1,)), ((), ())), preferred_element_type=f32
    )


class Stream:
    def __init__(self, refs, tiles, slots, sems):
        self.refs, self.tiles, self.slots, self.sems = refs, tiles, slots, sems
        self.next, self.begun = 0, 0

    def copy(self, k):
        kind, start, size = self.tiles[k]
        slot = k % self.slots.shape[0]
        cut = pl.ds(0, size)
        if kind:
            source, target = self.refs[1].at[pl.ds(start, size)], self.slots.at[slot, cut]
        else:
            source, target = self.refs[0].at[:, pl.ds(start, size)], self.slots.at[slot, :, cut]
        return pltpu.make_async_copy(source, target, self.sems.at[slot])

    def take(self):
        ahead = min(len(self.tiles), self.next + self.slots.shape[0])
        while self.begun < ahead:
            self.copy(self.begun).start()
            self.begun += 1
        k = self.next
        self.copy(k).wait()
        self.next += 1
        return self.slots.at[k % self.slots.shape[0]]


def back_into(total, left, start, size, tile, fresh):
    def chunk(n, _):
        cols = columns(n * 256, 256)
        part = against(left[:, start : start + size], tile[cols, 0:size])
        rows = pl.ds(0, left.shape[0])
        total[rows, cols] = part if fresh else total[rows, cols] + part
        return 0

    lax.fori_loop(0, D // 256, chunk, 0)


def back_rounded(out, left, tile):
    def chunk(n, _):
        cols = columns(n * 256, 256)
        out[:, cols] = against(left[...], tile[cols, :]).astype(bf16)
        return 0

    lax.fori_loop(0, D // 256, chunk, 0)


def self_scores(bias, scores, block, head):
    marked = bias[block, head].astype(f32)
    return jnp.where(marked < -1e29, masked_score, scores + marked)


def cross_scores(live, scores, block, head):
    return jnp.where(live[block, 0:1, :] > 0.0, scores, masked_score)


def pair_loop(first, last, body_of):
    def one(index, _):
        body_of(index // (H // 2), index % (H // 2))
        return 0

    lax.fori_loop(first, last, one, 0)


def softmax_rows(scores):
    weights = jnp.exp(scores - jnp.max(scores, axis=1, keepdims=True))
    return weights / jnp.sum(weights, axis=1, keepdims=True)


def attend_back_pairs(refs, grads, marks, mask, folded, first, last):
    q, k, v, da = refs
    dq, dk, dv = grads
    rows_q = 128
    tall = k.shape[0] // (q.shape[0] // rows_q)
    even = lax.broadcasted_iota(jnp.int32, (1, 128), 1) < DH
    down, right = [lax.broadcasted_iota(jnp.int32, (rows_q, rows_q), k) for k in (0, 1)]
    mirror = jnp.where(down + right == rows_q - 1, 1.0, 0.0).astype(bf16)

    def pair(block, p):
        rows = pl.ds(pl.multiple_of(block * rows_q, rows_q), rows_q)
        keys = pl.ds(pl.multiple_of(block * tall, tall), tall)
        cols = columns(p * 128, 128)
        q2, k2, v2, da2 = q[rows, cols], k[keys, cols], v[keys, cols], da[rows, cols]
        sums = [None, None, None]
        for e in (0, 1):
            keep = even if e == 0 else jnp.logical_not(even)

            def half(value):
                return jnp.where(keep, value.astype(f32), 0.0).astype(bf16)

            qe, dae, ke = half(q2), half(da2), half(k2)
            head = 2 * p + e
            probs = softmax_rows(mask(marks, against(qe, k2), block, head))
            dp = against(dae, v2)
            centre = jnp.sum(probs * dp, axis=1, keepdims=True)
            ds = (probs * (dp - centre)).astype(bf16)
            terms = (
                jnp.dot(ds, ke, preferred_element_type=f32),
                transposed(ds, qe),
                transposed(probs.astype(bf16), dae),
            )
            sums = [t if s is None else s + t for s, t in zip(sums, terms)]
            if folded is not None:
                upside = jnp.dot(mirror, ds, preferred_element_type=f32)
                turned = pltpu.roll(upside, 0, 1, stride=1, stride_axis=0)
                folded[block * H + head] = jnp.sum(turned, axis=0, keepdims=True)
        dq[rows, cols] = sums[0].astype(bf16)
        dk[keys, cols] = sums[1].astype(bf16)
        dv[keys, cols] = sums[2].astype(bf16)

    pair_loop(first, last, pair)


def norm_back_rows(values, gain_row, grad, base, out, total):
    total[...] = jnp.zeros_like(total)

    def chunk(k, _):
        rows = pl.ds(pl.multiple_of(k * 64, 64), 64)
        v = values[rows, :].astype(f32)
        inverse = inverse_rms(v)
        scaled = v * inverse
        g = grad[rows, :]
        weighted = g * gain_row[...]
        centre = jnp.mean(weighted * scaled, axis=-1, keepdims=True)
        out[rows, :] = base[rows, :].astype(f32) + inverse * (weighted - scaled * centre)
        total[...] += jnp.sum(g * scaled, axis=0, keepdims=True)
        return 0

    lax.fori_loop(0, values.shape[0] // 64, chunk, 0)


def small_tables(gain_sums, folded, buckets, tables, count):
    each, share = D // count, H * NB // count
    split, micro = NB // share, folded.shape[0] // H
    lane = lax.broadcasted_iota(jnp.int32, (D, 128), 1)
    col = lax.broadcasted_iota(jnp.int32, (D, 128), 0)
    device = lax.broadcasted_iota(jnp.int32, (count, D), 0)
    owner = lax.broadcasted_iota(jnp.int32, (count, D), 1) // each
    total = jnp.zeros((count, 128), f32)
    for k in range(3):
        pick = jnp.where(lane == k * each + col % each, 1.0, 0.0)
        mine = jnp.where(device == owner, gain_sums[k], 0.0)
        total = total + jnp.dot(mine, pick, precision=highest, preferred_element_type=f32)
    spot = lax.broadcasted_iota(jnp.int32, (128, 128), 1) - 3 * each
    inside = (spot >= 0) & (spot < share)
    for part in range(split):
        found = jnp.zeros((H, 128), f32)
        for block in range(micro):
            hit = inside & (buckets[block] == spot + part * share)
            rows = jnp.concatenate([folded[block * H + h] for h in range(H)], axis=0)
            found = found + jnp.dot(
                rows, jnp.where(hit, 1.0, 0.0), precision=highest, preferred_element_type=f32
            )
        for h in range(H):
            j = h * split + part
            row = total[j : j + 1] + found[h : h + 1]
            tables[j] = jnp.broadcast_to(row, (8, 128))


def swap_small(place, tables, got, send, recv, act):
    def one(d, _):
        peer = (place.me + d) % place.count
        act(remote(tables.at[peer], got.at[place.me], send, recv, d - 1, peer))
        return 0

    lax.fori_loop(1, place.count, one, 0)


BACK_INPUTS = (
    "result", "dy", "hd", "n3", "r2", "ac", "cq", "ck", "cv", "n2",
    "enc", "r1", "mixed", "q", "k", "v", "n1", "x", "bias", "pre",
)
BACK_ORDER = ("xo", "xq", "o", "xk", "xv", "q", "k", "v")
SCATTER_ORDER = ("xo", "xq", "xk", "xv", "o", "q", "k", "v")


def backward_kernel(pieces, depth, blocks, *refs):
    refs = list(refs)

    def pop(count):
        return [refs.pop(0) for _ in range(count)]

    whole, down, source, live, buckets, gains = pop(6)
    ins = dict(zip(BACK_INPUTS, pop(len(BACK_INPUTS))))
    out, out_deep, layer_out, grad_in, grad_enc, small_out = pop(6)
    held = dict(zip(BACK_INPUTS[:-1], pop(len(BACK_INPUTS) - 1)))
    load_sems, slots, slot_sems, pre, pre_sems, out_sems = pop(6)
    dgu, acc, dr2, dr1, low, dmix, dq, dk, dv, dck, dcv = pop(11)
    spread, moved, wanted, deal_send, deal_recv = pop(5)
    gain_sums, folded, tables, got, small_send, small_recv = pop(6)
    place = Place(depth)
    scatter = Scatter(place, pieces, blocks, (out, out_deep), refs)
    units = held["hd"].shape[1]
    rows = held["dy"].shape[0]

    loads = {
        name: pltpu.make_async_copy(ins[name], held[name], load_sems.at[i])
        for i, name in enumerate(BACK_INPUTS[:-1])
    }
    for load in loads.values():
        load.start()

    def need(*names):
        for name in names:
            loads.pop(name).wait()

    tiles = [(1, start, min(1024, units - start)) for start in range(0, units, 1024)]
    tiles += [(0, 8 * D + k, min(1024, 2 * units - k)) for k in range(0, 2 * units, 1024)]
    tiles += [(0, D * LEFT.index(w), D) for w in BACK_ORDER]
    stream = Stream((whole, down), tiles, slots, slot_sems)

    def ahead(k):
        return [
            pltpu.make_async_copy(
                ins["pre"].at[:, columns(j * units + k * 256, 256)],
                pre.at[k % 2, j],
                pre_sems.at[k % 2, j],
            )
            for j in (0, 1)
        ]

    for load in ahead(0):
        load.start()
    place.greet()
    redeal = Redeal(place, held["result"], spread, moved, wanted, deal_send, deal_recv)
    need("result")
    redeal.begin()

    need("dy", "hd")
    dy = held["dy"]
    scatter.produce(held["hd"], dy, 0)
    scatter.produce(held["hd"], dy, 512)
    for start in range(0, units, 1024):
        tile = stream.take()

        def chunk(n, _):
            k = start // 256 + n

            @pl.when(k + 1 < units // 256)
            def _():
                for load in ahead(k + 1):
                    load.start()

            for load in ahead(k):
                load.wait()
            part = against(dy[...], tile[pl.ds(pl.multiple_of(n * 256, 256), 256), :])
            act, slope = gelu_parts(pre[k % 2, 0])
            dgu[:, columns(k * 256, 256)] = (part * pre[k % 2, 1] * slope).astype(bf16)
            dgu[:, columns(units + k * 256, 256)] = (part * act).astype(bf16)
            return 0

        lax.fori_loop(0, min(1024, units - start) // 256, chunk, 0)
        scatter.pump()
    starts = list(range(0, 2 * units, 1024))
    halves = rows // 128 * (H // 2)
    quarter = halves // 4

    def cross(part):
        attend_back_pairs(
            (held["cq"], held["ck"], held["cv"], dmix),
            (dq, dck, dcv),
            live,
            cross_scores,
            None,
            part * quarter,
            part * quarter + quarter,
        )

    def within(part):
        attend_back_pairs(
            (held["q"], held["k"], held["v"], dmix),
            (dq, dk, dv),
            held["bias"],
            self_scores,
            folded,
            part * quarter,
            part * quarter + quarter,
        )

    def feed():
        start = starts.pop(0)
        scatter.produce(held["n3"], dgu, start)

    need("n3")
    feed()
    for k, start in enumerate(range(0, 2 * units, 1024)):
        back_into(acc, dgu, start, min(1024, 2 * units - start), stream.take(), k == 0)
        if k == 2:
            feed()
    need("r2")
    norm_back_rows(held["r2"], gains.at[2], acc, dy, dr2, gain_sums.at[2])
    low[...] = dr2[...].astype(bf16)
    back_rounded(dmix, low, stream.take())
    feed()
    need("cq", "ck", "cv")
    for part in range(4):
        cross(part)
        if starts:
            feed()
        else:
            scatter.pump()
    while starts:
        feed()
    redeal.middle(source)
    need("ac")
    scatter.produce(held["ac"], low, 0)
    back_into(acc, dq, 0, D, stream.take(), True)
    need("r1")
    norm_back_rows(held["r1"], gains.at[1], acc, dr2, dr1, gain_sums.at[1])
    low[...] = dr1[...].astype(bf16)
    back_rounded(dmix, low, stream.take())
    need("n2", "enc")
    scatter.produce(held["n2"], dq, 0)
    need("q", "k", "v", "bias")
    within(0)
    within(1)
    scatter.produce(held["enc"], dck, 0)
    within(2)
    within(3)
    scatter.produce(held["enc"], dcv, 0)
    back_into(acc, dck, 0, D, stream.take(), True)
    back_into(acc, dcv, 0, D, stream.take(), False)
    enc_out = pltpu.make_async_copy(acc, grad_enc, out_sems.at[0])
    enc_out.start()
    need("mixed")
    scatter.produce(held["mixed"], low, 0)
    need("n1")
    for grad in (dq, dk, dv):
        scatter.produce(held["n1"], grad, 0)
    scatter.produce(held["n1"], dv, 512)
    enc_out.wait()
    for index, grad in enumerate((dq, dk, dv)):
        back_into(acc, grad, 0, D, stream.take(), index == 0)
        scatter.pump(DRAIN)
    need("x")
    norm_back_rows(held["x"], gains.at[0], acc, dr1, dr2, gain_sums.at[0])
    in_out = pltpu.make_async_copy(dr2, grad_in, out_sems.at[1])
    in_out.start()
    scatter.pump(DRAIN)
    small_tables(gain_sums, folded, buckets, tables, place.count)
    swap_small(place, tables, got, small_send, small_recv, lambda copy: copy.start())
    got[place.me] = tables[place.me]
    scatter.pump(DRAIN)
    redeal.end()
    deal_out = pltpu.make_async_copy(wanted, layer_out, out_sems.at[2])
    deal_out.start()
    scatter.close()
    swap_small(place, tables, got, small_send, small_recv, lambda copy: copy.wait())
    small_out[...] = jnp.sum(got[...], axis=0)
    in_out.wait()
    deal_out.wait()


def backward_all(whole, down, source, live, buckets, gains, acts, depth):
    tall, width = whole.shape
    tall_deep = down.shape[0]
    blocks = (tall // (4 * depth), tall_deep // (4 * depth))
    micro, length = acts["result"].shape[:2]
    rows, keys = micro * length, acts["enc"].shape[0]
    units, count = tall_deep, 8 * depth
    pieces = [(1, 0, 512), (1, 512, 512)]
    pieces += [(0, 8 * D + k, min(1024, 2 * units - k)) for k in range(0, 2 * units, 1024)]
    pieces += [(0, D * LEFT.index(w), D) for w in SCATTER_ORDER[:-1]]
    pieces += [(0, D * LEFT.index(SCATTER_ORDER[-1]) + k, 512) for k in (0, 512)]
    anywhere = pl.BlockSpec(memory_space=pl.ANY)
    inside = pl.BlockSpec(memory_space=pltpu.VMEM)
    arrays = [acts[name] for name in BACK_INPUTS]
    spots = (micro, length // 8, D // depth)
    held = [pltpu.VMEM(a.shape, a.dtype) for a in arrays[:-1]]
    square = [pltpu.VMEM((rows, D), f32)] * 2 + [pltpu.VMEM((rows, D), bf16)] * 5
    return pl.pallas_call(
        functools.partial(backward_kernel, pieces, depth, blocks),
        out_shape=(
            jax.ShapeDtypeStruct((width // 128 * (blocks[0] // 2), 128), f32),
            jax.ShapeDtypeStruct((D // 128 * (blocks[1] // 2), 128), f32),
            jax.ShapeDtypeStruct((micro, length, D), bf16),
            jax.ShapeDtypeStruct((rows, D), f32),
            jax.ShapeDtypeStruct((keys, D), f32),
            jax.ShapeDtypeStruct((8, 128), f32),
        ),
        in_specs=[anywhere] * 2
        + [pl.BlockSpec(memory_space=pltpu.SMEM)]
        + [inside] * 3
        + [anywhere] * len(arrays),
        out_specs=(anywhere,) * 5 + (inside,),
        scratch_shapes=held
        + [
            pltpu.SemaphoreType.DMA((len(held),)),
            pltpu.VMEM((2, D, 1024), bf16),
            pltpu.SemaphoreType.DMA((2,)),
            pltpu.VMEM((2, 2, rows, 256), f32),
            pltpu.SemaphoreType.DMA((2, 2)),
            pltpu.SemaphoreType.DMA((3,)),
            pltpu.VMEM((rows, 2 * units), bf16),
            pltpu.VMEM((keys, D), f32),
        ]
        + square
        + [pltpu.VMEM((keys, D), bf16)] * 2
        + [
            pltpu.VMEM((count,) + spots, bf16),
            pltpu.VMEM((count,) + spots, bf16),
            pltpu.VMEM((micro, length, D), bf16),
            pltpu.SemaphoreType.DMA((2 * (count - 1),)),
            pltpu.SemaphoreType.DMA((2 * (count - 1),)),
            pltpu.VMEM((3, 1, D), f32),
            pltpu.VMEM((micro * H, 1, length), f32),
            pltpu.VMEM((count, 8, 128), f32),
            pltpu.VMEM((count, 8, 128), f32),
            pltpu.SemaphoreType.DMA((count - 1,)),
            pltpu.SemaphoreType.DMA((count - 1,)),
        ]
        + Scatter.scratch(pieces, depth, blocks),
        compiler_params=pltpu.CompilerParams(
            collective_id=1, has_side_effects=True, vmem_limit_bytes=67043328
        ),
        name="backward",
    )(whole, down, source, live, buckets, gains, *arrays)


ACTS = ("hd", "n3", "r2", "ac", "cq", "ck", "cv", "n2", "r1", "mixed", "q", "k", "v", "n1", "bias")
LEFT = ("xk", "xv", "q", "k", "v", "o", "xq", "xo")


def norm_rows(values, gain_row, out):
    def chunk(k, _):
        rows = pl.ds(pl.multiple_of(k * 64, 64), 64)
        v = values[rows, :].astype(f32)
        out[rows, :] = (v * inverse_rms(v) * gain_row[...]).astype(bf16)
        return 0

    lax.fori_loop(0, values.shape[0] // 64, chunk, 0)


def by_columns(left, tile, width, put):
    def chunk(k, _):
        part = tile[:, :, :, :, columns(k * 256, 256)].reshape(-1, 256)
        put(k, jnp.dot(left[...], part, preferred_element_type=f32))
        return 0

    lax.fori_loop(0, width // 256, chunk, 0)


def attend_pairs(refs, out, marks, mask, first, last):
    q, k, v = refs
    rows_q = 128
    tall = k.shape[0] // (q.shape[0] // rows_q)
    even = lax.broadcasted_iota(jnp.int32, (1, 128), 1) < DH

    def pair(block, p):
        rows = pl.ds(pl.multiple_of(block * rows_q, rows_q), rows_q)
        keys = pl.ds(pl.multiple_of(block * tall, tall), tall)
        cols = columns(p * 128, 128)
        q2, k2, v2 = q[rows, cols], k[keys, cols], v[keys, cols]
        total = None
        for e in (0, 1):
            keep = even if e == 0 else jnp.logical_not(even)

            def half(value):
                return jnp.where(keep, value.astype(f32), 0.0).astype(bf16)

            probs = softmax_rows(mask(marks, against(half(q2), k2), block, 2 * p + e))
            term = jnp.dot(probs.astype(bf16), half(v2), preferred_element_type=f32)
            total = term if total is None else total + term
        out[rows, cols] = total.astype(bf16)

    pair_loop(first, last, pair)


def gain_rows(table, gains, count):
    each = D // count
    values = jnp.sum(table[...], axis=1).astype(bf16)
    lane = lax.broadcasted_iota(jnp.int32, (128, D), 0)
    col = lax.broadcasted_iota(jnp.int32, (128, D), 1)
    device = lax.broadcasted_iota(jnp.int32, (count, D), 0)
    owner = lax.broadcasted_iota(jnp.int32, (count, D), 1) // each
    for k in range(3):
        pick = jnp.where(lane == k * each + col % each, 1.0, 0.0).astype(bf16)
        spread = jnp.dot(values, pick, preferred_element_type=f32)
        gains[k] = jnp.sum(jnp.where(device == owner, spread, 0.0), axis=0, keepdims=True)


def bias_block(table, buckets, allowed, by_offset, bias, count, block):
    first, share = 3 * (D // count), H * NB // count
    split = NB // share
    values = jnp.sum(table[...], axis=1).astype(bf16)
    lane = lax.broadcasted_iota(jnp.int32, (128, 128), 0) - first
    for part in range(split):
        hit = (lane + part * share == buckets[block, 0:1, :]) & (lane >= 0) & (lane < share)
        pick = jnp.where(hit, 1.0, 0.0).astype(bf16)
        found = jnp.dot(values, pick, preferred_element_type=f32)
        for device in range(count):
            by_offset[part, device] = found[device : device + 1]

    def head_bias(head, _):
        row = by_offset[0, head * split]
        for part in range(1, split):
            row = row + by_offset[part, head * split + part]
        grid = pltpu.roll(
            jnp.broadcast_to(row, (128, 128)), 0, 1, stride=1, stride_axis=0
        )
        bias[block, head] = jnp.where(allowed[block] > 0.0, grid, -1e30).astype(bf16)
        return 0

    lax.fori_loop(0, H, head_bias, 0)


def forward_kernel(pieces, depth, widths, *refs):
    refs = list(refs)

    def pop(count):
        return [refs.pop(0) for _ in range(count)]

    wide = pop(len(widths))
    (deep, tile, source, live, allowed, buckets, hidden, encoder, cotangent) = pop(9)
    whole, whole_deep, gains, dy, result, pre = pop(6)
    outs = dict(zip(ACTS, pop(len(ACTS))))
    staged, staged_deep, table, by_offset, x, enc, cot = pop(7)
    held = dict(zip(ACTS, pop(len(ACTS))))
    pre_held, result_held, slots, slot_sems, down_sems, down_slot, spread, moved, wanted = pop(9)
    stage_sems, load_sems, out_sems, own_sems, send, recv, small_send, small_recv = pop(8)
    deal_send, deal_recv = pop(2)
    place = Place(depth)
    count = place.count
    rows, units = x.shape[0], held["hd"].shape[1]
    gather = Gather(
        place, pieces, (staged, staged_deep), (whole, whole_deep), own_sems, send, recv
    )
    staging, start = [], 0
    for i, width in enumerate(widths):
        target = staged.at[:, pl.ds(start, width)]
        staging.append(pltpu.make_async_copy(wide[i], target, stage_sems.at[i]))
        start += width
    staging.append(pltpu.make_async_copy(deep, staged_deep, stage_sems.at[len(widths)]))
    loads = [
        pltpu.make_async_copy(a, b, load_sems.at[i])
        for i, (a, b) in enumerate(((cotangent, cot), (hidden, x), (encoder, enc)))
    ]
    for copy in staging + loads:
        copy.start()
    place.greet()
    spread_small(place, tile, table, small_send, small_recv)
    redeal = Redeal(place, cot, spread, moved, wanted, deal_send, deal_recv)
    loads[0].wait()
    redeal.begin()
    for copy in staging:
        copy.wait()
    gather.open()
    collect_small(place, tile, table, small_send, small_recv)
    loads[1].wait()
    loads[2].wait()

    leaving = []

    def leave(name, source_ref=None, target=None):
        copy = pltpu.make_async_copy(
            held[name] if source_ref is None else source_ref,
            outs[name] if target is None else target,
            out_sems.at[len(leaving)],
        )
        copy.start()
        leaving.append(copy)

    tiles = [(D * k, D) for k in range(len(LEFT))]
    tiles += [(8 * D + k, min(1024, 2 * units - k)) for k in range(0, 2 * units, 1024)]

    def fetch(k):
        start, width = tiles[k]
        slot = k % slots.shape[0]
        return pltpu.make_async_copy(
            whole.at[:, :, :, :, pl.ds(start, width)],
            slots.at[slot, :, :, :, :, pl.ds(0, width)],
            slot_sems.at[slot],
        )

    def rounded(out):
        def put(k, part):
            out[:, columns(k * 256, 256)] = part.astype(bf16)

        return put

    def added(base, out):
        def put(k, part):
            cols = columns(k * 256, 256)
            out[:, cols] = base[:, cols].astype(f32) + part

        return put

    def units_of(k, tile_ref):
        start, width = tiles[k][0] - 8 * D, tiles[k][1]

        def put(n, part):
            at = start // 256 + n
            pre_held[:, columns(at * 256, 256)] = part

            @pl.when(at >= units // 256)
            def _():
                cols = columns((at - units // 256) * 256, 256)
                act, _ = gelu_parts(pre_held[:, cols])
                held["hd"][:, cols] = (act * part).astype(bf16)

        by_columns(held["n3"], tile_ref, width, put)

    whole_pairs = rows // 128 * (H // 2)
    work = []

    def piece_of(k):
        kind, end = (1, 0) if k is None else (0, sum(tiles[k]))
        ends = [s + w if kd == 0 else 0 for kd, s, w in pieces]
        return next(i for i, e in enumerate(ends) if e >= end)

    def with_tile(k, cost, act):
        def run():
            if k not in fetched:
                fetch(k).start()
                fetched.append(k)
            fetch(k).wait()
            act(slots.at[k % slots.shape[0]])
            used.append(k)

        work.append((piece_of(k), cost, run))

    def then(cost, act):
        work.append((0, cost, act))

    fetched, used = [], []

    def encoded(name):
        def act(ref):
            by_columns(enc, ref, D, rounded(held[name]))
            leave(name)

        return act

    def projected(name, left):
        def act(ref):
            by_columns(held[left], ref, D, rounded(held[name]))
            leave(name)

        return act

    def summed(left, base, total, gain, normed):
        def act(ref):
            by_columns(held[left], ref, D, added(base, held[total]))
            norm_rows(held[total], gains.at[gain], held[normed])
            leave(total)
            leave(normed)

        return act

    def attention(cost, names, out, marks, mask):
        for part in range(4):

            def act(part=part):
                attend_pairs(
                    [held[name] for name in names],
                    held[out],
                    marks,
                    mask,
                    part * whole_pairs // 4,
                    (part + 1) * whole_pairs // 4,
                )
                if part == 3:
                    leave(out)

            then(cost, act)

    def first_norm():
        gain_rows(table, gains, count)
        norm_rows(x, gains.at[0], held["n1"])
        leave("n1")

    work.append((-count, 3, first_norm))
    for block in range(held["bias"].shape[0]):

        def biases(block=block):
            bias_block(table, buckets, allowed, by_offset, held["bias"], count, block)
            if block == held["bias"].shape[0] - 1:
                leave("bias")

        work.append((-count, 3, biases))
    for k, name in enumerate(("ck", "cv")):
        with_tile(k, 4, encoded(name))
    for k, name in enumerate(("q", "k", "v")):
        with_tile(2 + k, 2, projected(name, "n1"))
    attention(2, ("q", "k", "v"), "mixed", held["bias"], self_scores)
    with_tile(5, 3, summed("mixed", x, "r1", 1, "n2"))
    with_tile(6, 2, projected("cq", "n2"))
    attention(3, ("cq", "ck", "cv"), "ac", live, cross_scores)
    with_tile(7, 3, summed("ac", held["r1"], "r2", 2, "n3"))
    for k in range(len(LEFT), len(tiles)):
        with_tile(k, 3, functools.partial(units_of, k))

    deep_pieces = [i for i, piece in enumerate(pieces) if piece[0]]
    downs = []
    for number, i in enumerate(deep_pieces):
        cut = pl.ds(pieces[i][1], pieces[i][2])
        downs.append(
            pltpu.make_async_copy(
                whole_deep.at[:, :, :, :, cut],
                down_slot.at[:, :, :, :, cut],
                down_sems.at[number],
            )
        )

    def last(k, part):
        cols = columns(k * 256, 256)
        result_held[:, cols] = (held["r2"][:, cols] + part).astype(bf16)

    for t in range(len(pieces) + GATHER_LAGS[3]):
        gather.turn(t)
        ready = t - GATHER_LAGS[3]
        if ready in deep_pieces:
            downs[deep_pieces.index(ready)].start()
        while len(fetched) < len(tiles) and piece_of(len(fetched)) <= ready:
            if len(fetched) >= len(used) + slots.shape[0]:
                break
            fetch(len(fetched)).start()
            fetched.append(len(fetched))
        if t == 6:
            redeal.middle(source)
        spent = 0
        while work and spent < 6 and work[0][0] <= ready:
            _, cost, run = work.pop(0)
            run()
            spent += cost
    while work:
        work.pop(0)[2]()
    leave("", pre_held, pre)
    leave("hd")
    for down in downs:
        down.wait()
    by_columns(held["hd"], down_slot, D, last)
    leave("", result_held, result)
    redeal.end()
    leave("", wanted, dy)
    for copy in leaving:
        copy.wait()
    gather.close()


def forward_all(wide, deep, small, source, live, allowed, buckets, hidden, encoder, cotangent, depth):
    widths = [part.shape[1] for part in wide]
    width, tall = sum(widths), wide[0].shape[0]
    tall_deep, units = deep.shape[0], widths[-1]
    rows, keys = hidden.shape[0], encoder.shape[0]
    micro, length = cotangent.shape[:2]
    pieces = cut_columns([512, 512] + [1024] * 7)
    pieces += [(0, k, min(1024, width - k)) for k in range(8 * D, width, 1024)]
    pieces += [(1, 0, 512), (1, 512, 512)]
    copies = len(pieces) * (1 + 2 * (depth + 2))
    count = 8 * depth
    tile = jnp.zeros((8, 128), f32).at[0, : small.shape[0]].set(small.astype(f32))
    anywhere = pl.BlockSpec(memory_space=pl.ANY)
    inside = pl.BlockSpec(memory_space=pltpu.VMEM)
    spots = (micro, length // 8, D // depth)
    kinds = dict(
        hd=((rows, units), bf16),
        n3=((rows, D), bf16),
        r2=((rows, D), f32),
        ac=((rows, D), bf16),
        cq=((rows, D), bf16),
        ck=((keys, D), bf16),
        cv=((keys, D), bf16),
        n2=((rows, D), bf16),
        r1=((rows, D), f32),
        mixed=((rows, D), bf16),
        q=((rows, D), bf16),
        k=((rows, D), bf16),
        v=((rows, D), bf16),
        n1=((rows, D), bf16),
        bias=((micro, H, length, length), bf16),
    )
    results = pl.pallas_call(
        functools.partial(forward_kernel, pieces, depth, widths),
        out_shape=(
            jax.ShapeDtypeStruct((depth, 2, 2, 2 * tall, width), bf16),
            jax.ShapeDtypeStruct((depth, 2, 2, 2 * tall_deep, D), bf16),
            jax.ShapeDtypeStruct((3, 1, D), f32),
            jax.ShapeDtypeStruct((micro, length, D), bf16),
            jax.ShapeDtypeStruct((rows, D), bf16),
            jax.ShapeDtypeStruct((rows, 2 * units), f32),
        )
        + tuple(jax.ShapeDtypeStruct(*kinds[name]) for name in ACTS),
        in_specs=[anywhere] * (len(wide) + 1)
        + [inside, pl.BlockSpec(memory_space=pltpu.SMEM)]
        + [inside] * 3
        + [anywhere] * 3,
        out_specs=(anywhere,) * 2 + (inside,) + (anywhere,) * (3 + len(ACTS)),
        scratch_shapes=[
            pltpu.VMEM((tall, width), bf16),
            pltpu.VMEM((tall_deep, D), bf16),
            pltpu.VMEM((count, 8, 128), f32),
            pltpu.VMEM((2, count, 1, 128), f32),
            pltpu.VMEM((rows, D), bf16),
            pltpu.VMEM((keys, D), bf16),
            pltpu.VMEM((micro, length, D), bf16),
        ]
        + [pltpu.VMEM(*kinds[name]) for name in ACTS]
        + [
            pltpu.VMEM((rows, 2 * units), f32),
            pltpu.VMEM((rows, D), bf16),
            pltpu.VMEM((5, depth, 2, 2, 2 * tall, 1024), bf16),
            pltpu.SemaphoreType.DMA((5,)),
            pltpu.SemaphoreType.DMA((2,)),
            pltpu.VMEM((depth, 2, 2, 2 * tall_deep, D), bf16),
            pltpu.VMEM((count,) + spots, bf16),
            pltpu.VMEM((count,) + spots, bf16),
            pltpu.VMEM((micro, length, D), bf16),
            pltpu.SemaphoreType.DMA((len(wide) + 1,)),
            pltpu.SemaphoreType.DMA((3,)),
            pltpu.SemaphoreType.DMA((len(ACTS) + 3,)),
            pltpu.SemaphoreType.DMA((len(pieces),)),
            pltpu.SemaphoreType.DMA((copies,)),
            pltpu.SemaphoreType.DMA((copies,)),
            pltpu.SemaphoreType.DMA((count - 1,)),
            pltpu.SemaphoreType.DMA((count - 1,)),
            pltpu.SemaphoreType.DMA((2 * (count - 1),)),
            pltpu.SemaphoreType.DMA((2 * (count - 1),)),
        ],
        compiler_params=pltpu.CompilerParams(
            collective_id=0, has_side_effects=True, vmem_limit_bytes=67043328
        ),
        name="forward",
    )(*wide, deep, tile, source, live, allowed, buckets, hidden, encoder, cotangent)
    whole, whole_deep, gains, dy, result, pre = results[:6]
    acts = dict(zip(ACTS, results[6:]))
    acts.update(
        dy=dy.reshape(rows, D),
        result=result.reshape(micro, length, D),
        pre=pre,
        x=hidden,
        enc=encoder,
    )
    return whole.reshape(-1, width), whole_deep.reshape(-1, D), gains, acts


def fused(
    depth,
    hidden,
    encoder,
    cotangent,
    segments,
    buckets,
    live,
    dealing,
    small,
    wide,
    feed_down,
):
    micro, _, length, _ = hidden.shape
    enc_count = encoder.shape[2]
    count = 8 * depth
    slots = jnp.arange(count, dtype=jnp.int32)
    inverse = jnp.sum(
        jnp.where(dealing[:, None, :] == slots[:, None], slots, 0), axis=2, dtype=jnp.int32
    )
    positions = jnp.arange(length, dtype=jnp.int32)
    allowed = (positions[None, :] <= positions[:, None])[None] & (
        segments[:, :, None] == segments[:, None, :]
    )
    turned = jnp.concatenate([buckets[:, :1], buckets[:, :0:-1]], axis=1)
    live_rows = jnp.arange(enc_count, dtype=jnp.int32)[None, None, :] < live[:, None, None]
    live_rows = jnp.broadcast_to(live_rows, (micro, 8, enc_count)).astype(f32)
    whole, down, gains, acts = forward_all(
        wide,
        feed_down,
        small,
        inverse,
        live_rows,
        allowed.astype(f32),
        jnp.broadcast_to(turned[:, None], (micro, 8, length)),
        hidden.reshape(micro * length, D),
        encoder.reshape(micro * enc_count, D),
        cotangent.reshape(micro, length, D),
        depth,
    )
    flipped = jnp.broadcast_to(buckets[:, ::-1, None], (micro, length, 128))
    sums, piece_down, layer_out, grad_in, grad_enc, small_sum = backward_all(
        whole, down, dealing, live_rows, flipped, gains, acts, depth
    )
    small_sum = small_sum[0]
    tall, tall_deep = wide[0].shape[0], feed_down.shape[0]
    sums = sums.reshape(-1, tall, 128)
    piece_down = piece_down.reshape(-1, tall_deep, 128)

    def unpack(tiles):
        return tiles.transpose(1, 0, 2).reshape(tiles.shape[1], -1)

    grads, start = [], 0
    for part in wide:
        tiles = part.shape[1] // 128
        grads.append(unpack(sums[start : start + tiles]))
        start += tiles
    part = D // count
    return (
        layer_out.reshape(hidden.shape),
        grad_in.reshape(hidden.shape),
        grad_enc.reshape(encoder.shape),
        small_sum[:part],
        small_sum[part : 2 * part],
        small_sum[2 * part : 3 * part],
        small_sum[3 * part : 3 * part + H * NB // count],
        *[grads[k] for k in (2, 3, 4, 5, 6, 0, 1, 7, 8, 9)],
        unpack(piece_down),
    )


def body(
    hidden,
    encoder,
    cotangent,
    segment_ids,
    rel_buckets,
    enc_rows,
    dealing,
    gain_self,
    gain_cross,
    gain_ffn,
    rel_bias,
    self_query,
    self_key,
    self_value,
    self_out,
    cross_query,
    cross_key,
    cross_value,
    cross_out,
    feed_gate,
    feed_up,
    feed_down,
):
    device = lax.axis_index(AXIS)
    micro, own, length, _ = hidden.shape
    enc_count = encoder.shape[2]
    blocks = micro * own
    first = device * own

    def mine(table):
        return lax.dynamic_slice_in_dim(table, first, own, axis=1).reshape(
            (blocks,) + table.shape[2:]
        )

    segments, buckets, live = mine(segment_ids), mine(rel_buckets), mine(enc_rows)
    small = jnp.concatenate([gain_self, gain_cross, gain_ffn, rel_bias])
    wide = (
        cross_key,
        cross_value,
        self_query,
        self_key,
        self_value,
        self_out,
        cross_query,
        cross_out,
        feed_gate,
        feed_up,
    )
    depth = kernel_depth(lax.axis_size(AXIS), self_query, feed_down) if own == 1 else 0
    if depth:
        return fused(
            depth,
            hidden,
            encoder,
            cotangent,
            segments,
            buckets,
            live,
            dealing,
            small,
            wide,
            feed_down,
        )
    grad_out = redeal(cotangent, jnp.argsort(dealing, axis=1)).reshape(blocks * length, D)

    smalls = lax.all_gather(small, AXIS, axis=0)
    part = gain_self.shape[0]
    gain_one, gain_two, gain_three = [
        smalls[:, k * part : (k + 1) * part].reshape(D).astype(f32) for k in range(3)
    ]
    bias_table = smalls[:, 3 * part :].reshape(H, NB).astype(f32)
    (wq, wk, wv, wo, xq, xk, xv, xo, gate, up), down = gather_weights(
        (
            self_query,
            self_key,
            self_value,
            self_out,
            cross_query,
            cross_key,
            cross_value,
            cross_out,
            feed_gate,
            feed_up,
        ),
        feed_down,
    )

    positions = jnp.arange(length, dtype=jnp.int32)
    allowed = (positions[None, :] <= positions[:, None])[None] & (
        segments[:, :, None] == segments[:, None, :]
    )
    cross_allowed = jnp.broadcast_to(
        jnp.arange(enc_count, dtype=jnp.int32)[None, None, :] < live[:, None, None],
        (blocks, length, enc_count),
    )
    onehot = (buckets[:, :, None] == jnp.arange(NB, dtype=jnp.int32)).astype(f32)
    per_offset = jnp.einsum("hc,boc->bho", bias_table, onehot, precision=highest)
    bias_grid = toeplitz_expand(per_offset.reshape(blocks * H, length)).reshape(
        blocks, H, length, length
    )

    wide_in = hidden.reshape(blocks * length, D).astype(f32)
    enc_in = encoder.reshape(blocks * enc_count, D)
    inv_one = inverse_rms(wide_in)
    normed_one = (wide_in * inv_one * gain_one).astype(bf16)
    queries = product(normed_one, wq).astype(bf16)
    keys_self = product(normed_one, wk).astype(bf16)
    values_self = product(normed_one, wv).astype(bf16)
    mixed_self, probs_self = attend(queries, keys_self, values_self, bias_grid, allowed)
    first_sum = wide_in + product(mixed_self, wo)
    inv_two = inverse_rms(first_sum)
    normed_two = (first_sum * inv_two * gain_two).astype(bf16)
    cross_queries = product(normed_two, xq).astype(bf16)
    cross_keys = product(enc_in, xk).astype(bf16)
    cross_values = product(enc_in, xv).astype(bf16)
    mixed_cross, probs_cross = attend(
        cross_queries, cross_keys, cross_values, None, cross_allowed
    )
    second_sum = first_sum + product(mixed_cross, xo)
    inv_three = inverse_rms(second_sum)
    normed_three = (second_sum * inv_three * gain_three).astype(bf16)
    gate_pre = product(normed_three, gate)
    up_pre = product(normed_three, up)
    act, slope = gelu_parts(gate_pre)
    hidden_units = (act * up_pre).astype(bf16)
    result = (second_sum + product(hidden_units, down)).astype(bf16)
    layer_out = redeal(result.reshape(micro, own, length, D), dealing)

    g_down = product_left(hidden_units, grad_out)
    grad_units = product_right(grad_out, down)
    grad_gate = (grad_units * up_pre * slope).astype(bf16)
    grad_up = (grad_units * act).astype(bf16)
    g_gate = product_left(normed_three, grad_gate)
    g_up = product_left(normed_three, grad_up)
    grad_three = product_right(grad_gate, gate) + product_right(grad_up, up)
    back, g_gain_three = norm_back(second_sum, inv_three, gain_three, grad_three)
    grad_second = grad_out.astype(f32) + back
    grad_low = grad_second.astype(bf16)
    g_xo = product_left(mixed_cross, grad_low)
    grad_mixed = product_right(grad_low, xo).astype(bf16)
    grad_cq, grad_ck, grad_cv, _ = attend_back(
        cross_queries, cross_keys, cross_values, probs_cross, grad_mixed
    )
    g_xq = product_left(normed_two, grad_cq)
    g_xk = product_left(enc_in, grad_ck)
    g_xv = product_left(enc_in, grad_cv)
    grad_enc = product_right(grad_ck, xk) + product_right(grad_cv, xv)
    back, g_gain_two = norm_back(first_sum, inv_two, gain_two, product_right(grad_cq, xq))
    grad_first = grad_second + back
    grad_low = grad_first.astype(bf16)
    g_so = product_left(mixed_self, grad_low)
    grad_mixed = product_right(grad_low, wo).astype(bf16)
    grad_sq, grad_sk, grad_sv, grad_scores = attend_back(
        queries, keys_self, values_self, probs_self, grad_mixed
    )
    offsets = toeplitz_fold(
        grad_scores.astype(f32).reshape(blocks * H, length, length)
    ).reshape(blocks, H, length)
    g_bias = jnp.einsum("bho,boc->hc", offsets, onehot, precision=highest).reshape(H * NB)
    g_sq = product_left(normed_one, grad_sq)
    g_sk = product_left(normed_one, grad_sk)
    g_sv = product_left(normed_one, grad_sv)
    grad_one = (
        product_right(grad_sq, wq) + product_right(grad_sk, wk) + product_right(grad_sv, wv)
    )
    back, g_gain_one = norm_back(wide_in, inv_one, gain_one, grad_one)
    grad_in = grad_first + back

    pieces, piece_down = scatter_grads(
        (g_sq, g_sk, g_sv, g_so, g_xq, g_xk, g_xv, g_xo, g_gate, g_up), g_down
    )
    count = smalls.shape[0]
    small_grads = jnp.concatenate(
        [g.reshape(count, -1) for g in (g_gain_one, g_gain_two, g_gain_three, g_bias)], axis=1
    )
    small_sum = jnp.sum(
        lax.all_to_all(small_grads, AXIS, split_axis=0, concat_axis=0, tiled=True), axis=0
    )
    return (
        layer_out,
        grad_in.reshape(hidden.shape),
        grad_enc.reshape(encoder.shape),
        small_sum[:part],
        small_sum[part : 2 * part],
        small_sum[2 * part : 3 * part],
        small_sum[3 * part :],
        *pieces,
        piece_down,
    )


def solution(mesh):
    block = P(None, AXIS, None, None)
    row = P(AXIS)
    matrix = P(AXIS, None)
    return jax.shard_map(
        body,
        mesh=mesh,
        in_specs=(block,) * 3 + (P(),) * 4 + (row,) * 4 + (matrix,) * 11,
        out_specs=(block,) * 3 + (row,) * 4 + (matrix,) * 11,
        check_vma=False,
    )
```
